512 devices in a mesh: pipe: 2 (over x_lo), dp: 16 (over y, core), inner: 16 (over x_hi, z).
Axes of the slice: x: 4 (x_hi: 2, x_lo: 2; x = x_hi * 2 + x_lo), y: 8, z: 8, core: 2. Of those that a mesh axis runs over, the one named last changes fastest.
Arguments:
- pixels: bfloat16 [64, 48, 16, 256], P('dp', 'inner'), may hold values from -6 to 6
- date_days: int32 [64, 16], P('dp'), may hold values from 0 to 364
- clear_count: int32 [64], P('dp'), may hold values from 3 to 16, as said below
- batch_slot: int32 [64], P('dp'), may hold values from 0 to 3, as said below
- labels: int32 [64, 48], P('dp'), may hold values from 0 to 15
- class_tokens: bfloat16 [16, 256], replicated, may hold values from -6 to 6
- section_gain: float32 [2, 256], P('pipe'), may hold values from 0.5 to 2
- segment_probe_lookup_content: bfloat16 [2, 256, 768], P('pipe'), may hold values from -0.375 to 0.375
- section_out: bfloat16 [2, 256, 256], P('pipe'), may hold values from -0.375 to 0.375
- head_vec: float32 [256], replicated, may hold values from -1 to 1
Outputs:
- batch_loss: float32 [4], replicated
- class_grad: float32 [16, 256], replicated
- section_gain_grad: float32 [2, 256], P('pipe')
- section_qkv_grad: float32 [2, 256, 768], P('pipe')
- section_out_grad: float32 [2, 256, 256], P('pipe')
- readout_derivative: float32 [256], replicated
The draws below stay inside these ranges and needn't reach their ends.
Inputs may be any that keep to these rules, and one draw needn't show every extreme that they name: The clear dates of tile b are its dates 0 to clear_count[b] - 1. Some tile has all 16 dates clear and some tile has the fewest. `batch_slot`: within each aligned block of 4 tiles (the tiles of one index of dp) every micro-batch number appears exactly once.
All inputs are finite; a program needn't handle non-finite values.
Results may differ from the reference program's by a relative error of at most 0.0015.
The reference program's roundings to bfloat16 on the way count: a program that leaves them out, or rounds other values in their place, can miss the bound.
Values may be sent and summed in bfloat16 or wider, within the bound.
No kernel may reach another device: no remote copies, remote signals or barrier semaphores. Data moves between devices by JAX's collectives and lax.ppermute only.
A program may use at most 64 MiB of HBM per device.

```python
import math
import jax
import jax.numpy as jnp
from jax import lax

D = 256
HEADS = 8
CLASSES = 16
PATCHES = 48
DATES = 16
MICRO = 4
TILE_DEV = 4
TILES = 64


def draw_clear_count(key, part):
    lowest = DATES // 6 + 1
    counts = jax.random.randint(jax.random.fold_in(key, 11), (TILES,), lowest, DATES + 1)
    places = jax.random.permutation(jax.random.fold_in(key, 12), TILES)
    counts = counts.at[places[0]].set(DATES)
    counts = counts.at[places[1]].set(lowest)
    return counts.astype(jnp.int32)


def draw_batch_slot(key, part):
    blocks = TILES // TILE_DEV
    pattern = jnp.arange(TILE_DEV, dtype=jnp.int32) % MICRO
    block_keys = jax.random.split(jax.random.fold_in(key, 21), blocks)
    shuffled = jax.vmap(lambda block_key: jax.random.permutation(block_key, pattern))(block_keys)
    return shuffled.reshape(TILES).astype(jnp.int32)


def with_ends(array, key, smallest, largest):
    longest = array.shape.index(max(array.shape))
    spots = []
    for shift in (0, 1):
        where = [jax.random.randint(jax.random.fold_in(key, axis), (), 0, length) for axis, length in enumerate(array.shape)]
        where[longest] = (where[longest] + shift) % array.shape[longest]
        spots.append(tuple(where))
    return array.at[spots[0]].set(smallest).at[spots[1]].set(largest)


def block_levels(stream_key, extent, pieces, smallest, top_value):
    gain = 1.0
    for axis_at, parts in pieces:
        heights = jax.random.uniform(jax.random.fold_in(jax.random.fold_in(stream_key, 6), axis_at), (parts,), jnp.float32, smallest / len(pieces), top_value / len(pieces))
        gain = gain * jnp.repeat(jnp.exp(heights), extent[axis_at] // parts).reshape((-1,) + (1,) * (len(extent) - 1 - axis_at))
    return gain


def noise(own_key, dims, width, most, cuts=(), kind=jnp.bfloat16):
    values = width * jax.random.normal(own_key, dims, jnp.float32)
    if cuts:
        values = values * block_levels(own_key, dims, cuts, -0.22, 0.18)
    return jnp.clip(values, -most, most).astype(kind)


def setup_inputs(seed: int = 0) -> dict:
    streams_of = jax.random.split(jax.random.key(seed), 11)
    return {
        "pixels": noise(streams_of[0], (TILES, PATCHES, DATES, D), 1.0, 6.0, ((0, 16), (1, 16))),
        "date_days": with_ends(jax.random.randint(streams_of[1], (TILES, DATES), 0, 365), jax.random.fold_in(streams_of[1], 1), 0, 364).astype(jnp.int32),
        "clear_count": draw_clear_count(jax.random.fold_in(streams_of[10], 71), 0),
        "batch_slot": draw_batch_slot(jax.random.fold_in(streams_of[10], 71), 0),
        "labels": with_ends(jax.random.randint(streams_of[4], (TILES, PATCHES), 0, CLASSES), jax.random.fold_in(streams_of[4], 1), 0, CLASSES - 1).astype(jnp.int32),
        "class_tokens": noise(streams_of[5], (CLASSES, D), 1.0, 6.0),
        "section_gain": jnp.clip(jnp.exp(math.log(2.0) - 1.3862944 * jax.random.uniform(streams_of[6], (2, D), jnp.float32) ** block_levels(streams_of[6], (2, D), ((0, 2),), -0.2, 0.2)), 0.5, 2.0),
        "segment_probe_lookup_content": noise(streams_of[7], (2, D, 3 * D), D ** -0.5, 0.375, ((0, 2),)),
        "section_out": noise(streams_of[8], (2, D, D), D ** -0.5, 0.375, ((0, 2),)),
        "head_vec": noise(streams_of[9], (D,), (D // 9) ** -0.5, 1.0, (), jnp.float32),
    }


normalizer_sharpness = 10.0
logit_cap = 15.0
norm_eps = 1e-05
head_eps = 1e-06

def matmul_f32(left_side, right_side):
    return jnp.einsum('...d,de->...e', left_side.astype(jnp.float32), right_side.astype(jnp.float32), precision=lax.Precision.HIGHEST)

def rms_norm(inputs, gain_vec):
    inverse_rms = lax.rsqrt(lax.optimization_barrier(jnp.mean(inputs * inputs, axis=-1, keepdims=True)) + norm_eps)
    return inputs * inverse_rms * gain_vec

def unit_heads(values):
    shaped = values.reshape(values.shape[:-1] + (HEADS, values.shape[-1] // HEADS))
    return shaped * lax.rsqrt(lax.optimization_barrier(jnp.sum(shaped * shaped, axis=-1, keepdims=True)) + head_eps)

def temporal(pixel_rows, date_days, counts, params):
    class_init, gain_vec, w_qkv, w_out = params
    batch_count, patches, dates_max, model_width = pixel_rows.shape
    classes = class_init.shape[0]
    band_channel = jnp.arange(model_width)
    frequency = jnp.exp((band_channel // 2 * 2).astype(jnp.float32) * (-math.log(10000.0) / model_width))
    phases = date_days.astype(jnp.float32)[:, :, None] * frequency
    encoding = jnp.where(band_channel % 2 == 0, jnp.sin(phases), jnp.cos(phases))
    date_rows = pixel_rows.astype(jnp.float32) + encoding[:, None]
    class_rows = jnp.broadcast_to(class_init, (batch_count, patches, classes, model_width))
    sequence = jnp.concatenate([class_rows, date_rows], axis=2)
    normed = rms_norm(sequence, gain_vec).astype(jnp.bfloat16)
    probe_entry_lines = unit_heads(matmul_f32(normed[:, :, :classes], w_qkv[:, :model_width]))
    lookup_entry_lines = unit_heads(matmul_f32(normed, w_qkv[:, model_width:2 * model_width]))
    value_rows = matmul_f32(normed, w_qkv[:, 2 * model_width:]).astype(jnp.bfloat16)
    value_heads = value_rows.reshape(batch_count, patches, classes + dates_max, HEADS, model_width // HEADS)
    affinity_logit_grid = normalizer_sharpness * jnp.einsum('ohbyv,ohsyv->ohybs', probe_entry_lines, lookup_entry_lines, precision=lax.Precision.HIGHEST)
    position = jnp.arange(classes + dates_max)
    key_mask = ((position[None, :] < classes) | (position[None, :] - classes < counts[:, None])).astype(jnp.float32)
    raised = jnp.exp(affinity_logit_grid) * key_mask[:, None, None, None, :]
    weights = (raised / lax.optimization_barrier(jnp.sum(raised, axis=-1, keepdims=True))).astype(jnp.bfloat16)
    attended = jnp.einsum('bphqk,bpkhe->bpqhe', weights.astype(jnp.float32), value_heads.astype(jnp.float32), precision=lax.Precision.HIGHEST)
    attended = attended.reshape(batch_count, patches, classes, model_width).astype(jnp.bfloat16)
    updated = sequence[:, :, :classes] + matmul_f32(attended, w_out)
    return jnp.swapaxes(updated, 1, 2).astype(jnp.bfloat16)

def spatial(inputs, params):
    gain_vec, w_qkv, w_out, head_vec = params
    batch_count, groups, classes, patches, model_width = inputs.shape
    class_seq = jnp.swapaxes(inputs, 1, 2).reshape(batch_count, classes, groups * patches, model_width).astype(jnp.float32)
    normed = rms_norm(class_seq, gain_vec).astype(jnp.bfloat16)
    probe_entry_lines = unit_heads(matmul_f32(normed, w_qkv[:, :model_width]))
    lookup_entry_lines = unit_heads(matmul_f32(normed, w_qkv[:, model_width:2 * model_width]))
    value_rows = matmul_f32(normed, w_qkv[:, 2 * model_width:]).astype(jnp.bfloat16)
    value_heads = value_rows.reshape(batch_count, classes, groups * patches, HEADS, model_width // HEADS)
    affinity_logit_grid = normalizer_sharpness * jnp.einsum('wisbx,wiqbx->wibsq', probe_entry_lines, lookup_entry_lines, precision=lax.Precision.HIGHEST)
    raised = jnp.exp(affinity_logit_grid)
    weights = (raised / lax.optimization_barrier(jnp.sum(raised, axis=-1, keepdims=True))).astype(jnp.bfloat16)
    attended = jnp.einsum('bchqk,bckhe->bcqhe', weights.astype(jnp.float32), value_heads.astype(jnp.float32), precision=lax.Precision.HIGHEST)
    attended = attended.reshape(batch_count, classes, groups * patches, model_width).astype(jnp.bfloat16)
    hidden = class_seq + matmul_f32(attended, w_out)
    raw_logits = jnp.einsum('bcpd,d->bcp', hidden, head_vec, precision=lax.Precision.HIGHEST)
    logits = logit_cap * jnp.tanh(raw_logits / logit_cap)
    return logits.reshape(batch_count, classes, groups, patches)

def reference(pixels, date_days, clear_count, batch_slot, labels, class_tokens, section_gain, segment_probe_lookup_content, section_out, head_vec):
    first_params = (class_tokens.astype(jnp.float32), section_gain[0], segment_probe_lookup_content[0].astype(jnp.float32), section_out[0].astype(jnp.float32))
    second_params = (section_gain[1], segment_probe_lookup_content[1].astype(jnp.float32), section_out[1].astype(jnp.float32), head_vec)
    tile_count = pixels.shape[0]
    model_width = pixels.shape[3]
    class_ids = jnp.arange(CLASSES)

    def one_tile(totals, tile_args):
        pixel_rows, day_rows, count_one, label_row = tile_args
        encoded, pull_first = jax.vjp(lambda params: temporal(pixel_rows[None], day_rows[None], count_one[None], params), first_params)
        inputs = encoded.reshape(1, 1, CLASSES, PATCHES, model_width)
        logits, pull_second = jax.vjp(spatial, inputs, second_params)
        exp_logits = jnp.exp(logits)
        class_total = lax.optimization_barrier(jnp.sum(exp_logits, axis=1))
        indicator_rows = (label_row.reshape(1, 1, 1, PATCHES) == class_ids[None, :, None, None]).astype(jnp.float32)
        dlogit = (exp_logits / class_total[:, None] - indicator_rows) / tile_count
        grad_in, grads_second = pull_second(dlogit)
        first_gradients, = pull_first(grad_in.reshape(encoded.shape))
        tile_loss = jnp.sum(indicator_rows * (jnp.log(class_total)[:, None] - logits))
        new_totals = (totals[0] + first_gradients[0], totals[1] + first_gradients[1], totals[2] + first_gradients[2], totals[3] + first_gradients[3], totals[4] + grads_second[0], totals[5] + grads_second[1], totals[6] + grads_second[2], totals[7] + grads_second[3])
        return (new_totals, tile_loss)
    initial = (jnp.zeros((CLASSES, model_width), jnp.float32), jnp.zeros((model_width,), jnp.float32), jnp.zeros((model_width, 3 * model_width), jnp.float32), jnp.zeros((model_width, model_width), jnp.float32), jnp.zeros((model_width,), jnp.float32), jnp.zeros((model_width, 3 * model_width), jnp.float32), jnp.zeros((model_width, model_width), jnp.float32), jnp.zeros((model_width,), jnp.float32))
    totals, tile_losses = lax.scan(one_tile, initial, (pixels, date_days, clear_count, labels))
    slot_onehot = (batch_slot[None, :] == jnp.arange(MICRO)[:, None]).astype(jnp.float32)
    batch_loss = lax.optimization_barrier(jnp.sum(slot_onehot * tile_losses[None, :], axis=1)) / (tile_count // MICRO * PATCHES)
    section_gain_grad = jnp.stack([totals[1], totals[4]])
    section_qkv_grad = jnp.stack([totals[2], totals[5]])
    section_out_grad = jnp.stack([totals[3], totals[6]])
    return (batch_loss, totals[0], section_gain_grad, section_qkv_grad, section_out_grad, totals[7])
```

```python
import functools
import math

import jax
import jax.numpy as jnp
from jax import lax
from jax.experimental import pallas as pl
from jax.experimental.pallas import tpu as pltpu
from jax.sharding import PartitionSpec as P

D = 256
HEADS = 8
CLASSES = 16
PATCHES = 48
MICRO = 4
SHARP = 10.0
CAP = 15.0
NORM_EPS = 1e-05
HEAD_EPS = 1e-06
F32 = jnp.float32
BF16 = jnp.bfloat16
I32 = jnp.int32

TILES_DEV = 4
PATCH_DEV = 3
SEQS = TILES_DEV * PATCH_DEV
DATES = 16
ROWS = SEQS * 16
MEMBERS = 16
SLOT = 16
CHUNK = 72


def dot(a, b):
    return lax.dot_general(a, b, (((1,), (0,)), ((), ())), preferred_element_type=F32)


def dot_nt(a, b):
    return lax.dot_general(a, b, (((1,), (1,)), ((), ())), preferred_element_type=F32)


def dot_tn(a, b):
    return lax.dot_general(a, b, (((0,), (0,)), ((), ())), preferred_element_type=F32)


def split(x):
    hi = x.astype(BF16)
    return hi, (x - hi.astype(F32)).astype(BF16)


def rounded(x):
    return x.astype(BF16).astype(F32)


def iota(shape, axis):
    return lax.broadcasted_iota(I32, shape, axis)


def head_ones():
    same = (iota((D, D), 0) >> 5) == (iota((D, D), 1) >> 5)
    return jnp.where(same, 1.0, 0.0).astype(BF16)


def head_sums(x, ones):
    hi, lo = split(x)
    return dot(hi, ones) + dot(lo, ones)


def spread(rows_of):
    n = rows_of.shape[0]
    lane_head = iota((n, D), 1) >> 5
    zero = jnp.zeros_like(rows_of)
    return jnp.concatenate([jnp.where(lane_head == h, rows_of, zero) for h in range(HEADS)], axis=0)


def gathered_heads(wide):
    n = wide.shape[0] // HEADS
    lane_head = iota((n, D), 1) >> 5
    out = wide[:n]
    for h in range(1, HEADS):
        out = jnp.where(lane_head == h, wide[h * n : (h + 1) * n], out)
    return out


def slot_targets(shape, axis, temporal_rows):
    r = iota(shape, axis)
    group, tile, patch = r >> 4, (r >> 2) & 3, r & 3
    if temporal_rows:
        target = (tile * PATCH_DEV + patch) * 16 + group
    else:
        target = tile * PATCHES + group * PATCH_DEV + patch
    return jnp.where(patch < PATCH_DEV, target, -1)


def to_slots(temporal_rows):
    shape = (MEMBERS * SLOT, ROWS)
    hit = slot_targets(shape, 0, temporal_rows) == iota(shape, 1)
    return jnp.where(hit, 1.0, 0.0).astype(BF16)


def from_slots(temporal_rows):
    shape = (ROWS, MEMBERS * SLOT)
    hit = slot_targets(shape, 1, temporal_rows) == iota(shape, 0)
    return jnp.where(hit, 1.0, 0.0).astype(BF16)


def logits_t(k, q_wide):
    n = k.shape[0]
    k_hi, k_lo = split(k)
    q_hi, q_lo = split(q_wide)
    both = dot_nt(jnp.concatenate([k_hi, k_lo], axis=0), q_hi)
    return SHARP * (both[:n] + both[n:] + dot_nt(k_hi, q_lo))


def three_pass(x, w_hi, w_lo):
    n = x.shape[0]
    x_hi, x_lo = split(x)
    both = dot(jnp.concatenate([x_hi, x_lo], axis=0), w_hi)
    return both[:n] + both[n:] + dot(x_hi, w_lo)


def three_pass_tn(x, y):
    x_hi, x_lo = split(x)
    y_hi, y_lo = split(y)
    return dot_tn(
        jnp.concatenate([x_hi, x_hi, x_lo], axis=0), jnp.concatenate([y_hi, y_lo, y_hi], axis=0)
    )


def wide_dot_nt(x, w):
    n = x.shape[0]
    hi, lo = split(x)
    both = dot_nt(jnp.concatenate([hi, lo], axis=0), w)
    return both[:n] + both[n:]


def temporal_forward(
    counts, pix, enc, cls, gain, wqkv, wout, send, normed_o, xhat_o, k_o, kn_o, q_o, qn_o, v_o, ad_o, ac_o, att_o, rc_o
):
    ones = head_ones()
    w = wqkv[0]
    g = gain[0:1, :]
    enc_rows = enc[...]
    enc_all = jnp.concatenate(
        [enc_rows[b * 16 : b * 16 + 16] for b in range(TILES_DEV) for _ in range(PATCH_DEV)], axis=0
    )
    xd = pix[...].astype(F32) + enc_all
    xc = cls[...].astype(F32)
    x = jnp.concatenate([xd, xc], axis=0)
    inv = lax.rsqrt(jnp.mean(x * x, axis=-1, keepdims=True) + NORM_EPS)
    xhat = x * inv
    normed = (xhat * g).astype(BF16)
    xhat_o[...] = xhat
    normed_o[...] = normed
    rc_o[...] = jnp.broadcast_to(inv[ROWS:], (16, 128))
    kv = dot(normed, w[:, D:])
    q_raw = dot(normed[ROWS:], w[:, :D])
    v = kv[:, D:].astype(BF16)
    kq = jnp.concatenate([kv[:, :D], q_raw], axis=0)
    kq_inv = lax.rsqrt(head_sums(kq * kq, ones) + HEAD_EPS)
    kq_unit = kq * kq_inv
    n = ROWS + 16
    k, q = kq_unit[:n], kq_unit[n:]
    k_o[...] = k
    kn_o[...] = kq_inv[:n]
    q_o[...] = q
    qn_o[...] = kq_inv[n:]
    v_o[...] = v
    raised = jnp.exp(logits_t(k, spread(q)))
    date_at = iota((PATCHES, 128), 0) & 15
    mask = jnp.concatenate(
        [jnp.where(date_at < counts[b], 1.0, 0.0) for b in range(TILES_DEV)], axis=0
    )
    e_dates = (raised[:ROWS] * mask).reshape(SEQS, DATES, 128)
    e_class = raised[ROWS:]
    total = jnp.sum(e_dates, axis=1, keepdims=True) + jnp.sum(e_class, axis=0, keepdims=True)[None]
    a_dates = e_dates / total
    a_class = e_class[None] / total
    ad_o[...] = a_dates.reshape(ROWS, 128)
    ac_o[...] = a_class.reshape(ROWS, 128)
    v_class = v[ROWS:]
    parts = []
    for s in range(SEQS):
        weights = jnp.concatenate([a_class[s], a_dates[s]], axis=0).astype(BF16)
        values = jnp.concatenate([v_class, v[s * 16 : s * 16 + 16]], axis=0)
        parts.append(gathered_heads(dot_tn(weights, values)))
    att = jnp.concatenate(parts, axis=0).astype(BF16)
    att_o[...] = att
    updated = jnp.concatenate([xc] * SEQS, axis=0) + dot(att, wout[0])
    slots = dot(to_slots(True), updated.astype(BF16)).astype(BF16)
    send[0:16] = jnp.zeros((16, SLOT, D), BF16)
    send[16:32] = slots.reshape(16, SLOT, D)


def temporal_backward(
    first, gin, back, gain, wqkv, wout, normed_i, xhat_i, k_i, kn_i, q_i, qn_i, v_i, ad_i, ac_i, att_i, rc_i, out
):
    @pl.when(first[0] == 0)
    def _():
        out[...] = gin[...]

    @pl.when(first[0] == 1)
    def _():
        ones = head_ones()
        w = wqkv[0]
        gain_row = gain[0:1, :]
        g = dot(from_slots(True), back[...].reshape(MEMBERS * SLOT, D)).astype(BF16)
        att = att_i[...]
        d_att = dot_nt(g, wout[0]).astype(BF16)
        d_wout = dot_tn(att, g)
        v = v_i[...]
        v_class = v[ROWS:]
        a_dates = ad_i[...]
        a_class = ac_i[...]
        k = k_i[...]
        q = q_i[...]
        k_class = k[ROWS:]
        da_class, da_dates, dv_class, dv_dates = [], [], [], []
        for s in range(SEQS):
            rows = slice(s * 16, s * 16 + 16)
            wide = spread(d_att[rows])
            values = jnp.concatenate([v_class, v[rows]], axis=0)
            weights = jnp.concatenate([a_class[rows], a_dates[rows]], axis=0).astype(BF16)
            da = rounded(dot_nt(values, wide))
            dv = dot(weights, wide).astype(BF16)
            da_class.append(da[:16])
            da_dates.append(da[16:])
            dv_class.append(dv[:16])
            dv_dates.append(dv[16:])
        stack = lambda parts: jnp.concatenate(parts, axis=0)
        da_c, da_d = stack(da_class), stack(da_dates)
        tot = jnp.sum((da_c * a_class).reshape(SEQS, 16, 128), axis=1, keepdims=True) + jnp.sum(
            (da_d * a_dates).reshape(SEQS, 16, 128), axis=1, keepdims=True
        )
        ds_c = SHARP * a_class.reshape(SEQS, 16, 128) * (da_c.reshape(SEQS, 16, 128) - tot)
        ds_d = SHARP * a_dates.reshape(SEQS, 16, 128) * (da_d.reshape(SEQS, 16, 128) - tot)
        q_hi, q_lo = split(spread(q))
        ds_all = jnp.concatenate([ds_d.reshape(ROWS, 128), ds_c.reshape(ROWS, 128)], axis=0)
        dk = three_pass(ds_all, q_hi, q_lo)
        dq_parts = []
        for s in range(SEQS):
            ds_s = jnp.concatenate([ds_c[s], ds_d[s]], axis=0)
            k_s = jnp.concatenate([k_class, k[s * 16 : s * 16 + 16]], axis=0)
            dq_parts.append(gathered_heads(three_pass_tn(ds_s, k_s)))
        dq = stack(dq_parts)
        kn = kn_i[...]
        unit = jnp.concatenate([k[:ROWS]] + [k_class] * SEQS + [q] * SEQS, axis=0)
        scale = jnp.concatenate([kn[:ROWS]] + [kn[ROWS:]] * SEQS + [qn_i[...]] * SEQS, axis=0)
        d_unit = jnp.concatenate([dk, dq], axis=0)
        d_raw = scale * (d_unit - unit * head_sums(d_unit * unit, ones))
        dk_raw, dq_raw = d_raw[: 2 * ROWS], d_raw[2 * ROWS :]
        dv = jnp.concatenate([stack(dv_dates), stack(dv_class)], axis=0)
        c_v = rounded(dot_nt(dv, w[:, 2 * D :]))
        c_k = rounded(wide_dot_nt(dk_raw, w[:, D : 2 * D]))
        c_q = rounded(wide_dot_nt(dq_raw, w[:, :D]))
        dn_kv = rounded(c_v + c_k)
        dn_d = dn_kv[:ROWS]
        dn_c = jnp.sum(rounded(dn_kv[ROWS:] + c_q).reshape(SEQS, 16, D), axis=0)
        fold = lambda rows: jnp.sum(rows.reshape(SEQS, 16, D), axis=0)
        normed = normed_i[...]
        d_k = jnp.concatenate([dk_raw[:ROWS], fold(dk_raw[ROWS:])], axis=0)
        d_v = jnp.concatenate([dv[:ROWS].astype(F32), fold(dv[ROWS:].astype(F32))], axis=0)
        k_hi, k_lo = split(d_k)
        v_hi, v_lo = split(d_v)
        x_hi, x_lo = split(fold(dq_raw))
        d_wk = dot_tn(normed, k_hi) + dot_tn(normed, k_lo)
        d_wv = dot_tn(normed, v_hi) + dot_tn(normed[ROWS:], v_lo[ROWS:])
        d_wq = dot_tn(normed[ROWS:], x_hi) + dot_tn(normed[ROWS:], x_lo)
        xhat = xhat_i[...]
        xhat_c = xhat[ROWS:]
        d_gain = jnp.sum(dn_d * xhat[:ROWS], axis=0, keepdims=True) + jnp.sum(
            dn_c * xhat_c, axis=0, keepdims=True
        )
        z = dn_c * gain_row
        d_norm = rc_i[:, 0:1] * (z - xhat_c * jnp.mean(z * xhat_c, axis=-1, keepdims=True))
        d_class = fold(g.astype(F32)) + d_norm
        out[0:4, 0:64, :] = d_wq.reshape(4, 64, D)
        out[4:8, 0:64, :] = d_wk.reshape(4, 64, D)
        out[8:12, 0:64, :] = d_wv.reshape(4, 64, D)
        out[12:16, 0:64, :] = d_wout.reshape(4, 64, D)
        out[:, 64:72, :] = jnp.zeros((16, 8, D), F32)
        for i in range(16):
            out[i, 64:65, :] = d_class[i : i + 1]
        out[0, 65:66, :] = d_gain


def spatial_forward(
    arrived, gain, wqkv, wout, head, raised_o, u_o, normed_o, xhat_o, inv_o, k_o, kn_o, q_o, qn_o, v_o, a_o, att_o, log_o, hw_o
):
    ones = head_ones()
    w = wqkv[0]
    head_row = head[...]
    u = dot(from_slots(False), arrived[...].reshape(MEMBERS * SLOT, D))
    u_o[...] = u
    inv = lax.rsqrt(jnp.mean(u * u, axis=-1, keepdims=True) + NORM_EPS)
    xhat = u * inv
    normed = (xhat * gain[0:1, :]).astype(BF16)
    xhat_o[...] = xhat
    normed_o[...] = normed
    inv_o[...] = jnp.broadcast_to(inv, (ROWS, 128))
    qkv = dot(normed, w)
    v = qkv[:, 2 * D :].astype(BF16)
    kq = jnp.concatenate([qkv[:, D : 2 * D], qkv[:, :D]], axis=0)
    kq_inv = lax.rsqrt(head_sums(kq * kq, ones) + HEAD_EPS)
    kq_unit = kq * kq_inv
    k, q = kq_unit[:ROWS], kq_unit[ROWS:]
    k_o[...] = k
    q_o[...] = q
    kn_o[...] = kq_inv[:ROWS]
    qn_o[...] = kq_inv[ROWS:]
    v_o[...] = v
    parts = []
    for b in range(TILES_DEV):
        rows = slice(b * PATCHES, b * PATCHES + PATCHES)
        raised = jnp.exp(logits_t(k[rows], spread(q[rows])))
        a = raised / jnp.sum(raised, axis=0, keepdims=True)
        a_o[rows, :] = a
        parts.append(gathered_heads(dot_tn(a.astype(BF16), v[rows])))
    att = jnp.concatenate(parts, axis=0).astype(BF16)
    att_o[...] = att
    h_hi, h_mid = split(head_row)
    h_lo = (head_row - h_hi.astype(F32) - h_mid.astype(F32)).astype(BF16)
    h_rows = jnp.concatenate([h_hi, h_mid, h_lo, jnp.zeros((13, D), BF16)], axis=0)
    hw = jnp.sum(dot_nt(h_rows, wout[0]), axis=0, keepdims=True)
    hw_o[...] = hw
    raw = jnp.sum(u * head_row + att.astype(F32) * hw, axis=-1, keepdims=True)
    logit = CAP * jnp.tanh(raw / CAP)
    log_o[...] = jnp.broadcast_to(logit, (ROWS, 128))
    eye = iota((ROWS, D), 0) == iota((ROWS, D), 1)
    row = jnp.sum(jnp.where(eye, jnp.exp(logit), 0.0), axis=0, keepdims=True)
    raised_o[...] = jnp.broadcast_to(row, (16, D))


def spatial_backward(
    scal, sums, labels, gain, wqkv, wout, head, u_i, normed_i, xhat_i, inv_i, k_i, kn_i, q_i, qn_i, v_i, a_i, att_i, log_i, hw_i, send, out
):
    ones = head_ones()
    w = wqkv[0]
    head_row = head[...]
    u = u_i[...]
    att = att_i[...]
    attf = att.astype(F32)
    eye = iota((ROWS, D), 0) == iota((ROWS, D), 1)
    column = lambda row: jnp.sum(jnp.where(eye, row, 0.0), axis=-1, keepdims=True)
    total = column(jnp.sum(sums[...], axis=0, keepdims=True))
    logit = log_i[:, 0:1]
    mine = column(jnp.where(labels[...] == scal[0], 1.0, 0.0))
    d_logit = (jnp.exp(logit) / total - mine) * (1.0 / 64.0)
    ratio = logit / CAP
    d_raw_logit = d_logit * (1.0 - ratio * ratio)
    ce = mine * (jnp.log(total) - logit)
    lane = iota((1, D), 1)
    loss_row = jnp.zeros((1, D), F32)
    for b in range(TILES_DEV):
        tile_loss = jnp.sum(ce[b * PATCHES : b * PATCHES + PATCHES], axis=0, keepdims=True)
        loss_row = loss_row + jnp.where(lane == scal[1 + b], tile_loss * (1.0 / 768.0), 0.0)
    d_att = (d_raw_logit * hw_i[...]).astype(BF16)
    w_row = jnp.sum(attf * d_raw_logit, axis=0, keepdims=True)
    su_row = jnp.sum(u * d_raw_logit, axis=0, keepdims=True)
    w_hi, w_mid = split(w_row)
    w_lo = (w_row - w_hi.astype(F32) - w_mid.astype(F32)).astype(BF16)
    h_hi, h_mid = split(head_row)
    zero = jnp.zeros((12, D), BF16)
    d_wout = dot_tn(
        jnp.concatenate([w_hi, w_hi, w_mid, w_mid, zero], axis=0),
        jnp.concatenate([h_hi, h_mid, h_hi, h_mid, zero], axis=0),
    )
    w_rows = jnp.concatenate([w_hi, w_mid, w_lo, zero, zero[:1]], axis=0)
    d_head = su_row + jnp.sum(dot(w_rows, wout[0]), axis=0, keepdims=True)
    v = v_i[...]
    k = k_i[...]
    q = q_i[...]
    dv_parts, dk_parts, dq_parts = [], [], []
    for b in range(TILES_DEV):
        rows = slice(b * PATCHES, b * PATCHES + PATCHES)
        a = a_i[rows, :]
        wide = spread(d_att[rows])
        da = rounded(dot_nt(v[rows], wide))
        dv_parts.append(dot(a.astype(BF16), wide).astype(BF16))
        ds = SHARP * a * (da - jnp.sum(da * a, axis=0, keepdims=True))
        q_hi, q_lo = split(spread(q[rows]))
        dk_parts.append(three_pass(ds, q_hi, q_lo))
        dq_parts.append(gathered_heads(three_pass_tn(ds, k[rows])))
    dv = jnp.concatenate(dv_parts, axis=0)
    unit = jnp.concatenate([k, q], axis=0)
    scale = jnp.concatenate([kn_i[...], qn_i[...]], axis=0)
    d_unit = jnp.concatenate(dk_parts + dq_parts, axis=0)
    d_raw = scale * (d_unit - unit * head_sums(d_unit * unit, ones))
    dk_raw, dq_raw = d_raw[:ROWS], d_raw[ROWS:]
    c_v = rounded(dot_nt(dv, w[:, 2 * D :]))
    c_k = rounded(wide_dot_nt(dk_raw, w[:, D : 2 * D]))
    c_q = rounded(wide_dot_nt(dq_raw, w[:, :D]))
    dn = rounded(rounded(c_v + c_k) + c_q)
    normed = normed_i[...]
    q_hi, q_lo = split(dq_raw)
    k_hi, k_lo = split(dk_raw)
    xhat = xhat_i[...]
    z = dn * gain[0:1, :]
    dx = inv_i[:, 0:1] * (z - xhat * jnp.mean(z * xhat, axis=-1, keepdims=True))
    g = (d_raw_logit * head_row + dx).astype(BF16)
    send[0:16] = dot(to_slots(False), g).astype(BF16).reshape(16, SLOT, D)
    send[16:32] = jnp.zeros((16, SLOT, D), BF16)
    out[0:4, 0:64, :] = (dot_tn(normed, q_hi) + dot_tn(normed, q_lo)).reshape(4, 64, D)
    out[4:8, 0:64, :] = (dot_tn(normed, k_hi) + dot_tn(normed, k_lo)).reshape(4, 64, D)
    out[8:12, 0:64, :] = dot_tn(normed, dv).reshape(4, 64, D)
    out[12:16, 0:64, :] = d_wout.reshape(4, 64, D)
    out[:, 64:72, :] = jnp.zeros((16, 8, D), F32)
    out[0, 65:66, :] = jnp.sum(dn * xhat, axis=0, keepdims=True)
    out[1, 65:66, :] = d_head
    out[2, 65:66, :] = loss_row


def first_sum(parts, out):
    total = jnp.sum(parts[...], axis=0)
    for d in range(MEMBERS):
        out[d, 0:4, :] = total[4 * d : 4 * d + 4]
        out[d, 4:8, :] = total[64:68]


def second_sum(parts, out, small):
    total = jnp.sum(parts[...], axis=0)
    out[...] = jnp.broadcast_to(total[None], (MEMBERS, 8, D))
    small[...] = total


def assemble(blocks, other, out):
    mine = jnp.concatenate([blocks[d, 0:4, :] for d in range(MEMBERS)], axis=0)
    small = jnp.concatenate(
        [blocks[0, 4:6, :], other[4:6, :], jnp.zeros((4, D), F32)], axis=0
    )
    out[...] = jnp.broadcast_to(jnp.concatenate([mine, small], axis=0)[None], (MEMBERS, CHUNK, D))


def unpack(first, blocks, loss, d_class, d_gain, d_qkv, d_out, d_head):
    for part in range(3):
        d_qkv[0, :, part * D : part * D + D] = blocks[4 * part : 4 * part + 4, 0:64, :].reshape(D, D)
    d_out[0] = blocks[12:16, 0:64, :].reshape(D, D)
    d_gain[...] = blocks[0, 65:66, :]

    @pl.when(first[0] == 1)
    def _():
        for i in range(16):
            d_class[i : i + 1, :] = blocks[i, 64:65, :]
        d_head[...] = blocks[1, 67:68, :]
        loss[...] = blocks[2, 67:68, :]

    @pl.when(first[0] == 0)
    def _():
        for i in range(16):
            d_class[i : i + 1, :] = blocks[i, 66:67, :]
        d_head[...] = blocks[1, 65:66, :]
        loss[...] = blocks[2, 65:66, :]


VM = pl.BlockSpec(memory_space=pltpu.VMEM)
SM = pl.BlockSpec(memory_space=pltpu.SMEM)


def half(at):
    return pl.BlockSpec((16, SLOT, D), lambda *_: (at, 0, 0), memory_space=pltpu.VMEM)


def call(body, in_specs, outs, *args, name, aliases=None):
    return pl.pallas_call(
        body,
        grid=(1,),
        out_shape=[jax.ShapeDtypeStruct(s, t) for s, t in outs],
        in_specs=in_specs,
        out_specs=[VM] * len(outs),
        input_output_aliases=aliases or {},
        compiler_params=pltpu.CompilerParams(vmem_limit_bytes=48 * 1024 * 1024),
        name=name,
    )(*args)


def encodings(date_days):
    band = jnp.arange(D)
    frequency = jnp.exp((band // 2 * 2).astype(F32) * (-math.log(10000.0) / D))
    phases = date_days.astype(F32)[:, :, None] * frequency
    return jnp.where(band % 2 == 0, jnp.sin(phases), jnp.cos(phases)).reshape(TILES_DEV * 16, D)


def shards(
    pixels,
    date_days,
    clear_count,
    batch_slot,
    labels,
    class_tokens,
    section_gain,
    wqkv,
    wout,
    head_vec,
):
    first = (lax.axis_index("pipe") == 0).astype(I32)[None]
    inner = lax.axis_index("inner").astype(I32)
    head = head_vec.reshape(1, D)
    n = ROWS + 16
    saved = [
        ((n, D), BF16),
        ((n, D), F32),
        ((n, D), F32),
        ((n, D), F32),
        ((16, D), F32),
        ((16, D), F32),
        ((n, D), BF16),
        ((ROWS, 128), F32),
        ((ROWS, 128), F32),
        ((ROWS, D), BF16),
        ((16, 128), F32),
    ]
    send, *res_t = call(
        temporal_forward,
        [SM] + [VM] * 6,
        [((32, SLOT, D), BF16)] + saved,
        clear_count,
        pixels.reshape(ROWS, D),
        encodings(date_days),
        class_tokens,
        section_gain,
        wqkv,
        wout,
        name="temporal_forward",
    )
    arrived = lax.all_to_all(send, ("pipe", "inner"), 0, 0, tiled=True)
    saved = [
        ((ROWS, D), F32),
        ((ROWS, D), BF16),
        ((ROWS, D), F32),
        ((ROWS, 128), F32),
        ((ROWS, D), F32),
        ((ROWS, D), F32),
        ((ROWS, D), F32),
        ((ROWS, D), F32),
        ((ROWS, D), BF16),
        ((ROWS, HEADS * PATCHES), F32),
        ((ROWS, D), BF16),
        ((ROWS, 128), F32),
        ((1, D), F32),
    ]
    raised, *res_s = call(
        spatial_forward,
        [half(0)] + [VM] * 4,
        [((16, D), F32)] + saved,
        arrived,
        section_gain,
        wqkv,
        wout,
        head,
        name="spatial_forward",
    )
    sums = lax.all_to_all(raised, "inner", 0, 0, tiled=True)
    label_row = jnp.pad(labels.reshape(1, ROWS), ((0, 0), (0, D - ROWS)))
    back, grads = call(
        spatial_backward,
        [SM] + [VM] * (6 + len(res_s)),
        [((32, SLOT, D), BF16), ((MEMBERS, CHUNK, D), F32)],
        jnp.concatenate([inner[None], batch_slot]),
        sums,
        label_row,
        section_gain,
        wqkv,
        wout,
        head,
        *res_s,
        name="spatial_backward",
    )
    returned = lax.all_to_all(back, ("pipe", "inner"), 0, 0, tiled=True)
    (grads,) = call(
        temporal_backward,
        [SM, VM, half(1)] + [VM] * (3 + len(res_t)),
        [((MEMBERS, CHUNK, D), F32)],
        first,
        grads,
        returned,
        section_gain,
        wqkv,
        wout,
        *res_t,
        name="temporal_backward",
        aliases={1: 0},
    )
    parts = lax.all_to_all(grads, "inner", 0, 0, tiled=True)
    (parts,) = call(first_sum, [VM], [((MEMBERS, 8, D), F32)], parts, name="first_sum")
    parts = lax.all_to_all(parts, "dp", 0, 0, tiled=True)
    total, small = call(
        second_sum, [VM], [((MEMBERS, 8, D), F32), ((8, D), F32)], parts, name="second_sum"
    )
    other = lax.ppermute(small, "pipe", [(0, 1), (1, 0)])
    blocks = lax.all_to_all(total, "dp", 0, 0, tiled=True)
    (whole,) = call(assemble, [VM, VM], [((MEMBERS, CHUNK, D), F32)], blocks, other, name="assemble")
    whole = lax.all_to_all(whole, "inner", 0, 0, tiled=True)
    loss, d_class, d_gain, d_qkv, d_out, d_head = call(
        unpack,
        [SM, VM],
        [
            ((1, D), F32),
            ((16, D), F32),
            ((1, D), F32),
            ((1, D, 3 * D), F32),
            ((1, D, D), F32),
            ((1, D), F32),
        ],
        first,
        whole,
        name="unpack",
    )
    return (loss[0, :MICRO], d_class, d_gain, d_qkv, d_out, d_head.reshape(D))


def solution(mesh):
    placed = (
        P("dp", "inner", None, None),
        P("dp", None),
        P("dp"),
        P("dp"),
        P("dp", None),
        P(),
        P("pipe", None),
        P("pipe", None, None),
        P("pipe", None, None),
        P(),
    )
    return jax.shard_map(
        shards,
        mesh=mesh,
        in_specs=placed,
        out_specs=(P(), P(), P("pipe", None), P("pipe", None, None), P("pipe", None, None), P()),
        check_vma=False,
    )
```

```python
import functools
import math

import jax
import jax.numpy as jnp
from jax import lax
from jax.experimental import pallas as pl
from jax.experimental.pallas import tpu as pltpu
from jax.sharding import PartitionSpec as P

D = 256
HEADS = 8
CLASSES = 16
PATCHES = 48
MICRO = 4
SHARP = 10.0
CAP = 15.0
NORM_EPS = 1e-05
HEAD_EPS = 1e-06
F32 = jnp.float32
BF16 = jnp.bfloat16
I32 = jnp.int32

TILES_DEV = 4
DATES = 16
CHUNKS = 4
SEQS = PATCHES // CHUNKS
CLASS_CHUNK = CLASSES // CHUNKS
ROWS = SEQS * 16
ALL = CHUNKS * ROWS
MEMBERS = 16
SHARE = 4
CHUNK = 72


def dot(a, b):
    return lax.dot_general(a, b, (((1,), (0,)), ((), ())), preferred_element_type=F32)


def dot_nt(a, b):
    return lax.dot_general(a, b, (((1,), (1,)), ((), ())), preferred_element_type=F32)


def dot_tn(a, b):
    return lax.dot_general(a, b, (((0,), (0,)), ((), ())), preferred_element_type=F32)


def split(x):
    hi = x.astype(BF16)
    return hi, (x - hi.astype(F32)).astype(BF16)


def rounded(x):
    return x.astype(BF16).astype(F32)


def iota(shape, axis):
    return lax.broadcasted_iota(I32, shape, axis)


def head_ones():
    same = (iota((D, D), 0) >> 5) == (iota((D, D), 1) >> 5)
    return jnp.where(same, 1.0, 0.0).astype(BF16)


def head_sums(x, ones):
    hi, lo = split(x)
    return dot(hi, ones) + dot(lo, ones)


def spread(rows_of):
    n = rows_of.shape[0]
    lane_head = iota((n, D), 1) >> 5
    zero = jnp.zeros_like(rows_of)
    return jnp.concatenate([jnp.where(lane_head == h, rows_of, zero) for h in range(HEADS)], axis=0)


def gathered_heads(wide):
    n = wide.shape[0] // HEADS
    lane_head = iota((n, D), 1) >> 5
    out = wide[:n]
    for h in range(1, HEADS):
        out = jnp.where(lane_head == h, wide[h * n : (h + 1) * n], out)
    return out


def logits_t(k, q_wide):
    n = k.shape[0]
    k_hi, k_lo = split(k)
    q_hi, q_lo = split(q_wide)
    both = dot_nt(jnp.concatenate([k_hi, k_lo], axis=0), q_hi)
    return SHARP * (both[:n] + both[n:] + dot_nt(k_hi, q_lo))


def three_pass(x, w_hi, w_lo):
    n = x.shape[0]
    x_hi, x_lo = split(x)
    both = dot(jnp.concatenate([x_hi, x_lo], axis=0), w_hi)
    return both[:n] + both[n:] + dot(x_hi, w_lo)


def three_pass_tn(x, y):
    x_hi, x_lo = split(x)
    y_hi, y_lo = split(y)
    return dot_tn(
        jnp.concatenate([x_hi, x_hi, x_lo], axis=0), jnp.concatenate([y_hi, y_lo, y_hi], axis=0)
    )


def wide_dot_nt(x, w):
    n = x.shape[0]
    hi, lo = split(x)
    both = dot_nt(jnp.concatenate([hi, lo], axis=0), w)
    return both[:n] + both[n:]


def stack(parts):
    return jnp.concatenate(parts, axis=0)


def fold(rows):
    return jnp.sum(rows.reshape(-1, 16, D), axis=0)


def chunk_rows(c):
    return pl.ds(pl.multiple_of(c * ROWS, ROWS), ROWS)


def step(
    scal, counts, slots, labels, pix, enc, cls, gain_a, gain_b, wqkv_a, wqkv_b, wout_a, wout_b, head, out, *scratch
):
    (wt, ws, ot, os, seq_a, seq_b, xhat_t, normed_t, k_t, kn_t, v_t, ad, ac, att_t, q_t, qn_t, e_cls, inv_c,
     u_s, xhat_s, normed_s, inv_s, k_s, kn_s, q_s, qn_s, v_s, a_s, att_s, log_s, tot, rows_s, y_hi, y_lo,
     acc_q, acc_k, acc_v, acc_n, acc_g, d_cls) = scratch
    first = scal[1] == 1
    tile = scal[0] >> 2
    share = scal[0] & 3
    ones = head_ones()
    wt[...] = jnp.where(first, wqkv_a[0], wqkv_b[0])
    ws[...] = jnp.where(first, wqkv_b[0], wqkv_a[0])
    ot[...] = jnp.where(first, wout_a[0], wout_b[0])
    os[...] = jnp.where(first, wout_b[0], wout_a[0])
    gain_t = jnp.where(first, gain_a[...], gain_b[...])
    gain_s = jnp.where(first, gain_b[...], gain_a[...])
    head_row = head[...]
    h_hi, h_mid = split(head_row)
    h_lo = (head_row - h_hi.astype(F32) - h_mid.astype(F32)).astype(BF16)
    h_rows = stack([h_hi, h_mid, h_lo, jnp.zeros((13, D), BF16)])
    rows_s[...] = jnp.zeros((8, D), F32)
    rows_s[0:1, :] = jnp.sum(dot_nt(h_rows, os[...]), axis=0, keepdims=True)
    rows_s[6:7, :] = gain_t
    rows_s[7:8, :] = gain_s
    for ref in (acc_q, acc_k, acc_v, acc_n, acc_g):
        ref[...] = jnp.zeros((16, D), F32)

    xc = cls[...].astype(F32)
    inv = lax.rsqrt(jnp.mean(xc * xc, axis=-1, keepdims=True) + NORM_EPS)
    xhat_c = xc * inv
    normed_c = (xhat_c * gain_t).astype(BF16)
    qkv_c = dot(normed_c, wt[...])
    kq = stack([qkv_c[:, D : 2 * D], qkv_c[:, :D]])
    kq_inv = lax.rsqrt(head_sums(kq * kq, ones) + HEAD_EPS)
    kq_unit = kq * kq_inv
    xhat_t[ALL:, :] = xhat_c
    normed_t[ALL:, :] = normed_c
    inv_c[...] = jnp.broadcast_to(inv, (16, 128))
    k_t[ALL:, :] = kq_unit[:16]
    kn_t[ALL:, :] = kq_inv[:16]
    q_t[...] = kq_unit[16:]
    qn_t[...] = kq_inv[16:]
    v_t[ALL:, :] = qkv_c[:, 2 * D :].astype(BF16)
    e_cls[...] = jnp.exp(logits_t(kq_unit[:16], spread(kq_unit[16:])))

    @pl.loop(0, CHUNKS)
    def _(c):
        rows = chunk_rows(c)
        tile_enc = enc[pl.ds(pl.multiple_of(tile * 16, 16), 16), :]
        pixel = pix[pl.ds(c * 4, 4), :, :].astype(F32).reshape(SEQS, 16, D)
        x = (pixel + tile_enc[None]).reshape(ROWS, D)
        inv = lax.rsqrt(jnp.mean(x * x, axis=-1, keepdims=True) + NORM_EPS)
        xhat = x * inv
        normed = (xhat * rows_s[6:7, :]).astype(BF16)
        xhat_t[rows, :] = xhat
        normed_t[rows, :] = normed
        kv = dot(normed, wt[:, D:])
        v = kv[:, D:].astype(BF16)
        v_t[rows, :] = v
        k = kv[:, :D]
        k_inv = lax.rsqrt(head_sums(k * k, head_ones()) + HEAD_EPS)
        k = k * k_inv
        k_t[rows, :] = k
        kn_t[rows, :] = k_inv
        raised = jnp.exp(logits_t(k, spread(q_t[...])))
        shown = (iota((ROWS, 128), 0) & 15) < counts[tile]
        e_dates = jnp.where(shown, raised, 0.0).reshape(SEQS, DATES, 128)
        e_class = e_cls[...]
        total = jnp.sum(e_dates, axis=1, keepdims=True) + jnp.sum(e_class, axis=0, keepdims=True)[None]
        a_dates = e_dates / total
        a_class = e_class[None] / total
        ad[rows, :] = a_dates.reshape(ROWS, 128)
        ac[rows, :] = a_class.reshape(ROWS, 128)
        v_class = v_t[ALL:, :]
        parts = []
        for s in range(SEQS):
            weights = stack([a_class[s], a_dates[s]]).astype(BF16)
            values = stack([v_class, v[s * 16 : s * 16 + 16]])
            parts.append(gathered_heads(dot_tn(weights, values)))
        att = stack(parts).astype(BF16)
        att_t[rows, :] = att
        updated = rounded(stack([cls[...].astype(F32)] * SEQS) + dot(att, ot[...]))
        seq_a[rows, :] = updated[:, :128]
        seq_b[rows, :] = updated[:, 128:]

    for i in range(CLASSES):
        u_s[i * PATCHES : (i + 1) * PATCHES, :128] = seq_a[pl.ds(i, PATCHES, stride=16), :]
        u_s[i * PATCHES : (i + 1) * PATCHES, 128:] = seq_b[pl.ds(i, PATCHES, stride=16), :]

    @pl.loop(0, CHUNKS)
    def _(c):
        rows = chunk_rows(c)
        u = u_s[rows, :]
        inv = lax.rsqrt(jnp.mean(u * u, axis=-1, keepdims=True) + NORM_EPS)
        xhat = u * inv
        normed = (xhat * rows_s[7:8, :]).astype(BF16)
        xhat_s[rows, :] = xhat
        normed_s[rows, :] = normed
        inv_s[rows, :] = jnp.broadcast_to(inv, (ROWS, 128))
        qkv = dot(normed, ws[...])
        v = qkv[:, 2 * D :].astype(BF16)
        kq = stack([qkv[:, D : 2 * D], qkv[:, :D]])
        kq_inv = lax.rsqrt(head_sums(kq * kq, head_ones()) + HEAD_EPS)
        kq_unit = kq * kq_inv
        k, q = kq_unit[:ROWS], kq_unit[ROWS:]
        k_s[rows, :] = k
        q_s[rows, :] = q
        kn_s[rows, :] = kq_inv[:ROWS]
        qn_s[rows, :] = kq_inv[ROWS:]
        v_s[rows, :] = v
        parts, held = [], []
        for b in range(CLASS_CHUNK):
            part = slice(b * PATCHES, b * PATCHES + PATCHES)
            raised = jnp.exp(logits_t(k[part], spread(q[part])))
            a = raised / jnp.sum(raised, axis=0, keepdims=True)
            held.append(a)
            parts.append(gathered_heads(dot_tn(a.astype(BF16), v[part])))
        a_s[rows, :] = stack(held)
        att = stack(parts).astype(BF16)
        att_s[rows, :] = att
        raw = jnp.sum(u * head[...] + att.astype(F32) * rows_s[0:1, :], axis=-1, keepdims=True)
        log_s[rows, :] = jnp.broadcast_to(CAP * jnp.tanh(raw / CAP), (ROWS, 128))

    tot[...] = jnp.sum(jnp.exp(log_s[...]).reshape(CLASSES, PATCHES, 128), axis=0)

    @pl.loop(0, CHUNKS)
    def _(c):
        rows = chunk_rows(c)
        u = u_s[rows, :]
        xhat = xhat_s[rows, :]
        attf = att_s[rows, :].astype(F32)
        logit = log_s[rows, 0:1]
        total = stack([tot[:, 0:1]] * CLASS_CHUNK)
        eye = iota((PATCHES, PATCHES), 0) == iota((PATCHES, PATCHES), 1)
        label_row = labels[pl.ds(tile, 1), :].astype(F32)
        label = jnp.sum(jnp.where(eye, label_row, 0.0), axis=-1, keepdims=True)
        base = (c * CLASS_CHUNK).astype(F32)
        mine = stack([jnp.where(label == base + b, 1.0, 0.0) for b in range(CLASS_CHUNK)])
        d_logit = (jnp.exp(logit) / total - mine) * (1.0 / 64.0)
        ratio = logit / CAP
        d_raw_logit = d_logit * (1.0 - ratio * ratio)
        ce = jnp.sum(mine * (jnp.log(total) - logit), axis=0, keepdims=True) * (1.0 / 768.0)
        rows_s[5:6, :] += jnp.where(iota((1, D), 1) == slots[tile], ce, 0.0)
        rows_s[1:2, :] += jnp.sum(attf * d_raw_logit, axis=0, keepdims=True)
        rows_s[2:3, :] += jnp.sum(u * d_raw_logit, axis=0, keepdims=True)
        d_att = (d_raw_logit * rows_s[0:1, :]).astype(BF16)
        v = v_s[rows, :]
        k = k_s[rows, :]
        q = q_s[rows, :]
        a_all = a_s[rows, :]
        dv_parts, dk_parts, dq_parts = [], [], []
        for b in range(CLASS_CHUNK):
            part = slice(b * PATCHES, b * PATCHES + PATCHES)
            a = a_all[part]
            wide = spread(d_att[part])
            da = rounded(dot_nt(v[part], wide))
            dv_parts.append(dot(a.astype(BF16), wide).astype(BF16))
            ds = SHARP * a * (da - jnp.sum(da * a, axis=0, keepdims=True))
            q_hi, q_lo = split(spread(q[part]))
            dk_parts.append(three_pass(ds, q_hi, q_lo))
            dq_parts.append(gathered_heads(three_pass_tn(ds, k[part])))
        dv = stack(dv_parts)
        unit = stack([k, q])
        scale = stack([kn_s[rows, :], qn_s[rows, :]])
        d_unit = stack(dk_parts + dq_parts)
        d_raw = scale * (d_unit - unit * head_sums(d_unit * unit, head_ones()))
        dk_raw, dq_raw = d_raw[:ROWS], d_raw[ROWS:]
        c_v = rounded(dot_nt(dv, ws[:, 2 * D :]))
        c_k = rounded(wide_dot_nt(dk_raw, ws[:, D : 2 * D]))
        c_q = rounded(wide_dot_nt(dq_raw, ws[:, :D]))
        dn = rounded(rounded(c_v + c_k) + c_q)
        rows_s[4:5, :] += jnp.sum(dn * xhat, axis=0, keepdims=True)
        y = jnp.where(share == 0, dq_raw, jnp.where(share == 1, dk_raw, dv.astype(F32)))
        hi, lo = split(y)
        y_hi[rows, :] = hi
        y_lo[rows, :] = lo
        z = dn * rows_s[7:8, :]
        dx = inv_s[rows, 0:1] * (z - xhat * jnp.mean(z * xhat, axis=-1, keepdims=True))
        u_s[rows, :] = rounded(d_raw_logit * head[...] + dx)

    for i in range(CLASSES):
        seq_a[pl.ds(i, PATCHES, stride=16), :] = u_s[i * PATCHES : (i + 1) * PATCHES, :128]
        seq_b[pl.ds(i, PATCHES, stride=16), :] = u_s[i * PATCHES : (i + 1) * PATCHES, 128:]

    w_row = rows_s[1:2, :]
    w_hi, w_mid = split(w_row)
    w_lo = (w_row - w_hi.astype(F32) - w_mid.astype(F32)).astype(BF16)
    zero = jnp.zeros((12, D), BF16)
    w_rows = stack([w_hi, w_mid, w_lo, zero, zero[:1]])
    d_head = rows_s[2:3, :] + jnp.sum(dot(w_rows, os[...]), axis=0, keepdims=True)

    @pl.when(jnp.logical_and(scal[1] == 0, share < 3))
    def _():
        x = normed_s[...]
        d_w = dot_tn(x, y_hi[0:ALL, :]) + dot_tn(x, y_lo[0:ALL, :])
        out[:, 0:64, :] = d_w.reshape(SHARE, 64, D)

    @pl.when(jnp.logical_and(scal[1] == 0, share == 3))
    def _():
        d_w = dot_tn(stack([w_hi, w_hi, w_mid, w_mid, zero]), stack([h_hi, h_mid, h_hi, h_mid, zero]))
        out[:, 0:64, :] = d_w.reshape(SHARE, 64, D)

    @pl.loop(0, CHUNKS)
    def _(c):
        rows = chunk_rows(c)
        g = jnp.concatenate([seq_a[rows, :], seq_b[rows, :]], axis=1).astype(BF16)
        d_att = dot_nt(g, ot[...]).astype(BF16)
        v = v_t[rows, :]
        v_class = v_t[ALL:, :]
        k = k_t[rows, :]
        k_class = k_t[ALL:, :]
        q = q_t[...]
        a_dates = ad[rows, :]
        a_class = ac[rows, :]
        da_class, da_dates, dv_class, dv_dates = [], [], [], []
        for s in range(SEQS):
            part = slice(s * 16, s * 16 + 16)
            wide = spread(d_att[part])
            values = stack([v_class, v[part]])
            weights = stack([a_class[part], a_dates[part]]).astype(BF16)
            da = rounded(dot_nt(values, wide))
            dv = dot(weights, wide).astype(BF16)
            da_class.append(da[:16])
            da_dates.append(da[16:])
            dv_class.append(dv[:16])
            dv_dates.append(dv[16:])
        cube = lambda m: m.reshape(SEQS, 16, 128)
        da_c, da_d = stack(da_class), stack(da_dates)
        both = jnp.sum(cube(da_c * a_class), axis=1, keepdims=True) + jnp.sum(
            cube(da_d * a_dates), axis=1, keepdims=True
        )
        ds_c = SHARP * cube(a_class) * (cube(da_c) - both)
        ds_d = SHARP * cube(a_dates) * (cube(da_d) - both)
        q_hi, q_lo = split(spread(q))
        dk = three_pass(stack([ds_d.reshape(ROWS, 128), ds_c.reshape(ROWS, 128)]), q_hi, q_lo)
        dq_parts = []
        for s in range(SEQS):
            ds_s = stack([ds_c[s], ds_d[s]])
            k_all = stack([k_class, k[s * 16 : s * 16 + 16]])
            dq_parts.append(gathered_heads(three_pass_tn(ds_s, k_all)))
        unit = stack([k] + [k_class] * SEQS + [q] * SEQS)
        scale = stack([kn_t[rows, :]] + [kn_t[ALL:, :]] * SEQS + [qn_t[...]] * SEQS)
        d_unit = stack([dk] + dq_parts)
        d_raw = scale * (d_unit - unit * head_sums(d_unit * unit, head_ones()))
        dk_raw, dq_raw = d_raw[: 2 * ROWS], d_raw[2 * ROWS :]
        dv = stack(dv_dates + dv_class)
        c_v = rounded(dot_nt(dv, wt[:, 2 * D :]))
        c_k = rounded(wide_dot_nt(dk_raw, wt[:, D : 2 * D]))
        c_q = rounded(wide_dot_nt(dq_raw, wt[:, :D]))
        dn = rounded(c_v + c_k)
        rows_s[3:4, :] += jnp.sum(dn[:ROWS] * xhat_t[rows, :], axis=0, keepdims=True)
        acc_n[...] += fold(rounded(dn[ROWS:] + c_q))
        acc_g[...] += fold(g.astype(F32))
        acc_q[...] += fold(dq_raw)
        acc_k[...] += fold(dk_raw[ROWS:])
        acc_v[...] += fold(dv[ROWS:].astype(F32))
        of_dates = jnp.where(share == 1, dk_raw[:ROWS], dv[:ROWS].astype(F32))
        y = jnp.where(share == 0, 0.0, jnp.where(share == 3, g.astype(F32), of_dates))
        hi, lo = split(y)

        @pl.when(first)
        def _():
            y_hi[rows, :] = hi
            y_lo[rows, :] = lo

    dn_c = acc_n[...]
    xhat_c = xhat_t[ALL:, :]
    z = dn_c * rows_s[6:7, :]
    d_norm = inv_c[:, 0:1] * (z - xhat_c * jnp.mean(z * xhat_c, axis=-1, keepdims=True))
    d_cls[...] = acc_g[...] + d_norm
    gain_grad_t = rows_s[3:4, :] + jnp.sum(dn_c * xhat_c, axis=0, keepdims=True)
    gain_grad = jnp.where(first, gain_grad_t, rows_s[4:5, :])

    @pl.when(jnp.logical_and(first, share < 3))
    def _():
        y = jnp.where(share == 0, acc_q[...], jnp.where(share == 1, acc_k[...], acc_v[...]))
        hi, lo = split(y)
        y_hi[ALL:, :] = hi
        y_lo[ALL:, :] = lo
        x = normed_t[...]
        d_w = dot_tn(x, y_hi[...]) + dot_tn(x, y_lo[...])
        out[:, 0:64, :] = d_w.reshape(SHARE, 64, D)

    @pl.when(jnp.logical_and(first, share == 3))
    def _():
        out[:, 0:64, :] = dot_tn(att_t[...], y_hi[0:ALL, :]).reshape(SHARE, 64, D)

    out[:, 64:72, :] = jnp.zeros((SHARE, 8, D), F32)
    for b in range(SHARE):
        out[b, 64:65, :] = d_cls[pl.ds(4 * share + b, 1), :]
    out[0, 65:66, :] = jnp.where(share == 0, gain_grad, jnp.where(share == 1, d_head, rows_s[5:6, :]))


STEP_SCRATCH = [
    ((D, 3 * D), BF16), ((D, 3 * D), BF16), ((D, D), BF16), ((D, D), BF16),
    ((ALL, 128), F32), ((ALL, 128), F32), ((ALL + 16, D), F32), ((ALL + 16, D), BF16), ((ALL + 16, D), F32), ((ALL + 16, D), F32),
    ((ALL + 16, D), BF16), ((ALL, 128), F32), ((ALL, 128), F32), ((ALL, D), BF16),
    ((16, D), F32), ((16, D), F32), ((16, 128), F32), ((16, 128), F32),
    ((ALL, D), F32), ((ALL, D), F32), ((ALL, D), BF16), ((ALL, 128), F32),
    ((ALL, D), F32), ((ALL, D), F32), ((ALL, D), F32), ((ALL, D), F32), ((ALL, D), BF16),
    ((ALL, HEADS * PATCHES), F32), ((ALL, D), BF16), ((ALL, 128), F32), ((PATCHES, 128), F32), ((8, D), F32),
    ((ALL + 16, D), BF16), ((ALL + 16, D), BF16),
    ((16, D), F32), ((16, D), F32), ((16, D), F32), ((16, D), F32), ((16, D), F32), ((16, D), F32),
]


def first_sum(parts, out):
    total = jnp.sum(parts[...], axis=0)
    for d in range(MEMBERS):
        out[d, 0:4, :] = total[4 * d : 4 * d + 4]
        out[d, 4:8, :] = total[64:68]


def second_sum(parts, out):
    out[...] = jnp.broadcast_to(jnp.sum(parts[...], axis=0)[None], (MEMBERS, 8, D))


def assemble(blocks, out):
    mine = [blocks[d, 0:4, :] for d in range(MEMBERS)]
    whole = stack(mine + [blocks[0, 4:8, :], jnp.zeros((4, D), F32)])
    out[...] = jnp.broadcast_to(whole[None], (MEMBERS, CHUNK, D))


def unpack(blocks, loss, d_class, d_gain, d_qkv, d_out, d_head):
    for b in range(SHARE):
        rows = slice(64 * b, 64 * b + 64)
        for part in range(3):
            d_qkv[0, rows, part * D : part * D + D] = blocks[4 * b + part, 0:64, :]
        d_out[0, rows, :] = blocks[4 * b + 3, 0:64, :]
        for part in range(4):
            at = 4 * part + b
            d_class[at : at + 1, :] = blocks[4 * b + part, 64:65, :]
    d_gain[...] = blocks[0, 65:66, :]
    d_head[...] = blocks[1, 65:66, :]
    loss[...] = blocks[2, 65:66, :]


VM = pl.BlockSpec()
SM = pl.BlockSpec(memory_space=pltpu.SMEM)


def call(body, in_specs, outs, *args, name, scratch=()):
    return pl.pallas_call(
        body,
        out_shape=[jax.ShapeDtypeStruct(s, t) for s, t in outs],
        in_specs=in_specs,
        out_specs=[VM] * len(outs),
        scratch_shapes=[pltpu.VMEM(s, t) for s, t in scratch],
        compiler_params=pltpu.CompilerParams(vmem_limit_bytes=48 * 1024 * 1024),
        name=name,
    )(*args)


def encodings(date_days):
    band = jnp.arange(D)
    frequency = jnp.exp((band // 2 * 2).astype(F32) * (-math.log(10000.0) / D))
    phases = date_days.astype(F32)[:, :, None] * frequency
    return jnp.where(band % 2 == 0, jnp.sin(phases), jnp.cos(phases)).reshape(TILES_DEV * 16, D)


def shards(
    pixels,
    date_days,
    clear_count,
    batch_slot,
    labels,
    class_tokens,
    section_gain,
    wqkv,
    wout,
    head_vec,
):
    first = (lax.axis_index("pipe") == 0).astype(I32)
    inner = lax.axis_index("inner").astype(I32)
    swap = lambda v: lax.ppermute(v, "pipe", [(0, 1), (1, 0)])
    by_dest = jnp.repeat(pixels.reshape(TILES_DEV, PATCHES, D), SHARE, axis=0)
    whole_tile = lax.all_to_all(by_dest, "inner", 0, 0, tiled=True)
    (grads,) = call(
        step,
        [SM] * 3 + [VM] * 11,
        [((SHARE, CHUNK, D), F32)],
        jnp.stack([inner, first]),
        clear_count,
        batch_slot,
        labels,
        whole_tile,
        encodings(date_days),
        class_tokens,
        section_gain,
        swap(section_gain),
        wqkv,
        swap(wqkv),
        wout,
        swap(wout),
        head_vec.reshape(1, D),
        name="step",
        scratch=STEP_SCRATCH,
    )
    sharers = [[SHARE * b + s for b in range(TILES_DEV)] for s in range(SHARE)]
    parts = lax.all_to_all(grads, "inner", 0, 0, tiled=True, axis_index_groups=sharers)
    (parts,) = call(first_sum, [VM], [((MEMBERS, 8, D), F32)], parts, name="first_sum")
    parts = lax.all_to_all(parts, "dp", 0, 0, tiled=True)
    (total,) = call(second_sum, [VM], [((MEMBERS, 8, D), F32)], parts, name="second_sum")
    blocks = lax.all_to_all(total, "dp", 0, 0, tiled=True)
    (whole,) = call(assemble, [VM], [((MEMBERS, CHUNK, D), F32)], blocks, name="assemble")
    whole = lax.all_to_all(whole, "inner", 0, 0, tiled=True)
    loss, d_class, d_gain, d_qkv, d_out, d_head = call(
        unpack,
        [VM],
        [
            ((1, D), F32),
            ((16, D), F32),
            ((1, D), F32),
            ((1, D, 3 * D), F32),
            ((1, D, D), F32),
            ((1, D), F32),
        ],
        whole,
        name="unpack",
    )
    return (loss[0, :MICRO], d_class, d_gain, d_qkv, d_out, d_head.reshape(D))


def solution(mesh):
    placed = (
        P("dp", "inner", None, None),
        P("dp", None),
        P("dp"),
        P("dp"),
        P("dp", None),
        P(),
        P("pipe", None),
        P("pipe", None, None),
        P("pipe", None, None),
        P(),
    )
    return jax.shard_map(
        shards,
        mesh=mesh,
        in_specs=placed,
        out_specs=(P(), P(), P("pipe", None), P("pipe", None, None), P("pipe", None, None), P()),
        check_vma=False,
    )
```

```python
import math

import jax
import jax.numpy as jnp
from jax import lax
from jax.experimental import pallas as pl
from jax.experimental.pallas import tpu as pltpu
from jax.sharding import Mesh, PartitionSpec as P


D = 256
HEADS = 8
CLASSES = 16
PATCHES = 48
MICRO = 4
SHARP = 10.0
CAP = 15.0
NORM_EPS = 1e-05
HEAD_EPS = 1e-06
F32 = jnp.float32
BF16 = jnp.bfloat16
I32 = jnp.int32

TILES_DEV = 4
DATES = 16
CHUNKS = 4
SEQS = PATCHES // CHUNKS
CLASS_CHUNK = CLASSES // CHUNKS
ROWS = SEQS * 16
ALL = CHUNKS * ROWS
MEMBERS = 16
SHARE = 4
YS = 8
OWNERS = 64
CHUNK = 72
DP = ("y", "core")
INNER = ("b", "r")


def dot(a, b):
    return lax.dot_general(a, b, (((1,), (0,)), ((), ())), preferred_element_type=F32)


def dot_nt(a, b):
    return lax.dot_general(a, b, (((1,), (1,)), ((), ())), preferred_element_type=F32)


def dot_tn(a, b):
    return lax.dot_general(a, b, (((0,), (0,)), ((), ())), preferred_element_type=F32)


def split(x):
    hi = x.astype(BF16)
    return hi, (x - hi.astype(F32)).astype(BF16)


def rounded(x):
    return x.astype(BF16).astype(F32)


def iota(shape, axis):
    return lax.broadcasted_iota(I32, shape, axis)


def head_ones():
    same = (iota((D, D), 0) >> 5) == (iota((D, D), 1) >> 5)
    return jnp.where(same, 1.0, 0.0).astype(BF16)


def head_sums(x, ones):
    hi, lo = split(x)
    return dot(hi, ones) + dot(lo, ones)


def spread(rows_of):
    n = rows_of.shape[0]
    lane_head = iota((n, D), 1) >> 5
    zero = jnp.zeros_like(rows_of)
    return jnp.concatenate([jnp.where(lane_head == h, rows_of, zero) for h in range(HEADS)], axis=0)


def gathered_heads(wide):
    n = wide.shape[0] // HEADS
    lane_head = iota((n, D), 1) >> 5
    out = wide[:n]
    for h in range(1, HEADS):
        out = jnp.where(lane_head == h, wide[h * n : (h + 1) * n], out)
    return out


def logits_t(k, q_wide):
    n = k.shape[0]
    k_hi, k_lo = split(k)
    q_hi, q_lo = split(q_wide)
    both = dot_nt(jnp.concatenate([k_hi, k_lo], axis=0), q_hi)
    return SHARP * (both[:n] + both[n:] + dot_nt(k_hi, q_lo))


def three_pass(x, w_hi, w_lo):
    n = x.shape[0]
    x_hi, x_lo = split(x)
    both = dot(jnp.concatenate([x_hi, x_lo], axis=0), w_hi)
    return both[:n] + both[n:] + dot(x_hi, w_lo)


def three_pass_tn(x, y):
    x_hi, x_lo = split(x)
    y_hi, y_lo = split(y)
    return dot_tn(
        jnp.concatenate([x_hi, x_hi, x_lo], axis=0), jnp.concatenate([y_hi, y_lo, y_hi], axis=0)
    )


def wide_dot_nt(x, w):
    n = x.shape[0]
    hi, lo = split(x)
    both = dot_nt(jnp.concatenate([hi, lo], axis=0), w)
    return both[:n] + both[n:]


def stack(parts):
    return jnp.concatenate(parts, axis=0)


def fold(rows):
    return jnp.sum(rows.reshape(-1, 16, D), axis=0)


def chunk_rows(c):
    return pl.ds(pl.multiple_of(c * ROWS, ROWS), ROWS)


def put_tiles(out, d_w):
    for n in range(OWNERS):
        row, lane = 8 * (n // 2), 128 * (n % 2)
        out[n, 0:8, :] = d_w[row : row + 8, lane : lane + 128]


def step(
    scal, counts, slots, labels, pix, enc, cls, gain_a, gain_b, wqkv_a, wqkv_b, wout_a, wout_b, head, out, *scratch
):
    (wt, ws, ot, os, seq_a, seq_b, xhat_t, normed_t, k_t, kn_t, v_t, ad, ac, att_t, q_t, qn_t, e_cls, inv_c,
     u_s, xhat_s, normed_s, inv_s, k_s, kn_s, q_s, qn_s, v_s, a_s, att_s, log_s, tot, rows_s, y_hi, y_lo,
     acc_q, acc_k, acc_v, acc_n, acc_g, d_cls) = scratch
    first = scal[1] == 1
    tile = scal[0] >> 2
    share = scal[0] & 3
    ones = head_ones()
    wt[...] = jnp.where(first, wqkv_a[0], wqkv_b[0])
    ws[...] = jnp.where(first, wqkv_b[0], wqkv_a[0])
    ot[...] = jnp.where(first, wout_a[0], wout_b[0])
    os[...] = jnp.where(first, wout_b[0], wout_a[0])
    gain_t = jnp.where(first, gain_a[...], gain_b[...])
    gain_s = jnp.where(first, gain_b[...], gain_a[...])
    head_row = head[...]
    h_hi, h_mid = split(head_row)
    h_lo = (head_row - h_hi.astype(F32) - h_mid.astype(F32)).astype(BF16)
    h_rows = stack([h_hi, h_mid, h_lo, jnp.zeros((13, D), BF16)])
    rows_s[...] = jnp.zeros((8, D), F32)
    rows_s[0:1, :] = jnp.sum(dot_nt(h_rows, os[...]), axis=0, keepdims=True)
    rows_s[6:7, :] = gain_t
    rows_s[7:8, :] = gain_s
    for ref in (acc_q, acc_k, acc_v, acc_n, acc_g):
        ref[...] = jnp.zeros((16, D), F32)

    xc = cls[...].astype(F32)
    inv = lax.rsqrt(jnp.mean(xc * xc, axis=-1, keepdims=True) + NORM_EPS)
    xhat_c = xc * inv
    normed_c = (xhat_c * gain_t).astype(BF16)
    qkv_c = dot(normed_c, wt[...])
    kq = stack([qkv_c[:, D : 2 * D], qkv_c[:, :D]])
    kq_inv = lax.rsqrt(head_sums(kq * kq, ones) + HEAD_EPS)
    kq_unit = kq * kq_inv
    xhat_t[ALL:, :] = xhat_c
    normed_t[ALL:, :] = normed_c
    inv_c[...] = jnp.broadcast_to(inv, (16, 128))
    k_t[ALL:, :] = kq_unit[:16]
    kn_t[ALL:, :] = kq_inv[:16]
    q_t[...] = kq_unit[16:]
    qn_t[...] = kq_inv[16:]
    v_t[ALL:, :] = qkv_c[:, 2 * D :].astype(BF16)
    e_cls[...] = jnp.exp(logits_t(kq_unit[:16], spread(kq_unit[16:])))

    @pl.loop(0, CHUNKS)
    def _(c):
        rows = chunk_rows(c)
        tile_enc = enc[pl.ds(pl.multiple_of(tile * 16, 16), 16), :]
        pixel = pix[pl.ds(c * 4, 4), :, :].astype(F32).reshape(SEQS, 16, D)
        x = (pixel + tile_enc[None]).reshape(ROWS, D)
        inv = lax.rsqrt(jnp.mean(x * x, axis=-1, keepdims=True) + NORM_EPS)
        xhat = x * inv
        normed = (xhat * rows_s[6:7, :]).astype(BF16)
        xhat_t[rows, :] = xhat
        normed_t[rows, :] = normed
        kv = dot(normed, wt[:, D:])
        v = kv[:, D:].astype(BF16)
        v_t[rows, :] = v
        k = kv[:, :D]
        k_inv = lax.rsqrt(head_sums(k * k, head_ones()) + HEAD_EPS)
        k = k * k_inv
        k_t[rows, :] = k
        kn_t[rows, :] = k_inv
        raised = jnp.exp(logits_t(k, spread(q_t[...])))
        shown = (iota((ROWS, 128), 0) & 15) < counts[tile]
        e_dates = jnp.where(shown, raised, 0.0).reshape(SEQS, DATES, 128)
        e_class = e_cls[...]
        total = jnp.sum(e_dates, axis=1, keepdims=True) + jnp.sum(e_class, axis=0, keepdims=True)[None]
        a_dates = e_dates / total
        a_class = e_class[None] / total
        ad[rows, :] = a_dates.reshape(ROWS, 128)
        ac[rows, :] = a_class.reshape(ROWS, 128)
        v_class = v_t[ALL:, :]
        parts = []
        for s in range(SEQS):
            weights = stack([a_class[s], a_dates[s]]).astype(BF16)
            values = stack([v_class, v[s * 16 : s * 16 + 16]])
            parts.append(gathered_heads(dot_tn(weights, values)))
        att = stack(parts).astype(BF16)
        att_t[rows, :] = att
        updated = rounded(stack([cls[...].astype(F32)] * SEQS) + dot(att, ot[...]))
        seq_a[rows, :] = updated[:, :128]
        seq_b[rows, :] = updated[:, 128:]

    for i in range(CLASSES):
        u_s[i * PATCHES : (i + 1) * PATCHES, :128] = seq_a[pl.ds(i, PATCHES, stride=16), :]
        u_s[i * PATCHES : (i + 1) * PATCHES, 128:] = seq_b[pl.ds(i, PATCHES, stride=16), :]

    @pl.loop(0, CHUNKS)
    def _(c):
        rows = chunk_rows(c)
        u = u_s[rows, :]
        inv = lax.rsqrt(jnp.mean(u * u, axis=-1, keepdims=True) + NORM_EPS)
        xhat = u * inv
        normed = (xhat * rows_s[7:8, :]).astype(BF16)
        xhat_s[rows, :] = xhat
        normed_s[rows, :] = normed
        inv_s[rows, :] = jnp.broadcast_to(inv, (ROWS, 128))
        qkv = dot(normed, ws[...])
        v = qkv[:, 2 * D :].astype(BF16)
        kq = stack([qkv[:, D : 2 * D], qkv[:, :D]])
        kq_inv = lax.rsqrt(head_sums(kq * kq, head_ones()) + HEAD_EPS)
        kq_unit = kq * kq_inv
        k, q = kq_unit[:ROWS], kq_unit[ROWS:]
        k_s[rows, :] = k
        q_s[rows, :] = q
        kn_s[rows, :] = kq_inv[:ROWS]
        qn_s[rows, :] = kq_inv[ROWS:]
        v_s[rows, :] = v
        parts, held = [], []
        for b in range(CLASS_CHUNK):
            part = slice(b * PATCHES, b * PATCHES + PATCHES)
            raised = jnp.exp(logits_t(k[part], spread(q[part])))
            a = raised / jnp.sum(raised, axis=0, keepdims=True)
            held.append(a)
            parts.append(gathered_heads(dot_tn(a.astype(BF16), v[part])))
        a_s[rows, :] = stack(held)
        att = stack(parts).astype(BF16)
        att_s[rows, :] = att
        raw = jnp.sum(u * head[...] + att.astype(F32) * rows_s[0:1, :], axis=-1, keepdims=True)
        log_s[rows, :] = jnp.broadcast_to(CAP * jnp.tanh(raw / CAP), (ROWS, 128))

    tot[...] = jnp.sum(jnp.exp(log_s[...]).reshape(CLASSES, PATCHES, 128), axis=0)

    @pl.loop(0, CHUNKS)
    def _(c):
        rows = chunk_rows(c)
        u = u_s[rows, :]
        xhat = xhat_s[rows, :]
        attf = att_s[rows, :].astype(F32)
        logit = log_s[rows, 0:1]
        total = stack([tot[:, 0:1]] * CLASS_CHUNK)
        eye = iota((PATCHES, PATCHES), 0) == iota((PATCHES, PATCHES), 1)
        label_row = labels[pl.ds(tile, 1), :].astype(F32)
        label = jnp.sum(jnp.where(eye, label_row, 0.0), axis=-1, keepdims=True)
        base = (c * CLASS_CHUNK).astype(F32)
        mine = stack([jnp.where(label == base + b, 1.0, 0.0) for b in range(CLASS_CHUNK)])
        d_logit = (jnp.exp(logit) / total - mine) * (1.0 / 64.0)
        ratio = logit / CAP
        d_raw_logit = d_logit * (1.0 - ratio * ratio)
        ce = jnp.sum(mine * (jnp.log(total) - logit), axis=0, keepdims=True) * (1.0 / 768.0)
        rows_s[5:6, :] += jnp.where(iota((1, D), 1) == slots[tile], ce, 0.0)
        rows_s[1:2, :] += jnp.sum(attf * d_raw_logit, axis=0, keepdims=True)
        rows_s[2:3, :] += jnp.sum(u * d_raw_logit, axis=0, keepdims=True)
        d_att = (d_raw_logit * rows_s[0:1, :]).astype(BF16)
        v = v_s[rows, :]
        k = k_s[rows, :]
        q = q_s[rows, :]
        a_all = a_s[rows, :]
        dv_parts, dk_parts, dq_parts = [], [], []
        for b in range(CLASS_CHUNK):
            part = slice(b * PATCHES, b * PATCHES + PATCHES)
            a = a_all[part]
            wide = spread(d_att[part])
            da = rounded(dot_nt(v[part], wide))
            dv_parts.append(dot(a.astype(BF16), wide).astype(BF16))
            ds = SHARP * a * (da - jnp.sum(da * a, axis=0, keepdims=True))
            q_hi, q_lo = split(spread(q[part]))
            dk_parts.append(three_pass(ds, q_hi, q_lo))
            dq_parts.append(gathered_heads(three_pass_tn(ds, k[part])))
        dv = stack(dv_parts)
        unit = stack([k, q])
        scale = stack([kn_s[rows, :], qn_s[rows, :]])
        d_unit = stack(dk_parts + dq_parts)
        d_raw = scale * (d_unit - unit * head_sums(d_unit * unit, head_ones()))
        dk_raw, dq_raw = d_raw[:ROWS], d_raw[ROWS:]
        c_v = rounded(dot_nt(dv, ws[:, 2 * D :]))
        c_k = rounded(wide_dot_nt(dk_raw, ws[:, D : 2 * D]))
        c_q = rounded(wide_dot_nt(dq_raw, ws[:, :D]))
        dn = rounded(rounded(c_v + c_k) + c_q)
        rows_s[4:5, :] += jnp.sum(dn * xhat, axis=0, keepdims=True)
        y = jnp.where(share == 0, dq_raw, jnp.where(share == 1, dk_raw, dv.astype(F32)))
        hi, lo = split(y)
        y_hi[rows, :] = hi
        y_lo[rows, :] = lo
        z = dn * rows_s[7:8, :]
        dx = inv_s[rows, 0:1] * (z - xhat * jnp.mean(z * xhat, axis=-1, keepdims=True))
        u_s[rows, :] = rounded(d_raw_logit * head[...] + dx)

    for i in range(CLASSES):
        seq_a[pl.ds(i, PATCHES, stride=16), :] = u_s[i * PATCHES : (i + 1) * PATCHES, :128]
        seq_b[pl.ds(i, PATCHES, stride=16), :] = u_s[i * PATCHES : (i + 1) * PATCHES, 128:]

    w_row = rows_s[1:2, :]
    w_hi, w_mid = split(w_row)
    w_lo = (w_row - w_hi.astype(F32) - w_mid.astype(F32)).astype(BF16)
    zero = jnp.zeros((12, D), BF16)
    w_rows = stack([w_hi, w_mid, w_lo, zero, zero[:1]])
    d_head = rows_s[2:3, :] + jnp.sum(dot(w_rows, os[...]), axis=0, keepdims=True)

    @pl.when(jnp.logical_and(scal[1] == 0, share < 3))
    def _():
        x = normed_s[...]
        d_w = dot_tn(x, y_hi[0:ALL, :]) + dot_tn(x, y_lo[0:ALL, :])
        put_tiles(out, d_w)

    @pl.when(jnp.logical_and(scal[1] == 0, share == 3))
    def _():
        d_w = dot_tn(stack([w_hi, w_hi, w_mid, w_mid, zero]), stack([h_hi, h_mid, h_hi, h_mid, zero]))
        put_tiles(out, d_w)

    @pl.loop(0, CHUNKS)
    def _(c):
        rows = chunk_rows(c)
        g = jnp.concatenate([seq_a[rows, :], seq_b[rows, :]], axis=1).astype(BF16)
        d_att = dot_nt(g, ot[...]).astype(BF16)
        v = v_t[rows, :]
        v_class = v_t[ALL:, :]
        k = k_t[rows, :]
        k_class = k_t[ALL:, :]
        q = q_t[...]
        a_dates = ad[rows, :]
        a_class = ac[rows, :]
        da_class, da_dates, dv_class, dv_dates = [], [], [], []
        for s in range(SEQS):
            part = slice(s * 16, s * 16 + 16)
            wide = spread(d_att[part])
            values = stack([v_class, v[part]])
            weights = stack([a_class[part], a_dates[part]]).astype(BF16)
            da = rounded(dot_nt(values, wide))
            dv = dot(weights, wide).astype(BF16)
            da_class.append(da[:16])
            da_dates.append(da[16:])
            dv_class.append(dv[:16])
            dv_dates.append(dv[16:])
        cube = lambda m: m.reshape(SEQS, 16, 128)
        da_c, da_d = stack(da_class), stack(da_dates)
        both = jnp.sum(cube(da_c * a_class), axis=1, keepdims=True) + jnp.sum(
            cube(da_d * a_dates), axis=1, keepdims=True
        )
        ds_c = SHARP * cube(a_class) * (cube(da_c) - both)
        ds_d = SHARP * cube(a_dates) * (cube(da_d) - both)
        q_hi, q_lo = split(spread(q))
        dk = three_pass(stack([ds_d.reshape(ROWS, 128), ds_c.reshape(ROWS, 128)]), q_hi, q_lo)
        dq_parts = []
        for s in range(SEQS):
            ds_s = stack([ds_c[s], ds_d[s]])
            k_all = stack([k_class, k[s * 16 : s * 16 + 16]])
            dq_parts.append(gathered_heads(three_pass_tn(ds_s, k_all)))
        unit = stack([k] + [k_class] * SEQS + [q] * SEQS)
        scale = stack([kn_t[rows, :]] + [kn_t[ALL:, :]] * SEQS + [qn_t[...]] * SEQS)
        d_unit = stack([dk] + dq_parts)
        d_raw = scale * (d_unit - unit * head_sums(d_unit * unit, head_ones()))
        dk_raw, dq_raw = d_raw[: 2 * ROWS], d_raw[2 * ROWS :]
        dv = stack(dv_dates + dv_class)
        c_v = rounded(dot_nt(dv, wt[:, 2 * D :]))
        c_k = rounded(wide_dot_nt(dk_raw, wt[:, D : 2 * D]))
        c_q = rounded(wide_dot_nt(dq_raw, wt[:, :D]))
        dn = rounded(c_v + c_k)
        rows_s[3:4, :] += jnp.sum(dn[:ROWS] * xhat_t[rows, :], axis=0, keepdims=True)
        acc_n[...] += fold(rounded(dn[ROWS:] + c_q))
        acc_g[...] += fold(g.astype(F32))
        acc_q[...] += fold(dq_raw)
        acc_k[...] += fold(dk_raw[ROWS:])
        acc_v[...] += fold(dv[ROWS:].astype(F32))
        of_dates = jnp.where(share == 1, dk_raw[:ROWS], dv[:ROWS].astype(F32))
        y = jnp.where(share == 0, 0.0, jnp.where(share == 3, g.astype(F32), of_dates))
        hi, lo = split(y)

        @pl.when(first)
        def _():
            y_hi[rows, :] = hi
            y_lo[rows, :] = lo

    dn_c = acc_n[...]
    xhat_c = xhat_t[ALL:, :]
    z = dn_c * rows_s[6:7, :]
    d_norm = inv_c[:, 0:1] * (z - xhat_c * jnp.mean(z * xhat_c, axis=-1, keepdims=True))
    d_cls[...] = acc_g[...] + d_norm
    gain_grad_t = rows_s[3:4, :] + jnp.sum(dn_c * xhat_c, axis=0, keepdims=True)
    gain_grad = jnp.where(first, gain_grad_t, rows_s[4:5, :])

    @pl.when(jnp.logical_and(first, share < 3))
    def _():
        y = jnp.where(share == 0, acc_q[...], jnp.where(share == 1, acc_k[...], acc_v[...]))
        hi, lo = split(y)
        y_hi[ALL:, :] = hi
        y_lo[ALL:, :] = lo
        x = normed_t[...]
        d_w = dot_tn(x, y_hi[...]) + dot_tn(x, y_lo[...])
        put_tiles(out, d_w)

    @pl.when(jnp.logical_and(first, share == 3))
    def _():
        put_tiles(out, dot_tn(att_t[...], y_hi[0:ALL, :]))

    misc = jnp.where(share == 0, gain_grad, jnp.where(share == 1, d_head, rows_s[5:6, :]))
    for b in range(SHARE):
        row = d_cls[pl.ds(4 * share + b, 1), :]
        small = stack([row[:, :128], row[:, 128:], misc[:, :128], misc[:, 128:], jnp.zeros((4, 128), F32)])
        for d in range(MEMBERS):
            out[SHARE * d + b, 8:16, :] = small


STEP_SCRATCH = [
    ((D, 3 * D), BF16), ((D, 3 * D), BF16), ((D, D), BF16), ((D, D), BF16),
    ((ALL, 128), F32), ((ALL, 128), F32), ((ALL + 16, D), F32), ((ALL + 16, D), BF16), ((ALL + 16, D), F32), ((ALL + 16, D), F32),
    ((ALL + 16, D), BF16), ((ALL, 128), F32), ((ALL, 128), F32), ((ALL, D), BF16),
    ((16, D), F32), ((16, D), F32), ((16, 128), F32), ((16, 128), F32),
    ((ALL, D), F32), ((ALL, D), F32), ((ALL, D), BF16), ((ALL, 128), F32),
    ((ALL, D), F32), ((ALL, D), F32), ((ALL, D), F32), ((ALL, D), F32), ((ALL, D), BF16),
    ((ALL, HEADS * PATCHES), F32), ((ALL, D), BF16), ((ALL, 128), F32), ((PATCHES, 128), F32), ((8, D), F32),
    ((ALL + 16, D), BF16), ((ALL + 16, D), BF16),
    ((16, D), F32), ((16, D), F32), ((16, D), F32), ((16, D), F32), ((16, D), F32), ((16, D), F32),
]


def reduce_tiles(parts, out):
    out[...] = jnp.broadcast_to(jnp.sum(parts[...], axis=0)[None], (YS, 16, 128))


def assemble(blocks, out):
    whole = stack([blocks[y, 0:8, :] for y in range(YS)] + [blocks[0, 8:16, :]])
    out[...] = jnp.broadcast_to(whole[None], (MEMBERS, CHUNK, 128))


def unpack(core, mine, other, loss, d_class, d_gain, d_qkv, d_out, d_head):
    lower = core[0] == 0
    for b in range(SHARE):
        for part in range(4):
            own, far = mine[SHARE * b + part], other[SHARE * b + part]
            blocks = (jnp.where(lower, own, far), jnp.where(lower, far, own))
            for c in range(2):
                for y in range(YS):
                    n = (2 * y + c) * SHARE + b
                    tile = blocks[c][8 * y : 8 * y + 8]
                    row, lane = 8 * (n // 2), 128 * (n % 2)
                    if part < 3:
                        d_qkv[0, row : row + 8, part * D + lane : part * D + lane + 128] = tile
                    else:
                        d_out[0, row : row + 8, lane : lane + 128] = tile
            at = 4 * part + b
            d_class[at : at + 1, :128] = own[64:65]
            d_class[at : at + 1, 128:] = own[65:66]
            if b == 0 and part < 3:
                ref = (d_gain, d_head, loss)[part]
                ref[:, :128] = own[66:67]
                ref[:, 128:] = own[67:68]


VM = pl.BlockSpec()
SM = pl.BlockSpec(memory_space=pltpu.SMEM)


def call(body, in_specs, outs, *args, scratch=()):
    return pl.pallas_call(
        body,
        out_shape=[jax.ShapeDtypeStruct(s, t) for s, t in outs],
        in_specs=in_specs,
        out_specs=[VM] * len(outs),
        scratch_shapes=[pltpu.VMEM(s, t) for s, t in scratch],
        compiler_params=pltpu.CompilerParams(vmem_limit_bytes=48 * 1024 * 1024),
    )(*args)


def encodings(date_days):
    band = jnp.arange(D)
    frequency = jnp.exp((band // 2 * 2).astype(F32) * (-math.log(10000.0) / D))
    phases = date_days.astype(F32)[:, :, None] * frequency
    return jnp.where(band % 2 == 0, jnp.sin(phases), jnp.cos(phases)).reshape(TILES_DEV * 16, D)


def swap(v):
    return lax.ppermute(v, "pipe", [(0, 1), (1, 0)])


def whole_step(
    pixels,
    date_days,
    clear_count,
    batch_slot,
    labels,
    class_tokens,
    section_gain,
    wqkv,
    wout,
    head_vec,
):
    first = (lax.axis_index("pipe") == 0).astype(I32)
    inner = lax.axis_index(INNER).astype(I32)
    by_dest = jnp.repeat(pixels.reshape(TILES_DEV, PATCHES, D), SHARE, axis=0)
    whole_tile = lax.all_to_all(by_dest, INNER, 0, 0, tiled=True)
    (grads,) = call(
        step,
        [SM] * 3 + [VM] * 11,
        [((OWNERS, 16, 128), F32)],
        jnp.stack([inner, first]),
        clear_count,
        batch_slot,
        labels,
        whole_tile,
        encodings(date_days),
        class_tokens,
        section_gain,
        swap(section_gain),
        wqkv,
        swap(wqkv),
        wout,
        swap(wout),
        head_vec.reshape(1, D),
        scratch=STEP_SCRATCH,
    )
    parts = lax.all_to_all(grads, DP + ("b",), 0, 0, tiled=True)
    (total,) = call(reduce_tiles, [VM], [((YS, 16, 128), F32)], parts)
    blocks = lax.all_to_all(total, "y", 0, 0, tiled=True)
    (whole,) = call(assemble, [VM], [((MEMBERS, CHUNK, 128), F32)], blocks)
    mine = lax.all_to_all(whole, INNER, 0, 0, tiled=True)
    other = lax.ppermute(mine, "core", [(0, 1), (1, 0)])
    loss, d_class, d_gain, d_qkv, d_out, d_head = call(
        unpack,
        [SM, VM, VM],
        [
            ((1, D), F32),
            ((16, D), F32),
            ((1, D), F32),
            ((1, D, 3 * D), F32),
            ((1, D, D), F32),
            ((1, D), F32),
        ],
        lax.axis_index("core").astype(I32)[None],
        mine,
        other,
    )
    return (loss[0, :MICRO], d_class, d_gain, d_qkv, d_out, d_head.reshape(D))


def solution(mesh):
    cut = Mesh(mesh.devices.reshape(2, YS, 2, TILES_DEV, SHARE), ("pipe",) + DP + INNER)
    placed = (
        P(DP, INNER, None, None),
        P(DP, None),
        P(DP),
        P(DP),
        P(DP, None),
        P(),
        P("pipe", None),
        P("pipe", None, None),
        P("pipe", None, None),
        P(),
    )
    return jax.shard_map(
        whole_step,
        mesh=cut,
        in_specs=placed,
        out_specs=(P(), P(), P("pipe", None), P("pipe", None, None), P("pipe", None, None), P()),
        check_vma=False,
    )
```

```python
import math

import jax
import jax.numpy as jnp
from jax import lax
from jax.experimental import pallas as pl
from jax.experimental.pallas import tpu as pltpu
from jax.sharding import Mesh, PartitionSpec as P


D = 256
HEADS = 8
CLASSES = 16
PATCHES = 48
MICRO = 4
SHARP = 10.0
CAP = 15.0
NORM_EPS = 1e-05
HEAD_EPS = 1e-06
F32 = jnp.float32
BF16 = jnp.bfloat16
I32 = jnp.int32

TILES_DEV = 4
DATES = 16
CHUNKS = 4
SEQS = PATCHES // CHUNKS
CLASS_CHUNK = CLASSES // CHUNKS
ROWS = SEQS * 16
ALL = CHUNKS * ROWS
MEMBERS = 16
SHARE = 4
YS = 8
OWNERS = 32
CHUNK = 72
DP = ("y", "core")
INNER = ("r", "b")


def dot(a, b):
    return lax.dot_general(a, b, (((1,), (0,)), ((), ())), preferred_element_type=F32)


def dot_nt(a, b):
    return lax.dot_general(a, b, (((1,), (1,)), ((), ())), preferred_element_type=F32)


def dot_tn(a, b):
    return lax.dot_general(a, b, (((0,), (0,)), ((), ())), preferred_element_type=F32)


def split(x):
    hi = x.astype(BF16)
    return hi, (x - hi.astype(F32)).astype(BF16)


def rounded(x):
    return x.astype(BF16).astype(F32)


def iota(shape, axis):
    return lax.broadcasted_iota(I32, shape, axis)


def head_ones():
    same = (iota((D, D), 0) >> 5) == (iota((D, D), 1) >> 5)
    return jnp.where(same, 1.0, 0.0).astype(BF16)


def head_sums(x, ones):
    hi, lo = split(x)
    return dot(hi, ones) + dot(lo, ones)


def spread(rows_of, masks):
    n = rows_of.shape[0]
    return jnp.concatenate([rows_of * masks[h, 0:n, :] for h in range(HEADS)], axis=0)


def spread_pair(rows_of, masks):
    hi, lo = split(rows_of)
    return spread(hi, masks), spread(lo, masks)


def gathered_heads(wide):
    n = wide.shape[0] // HEADS
    lane_head = iota((n, D), 1) >> 5
    out = wide[:n]
    for h in range(1, HEADS):
        out = jnp.where(lane_head == h, wide[h * n : (h + 1) * n], out)
    return out


def logits_t(k, q, masks):
    n = k.shape[0]
    k_hi, k_lo = split(k)
    q_hi, q_lo = spread_pair(q, masks)
    both = dot_nt(jnp.concatenate([k_hi, k_lo], axis=0), q_hi)
    return SHARP * (both[:n] + both[n:] + dot_nt(k_hi, q_lo))


def three_pass(x, w_hi, w_lo):
    n = x.shape[0]
    x_hi, x_lo = split(x)
    both = dot(jnp.concatenate([x_hi, x_lo], axis=0), w_hi)
    return both[:n] + both[n:] + dot(x_hi, w_lo)


def three_pass_tn(x, y):
    x_hi, x_lo = split(x)
    y_hi, y_lo = split(y)
    return dot_tn(
        jnp.concatenate([x_hi, x_hi, x_lo], axis=0), jnp.concatenate([y_hi, y_lo, y_hi], axis=0)
    )


def wide_dot_nt(x, w):
    n = x.shape[0]
    hi, lo = split(x)
    both = dot_nt(jnp.concatenate([hi, lo], axis=0), w)
    return both[:n] + both[n:]


def stack(parts):
    return jnp.concatenate(parts, axis=0)


def fold(rows):
    return jnp.sum(rows.reshape(-1, 16, D), axis=0)


def chunk_rows(c):
    return pl.ds(pl.multiple_of(c * ROWS, ROWS), ROWS)


def tile_at(y, c, b):
    n = (2 * y + c) * TILES_DEV + b
    return 8 * (n // 2), 128 * (n % 2)


def put_tiles(keep, give, lower, d_w):
    for y in range(YS):
        for b in range(TILES_DEV):
            pair = []
            for c in range(2):
                row, lane = tile_at(y, c, b)
                pair.append(d_w[row : row + 8, lane : lane + 128])
            keep[TILES_DEV * y + b, 0:8, :] = jnp.where(lower, pair[0], pair[1])
            give[TILES_DEV * y + b, 0:8, :] = jnp.where(lower, pair[1], pair[0])


def step(
    scal, counts, slots, labels, pix, enc, cls, gain_a, gain_b, wqkv_a, wqkv_b, wout_a, wout_b, head, keep, give, *scratch
):
    (wt, ws, ot, os, seq_a, seq_b, xhat_t, normed_t, k_t, kn_t, v_t, ad, ac, att_t, q_t, qn_t, e_cls, inv_c,
     u_s, xhat_s, normed_s, inv_s, k_s, kn_s, q_s, qn_s, v_s, a_s, att_s, log_s, tot, rows_s, y_hi, y_lo,
     acc_q, acc_k, acc_v, acc_n, acc_g, d_cls, masks) = scratch
    first = scal[1] == 1
    tile = scal[0] & 3
    share = scal[0] >> 2
    lower = scal[2] == 0
    ones = head_ones()
    lane_head = iota((PATCHES, D), 1) >> 5
    for h in range(HEADS):
        masks[h] = jnp.where(lane_head == h, 1.0, 0.0).astype(BF16)
    wt[...] = jnp.where(first, wqkv_a[0], wqkv_b[0])
    ws[...] = jnp.where(first, wqkv_b[0], wqkv_a[0])
    ot[...] = jnp.where(first, wout_a[0], wout_b[0])
    os[...] = jnp.where(first, wout_b[0], wout_a[0])
    gain_t = jnp.where(first, gain_a[...], gain_b[...])
    gain_s = jnp.where(first, gain_b[...], gain_a[...])
    head_row = head[...]
    h_hi, h_mid = split(head_row)
    h_lo = (head_row - h_hi.astype(F32) - h_mid.astype(F32)).astype(BF16)
    h_rows = stack([h_hi, h_mid, h_lo, jnp.zeros((13, D), BF16)])
    rows_s[...] = jnp.zeros((8, D), F32)
    rows_s[0:1, :] = jnp.sum(dot_nt(h_rows, os[...]), axis=0, keepdims=True)
    rows_s[6:7, :] = gain_t
    rows_s[7:8, :] = gain_s
    for ref in (acc_q, acc_k, acc_v, acc_n, acc_g):
        ref[...] = jnp.zeros((16, D), F32)

    xc = cls[...].astype(F32)
    inv = lax.rsqrt(jnp.mean(xc * xc, axis=-1, keepdims=True) + NORM_EPS)
    xhat_c = xc * inv
    normed_c = (xhat_c * gain_t).astype(BF16)
    qkv_c = dot(normed_c, wt[...])
    kq = stack([qkv_c[:, D : 2 * D], qkv_c[:, :D]])
    kq_inv = lax.rsqrt(head_sums(kq * kq, ones) + HEAD_EPS)
    kq_unit = kq * kq_inv
    xhat_t[ALL:, :] = xhat_c
    normed_t[ALL:, :] = normed_c
    inv_c[...] = jnp.broadcast_to(inv, (16, 128))
    k_t[ALL:, :] = kq_unit[:16]
    kn_t[ALL:, :] = kq_inv[:16]
    q_t[...] = kq_unit[16:]
    qn_t[...] = kq_inv[16:]
    v_t[ALL:, :] = qkv_c[:, 2 * D :].astype(BF16)
    e_cls[...] = jnp.exp(logits_t(kq_unit[:16], kq_unit[16:], masks))

    @pl.loop(0, CHUNKS)
    def _(c):
        rows = chunk_rows(c)
        tile_enc = enc[pl.ds(pl.multiple_of(tile * 16, 16), 16), :]
        pixel = pix[pl.ds(c * 4, 4), :, :].astype(F32).reshape(SEQS, 16, D)
        x = (pixel + tile_enc[None]).reshape(ROWS, D)
        inv = lax.rsqrt(jnp.mean(x * x, axis=-1, keepdims=True) + NORM_EPS)
        xhat = x * inv
        normed = (xhat * rows_s[6:7, :]).astype(BF16)
        xhat_t[rows, :] = xhat
        normed_t[rows, :] = normed
        kv = dot(normed, wt[:, D:])
        v = kv[:, D:].astype(BF16)
        v_t[rows, :] = v
        k = kv[:, :D]
        k_inv = lax.rsqrt(head_sums(k * k, head_ones()) + HEAD_EPS)
        k = k * k_inv
        k_t[rows, :] = k
        kn_t[rows, :] = k_inv
        raised = jnp.exp(logits_t(k, q_t[...], masks))
        shown = (iota((ROWS, 128), 0) & 15) < counts[tile]
        e_dates = jnp.where(shown, raised, 0.0).reshape(SEQS, DATES, 128)
        e_class = e_cls[...]
        total = jnp.sum(e_dates, axis=1, keepdims=True) + jnp.sum(e_class, axis=0, keepdims=True)[None]
        a_dates = e_dates / total
        a_class = e_class[None] / total
        ad[rows, :] = a_dates.reshape(ROWS, 128)
        ac[rows, :] = a_class.reshape(ROWS, 128)
        v_class = v_t[ALL:, :]
        parts = []
        for s in range(SEQS):
            weights = stack([a_class[s], a_dates[s]]).astype(BF16)
            values = stack([v_class, v[s * 16 : s * 16 + 16]])
            parts.append(gathered_heads(dot_tn(weights, values)))
        att = stack(parts).astype(BF16)
        att_t[rows, :] = att
        updated = rounded(stack([cls[...].astype(F32)] * SEQS) + dot(att, ot[...]))
        seq_a[rows, :] = updated[:, :128]
        seq_b[rows, :] = updated[:, 128:]

    for i in range(CLASSES):
        u_s[i * PATCHES : (i + 1) * PATCHES, :128] = seq_a[pl.ds(i, PATCHES, stride=16), :]
        u_s[i * PATCHES : (i + 1) * PATCHES, 128:] = seq_b[pl.ds(i, PATCHES, stride=16), :]

    @pl.loop(0, CHUNKS)
    def _(c):
        rows = chunk_rows(c)
        u = u_s[rows, :]
        inv = lax.rsqrt(jnp.mean(u * u, axis=-1, keepdims=True) + NORM_EPS)
        xhat = u * inv
        normed = (xhat * rows_s[7:8, :]).astype(BF16)
        xhat_s[rows, :] = xhat
        normed_s[rows, :] = normed
        inv_s[rows, :] = jnp.broadcast_to(inv, (ROWS, 128))
        qkv = dot(normed, ws[...])
        v = qkv[:, 2 * D :].astype(BF16)
        kq = stack([qkv[:, D : 2 * D], qkv[:, :D]])
        kq_inv = lax.rsqrt(head_sums(kq * kq, head_ones()) + HEAD_EPS)
        kq_unit = kq * kq_inv
        k, q = kq_unit[:ROWS], kq_unit[ROWS:]
        k_s[rows, :] = k
        q_s[rows, :] = q
        kn_s[rows, :] = kq_inv[:ROWS]
        qn_s[rows, :] = kq_inv[ROWS:]
        v_s[rows, :] = v
        parts, held = [], []
        for b in range(CLASS_CHUNK):
            part = slice(b * PATCHES, b * PATCHES + PATCHES)
            raised = jnp.exp(logits_t(k[part], q[part], masks))
            a = raised / jnp.sum(raised, axis=0, keepdims=True)
            held.append(a)
            parts.append(gathered_heads(dot_tn(a.astype(BF16), v[part])))
        a_s[rows, :] = stack(held)
        att = stack(parts).astype(BF16)
        att_s[rows, :] = att
        raw = jnp.sum(u * head[...] + att.astype(F32) * rows_s[0:1, :], axis=-1, keepdims=True)
        log_s[rows, :] = jnp.broadcast_to(CAP * jnp.tanh(raw / CAP), (ROWS, 128))

    tot[...] = jnp.sum(jnp.exp(log_s[...]).reshape(CLASSES, PATCHES, 128), axis=0)

    @pl.loop(0, CHUNKS)
    def _(c):
        rows = chunk_rows(c)
        u = u_s[rows, :]
        xhat = xhat_s[rows, :]
        attf = att_s[rows, :].astype(F32)
        logit = log_s[rows, 0:1]
        total = stack([tot[:, 0:1]] * CLASS_CHUNK)
        eye = iota((PATCHES, PATCHES), 0) == iota((PATCHES, PATCHES), 1)
        label_row = labels[pl.ds(tile, 1), :].astype(F32)
        label = jnp.sum(jnp.where(eye, label_row, 0.0), axis=-1, keepdims=True)
        base = (c * CLASS_CHUNK).astype(F32)
        mine = stack([jnp.where(label == base + b, 1.0, 0.0) for b in range(CLASS_CHUNK)])
        d_logit = (jnp.exp(logit) / total - mine) * (1.0 / 64.0)
        ratio = logit / CAP
        d_raw_logit = d_logit * (1.0 - ratio * ratio)
        ce = jnp.sum(mine * (jnp.log(total) - logit), axis=0, keepdims=True) * (1.0 / 768.0)
        rows_s[5:6, :] += jnp.where(iota((1, D), 1) == slots[tile], ce, 0.0)
        rows_s[1:2, :] += jnp.sum(attf * d_raw_logit, axis=0, keepdims=True)
        rows_s[2:3, :] += jnp.sum(u * d_raw_logit, axis=0, keepdims=True)
        d_att = (d_raw_logit * rows_s[0:1, :]).astype(BF16)
        v = v_s[rows, :]
        k = k_s[rows, :]
        q = q_s[rows, :]
        a_all = a_s[rows, :]
        dv_parts, dk_parts, dq_parts = [], [], []
        for b in range(CLASS_CHUNK):
            part = slice(b * PATCHES, b * PATCHES + PATCHES)
            a = a_all[part]
            wide = spread(d_att[part], masks)
            da = rounded(dot_nt(v[part], wide))
            dv_parts.append(dot(a.astype(BF16), wide).astype(BF16))
            ds = SHARP * a * (da - jnp.sum(da * a, axis=0, keepdims=True))
            q_hi, q_lo = spread_pair(q[part], masks)
            dk_parts.append(three_pass(ds, q_hi, q_lo))
            dq_parts.append(gathered_heads(three_pass_tn(ds, k[part])))
        dv = stack(dv_parts)
        unit = stack([k, q])
        scale = stack([kn_s[rows, :], qn_s[rows, :]])
        d_unit = stack(dk_parts + dq_parts)
        d_raw = scale * (d_unit - unit * head_sums(d_unit * unit, head_ones()))
        dk_raw, dq_raw = d_raw[:ROWS], d_raw[ROWS:]
        c_v = rounded(dot_nt(dv, ws[:, 2 * D :]))
        c_k = rounded(wide_dot_nt(dk_raw, ws[:, D : 2 * D]))
        c_q = rounded(wide_dot_nt(dq_raw, ws[:, :D]))
        dn = rounded(rounded(c_v + c_k) + c_q)
        rows_s[4:5, :] += jnp.sum(dn * xhat, axis=0, keepdims=True)
        y = jnp.where(share == 0, dq_raw, jnp.where(share == 1, dk_raw, dv.astype(F32)))
        hi, lo = split(y)
        y_hi[rows, :] = hi
        y_lo[rows, :] = lo
        z = dn * rows_s[7:8, :]
        dx = inv_s[rows, 0:1] * (z - xhat * jnp.mean(z * xhat, axis=-1, keepdims=True))
        u_s[rows, :] = rounded(d_raw_logit * head[...] + dx)

    for i in range(CLASSES):
        seq_a[pl.ds(i, PATCHES, stride=16), :] = u_s[i * PATCHES : (i + 1) * PATCHES, :128]
        seq_b[pl.ds(i, PATCHES, stride=16), :] = u_s[i * PATCHES : (i + 1) * PATCHES, 128:]

    w_row = rows_s[1:2, :]
    w_hi, w_mid = split(w_row)
    w_lo = (w_row - w_hi.astype(F32) - w_mid.astype(F32)).astype(BF16)
    zero = jnp.zeros((12, D), BF16)
    w_rows = stack([w_hi, w_mid, w_lo, zero, zero[:1]])
    d_head = rows_s[2:3, :] + jnp.sum(dot(w_rows, os[...]), axis=0, keepdims=True)

    @pl.when(jnp.logical_and(scal[1] == 0, share < 3))
    def _():
        x = normed_s[...]
        d_w = dot_tn(x, y_hi[0:ALL, :]) + dot_tn(x, y_lo[0:ALL, :])
        put_tiles(keep, give, lower, d_w)

    @pl.when(jnp.logical_and(scal[1] == 0, share == 3))
    def _():
        d_w = dot_tn(stack([w_hi, w_hi, w_mid, w_mid, zero]), stack([h_hi, h_mid, h_hi, h_mid, zero]))
        put_tiles(keep, give, lower, d_w)

    @pl.loop(0, CHUNKS)
    def _(c):
        rows = chunk_rows(c)
        g = jnp.concatenate([seq_a[rows, :], seq_b[rows, :]], axis=1).astype(BF16)
        d_att = dot_nt(g, ot[...]).astype(BF16)
        v = v_t[rows, :]
        v_class = v_t[ALL:, :]
        k = k_t[rows, :]
        k_class = k_t[ALL:, :]
        q = q_t[...]
        a_dates = ad[rows, :]
        a_class = ac[rows, :]
        da_class, da_dates, dv_class, dv_dates = [], [], [], []
        for s in range(SEQS):
            part = slice(s * 16, s * 16 + 16)
            wide = spread(d_att[part], masks)
            values = stack([v_class, v[part]])
            weights = stack([a_class[part], a_dates[part]]).astype(BF16)
            da = rounded(dot_nt(values, wide))
            dv = dot(weights, wide).astype(BF16)
            da_class.append(da[:16])
            da_dates.append(da[16:])
            dv_class.append(dv[:16])
            dv_dates.append(dv[16:])
        cube = lambda m: m.reshape(SEQS, 16, 128)
        da_c, da_d = stack(da_class), stack(da_dates)
        both = jnp.sum(cube(da_c * a_class), axis=1, keepdims=True) + jnp.sum(
            cube(da_d * a_dates), axis=1, keepdims=True
        )
        ds_c = SHARP * cube(a_class) * (cube(da_c) - both)
        ds_d = SHARP * cube(a_dates) * (cube(da_d) - both)
        q_hi, q_lo = spread_pair(q, masks)
        dk = three_pass(stack([ds_d.reshape(ROWS, 128), ds_c.reshape(ROWS, 128)]), q_hi, q_lo)
        dq_parts = []
        for s in range(SEQS):
            ds_s = stack([ds_c[s], ds_d[s]])
            k_all = stack([k_class, k[s * 16 : s * 16 + 16]])
            dq_parts.append(gathered_heads(three_pass_tn(ds_s, k_all)))
        unit = stack([k] + [k_class] * SEQS + [q] * SEQS)
        scale = stack([kn_t[rows, :]] + [kn_t[ALL:, :]] * SEQS + [qn_t[...]] * SEQS)
        d_unit = stack([dk] + dq_parts)
        d_raw = scale * (d_unit - unit * head_sums(d_unit * unit, head_ones()))
        dk_raw, dq_raw = d_raw[: 2 * ROWS], d_raw[2 * ROWS :]
        dv = stack(dv_dates + dv_class)
        c_v = rounded(dot_nt(dv, wt[:, 2 * D :]))
        c_k = rounded(wide_dot_nt(dk_raw, wt[:, D : 2 * D]))
        c_q = rounded(wide_dot_nt(dq_raw, wt[:, :D]))
        dn = rounded(c_v + c_k)
        rows_s[3:4, :] += jnp.sum(dn[:ROWS] * xhat_t[rows, :], axis=0, keepdims=True)
        acc_n[...] += fold(rounded(dn[ROWS:] + c_q))
        acc_g[...] += fold(g.astype(F32))
        acc_q[...] += fold(dq_raw)
        acc_k[...] += fold(dk_raw[ROWS:])
        acc_v[...] += fold(dv[ROWS:].astype(F32))
        of_dates = jnp.where(share == 1, dk_raw[:ROWS], dv[:ROWS].astype(F32))
        y = jnp.where(share == 0, 0.0, jnp.where(share == 3, g.astype(F32), of_dates))
        hi, lo = split(y)

        @pl.when(first)
        def _():
            y_hi[rows, :] = hi
            y_lo[rows, :] = lo

    dn_c = acc_n[...]
    xhat_c = xhat_t[ALL:, :]
    z = dn_c * rows_s[6:7, :]
    d_norm = inv_c[:, 0:1] * (z - xhat_c * jnp.mean(z * xhat_c, axis=-1, keepdims=True))
    d_cls[...] = acc_g[...] + d_norm
    gain_grad_t = rows_s[3:4, :] + jnp.sum(dn_c * xhat_c, axis=0, keepdims=True)
    gain_grad = jnp.where(first, gain_grad_t, rows_s[4:5, :])

    @pl.when(jnp.logical_and(first, share < 3))
    def _():
        y = jnp.where(share == 0, acc_q[...], jnp.where(share == 1, acc_k[...], acc_v[...]))
        hi, lo = split(y)
        y_hi[ALL:, :] = hi
        y_lo[ALL:, :] = lo
        x = normed_t[...]
        d_w = dot_tn(x, y_hi[...]) + dot_tn(x, y_lo[...])
        put_tiles(keep, give, lower, d_w)

    @pl.when(jnp.logical_and(first, share == 3))
    def _():
        put_tiles(keep, give, lower, dot_tn(att_t[...], y_hi[0:ALL, :]))

    misc = jnp.where(share == 0, gain_grad, jnp.where(share == 1, d_head, rows_s[5:6, :]))
    for b in range(SHARE):
        row = d_cls[pl.ds(4 * share + b, 1), :]
        small = stack([row[:, :128], row[:, 128:], misc[:, :128], misc[:, 128:], jnp.zeros((4, 128), F32)])
        for y in range(YS):
            keep[TILES_DEV * y + b, 8:16, :] = small
            give[TILES_DEV * y + b, 8:16, :] = small


STEP_SCRATCH = [
    ((D, 3 * D), BF16), ((D, 3 * D), BF16), ((D, D), BF16), ((D, D), BF16),
    ((ALL, 128), F32), ((ALL, 128), F32), ((ALL + 16, D), F32), ((ALL + 16, D), BF16), ((ALL + 16, D), F32), ((ALL + 16, D), F32),
    ((ALL + 16, D), BF16), ((ALL, 128), F32), ((ALL, 128), F32), ((ALL, D), BF16),
    ((16, D), F32), ((16, D), F32), ((16, 128), F32), ((16, 128), F32),
    ((ALL, D), F32), ((ALL, D), F32), ((ALL, D), BF16), ((ALL, 128), F32),
    ((ALL, D), F32), ((ALL, D), F32), ((ALL, D), F32), ((ALL, D), F32), ((ALL, D), BF16),
    ((ALL, HEADS * PATCHES), F32), ((ALL, D), BF16), ((ALL, 128), F32), ((PATCHES, 128), F32), ((8, D), F32),
    ((ALL + 16, D), BF16), ((ALL + 16, D), BF16),
    ((16, D), F32), ((16, D), F32), ((16, D), F32), ((16, D), F32), ((16, D), F32), ((16, D), F32),
    ((HEADS, PATCHES, D), BF16),
]


def reduce_tiles(parts, out):
    out[...] = jnp.broadcast_to(jnp.sum(parts[...], axis=0)[None], (YS, 16, 128))


def assemble(blocks, out):
    whole = stack([blocks[y, 0:8, :] for y in range(YS)] + [blocks[0, 8:16, :]])
    out[...] = jnp.broadcast_to(whole[None], (MEMBERS, CHUNK, 128))


def unpack(core, mine, other, loss, d_class, d_gain, d_qkv, d_out, d_head):
    lower = core[0] == 0
    for b in range(SHARE):
        for part in range(4):
            own, far = mine[SHARE * part + b], other[SHARE * part + b]
            blocks = (jnp.where(lower, own, far), jnp.where(lower, far, own))
            for c in range(2):
                for y in range(YS):
                    tile = blocks[c][8 * y : 8 * y + 8]
                    row, lane = tile_at(y, c, b)
                    if part < 3:
                        d_qkv[0, row : row + 8, part * D + lane : part * D + lane + 128] = tile
                    else:
                        d_out[0, row : row + 8, lane : lane + 128] = tile
            at = 4 * part + b
            d_class[at : at + 1, :128] = own[64:65]
            d_class[at : at + 1, 128:] = own[65:66]
            if b == 0 and part < 3:
                ref = (d_gain, d_head, loss)[part]
                ref[:, :128] = own[66:67]
                ref[:, 128:] = own[67:68]


VM = pl.BlockSpec()
SM = pl.BlockSpec(memory_space=pltpu.SMEM)


def call(body, in_specs, outs, *args, scratch=()):
    return pl.pallas_call(
        body,
        out_shape=[jax.ShapeDtypeStruct(s, t) for s, t in outs],
        in_specs=in_specs,
        out_specs=[VM] * len(outs),
        scratch_shapes=[pltpu.VMEM(s, t) for s, t in scratch],
        compiler_params=pltpu.CompilerParams(vmem_limit_bytes=48 * 1024 * 1024),
    )(*args)


def encodings(date_days):
    band = jnp.arange(D)
    frequency = jnp.exp((band // 2 * 2).astype(F32) * (-math.log(10000.0) / D))
    phases = date_days.astype(F32)[:, :, None] * frequency
    return jnp.where(band % 2 == 0, jnp.sin(phases), jnp.cos(phases)).reshape(TILES_DEV * 16, D)


def swap(v):
    return lax.ppermute(v, "pipe", [(0, 1), (1, 0)])


def whole_step(
    pixels,
    date_days,
    clear_count,
    batch_slot,
    labels,
    class_tokens,
    section_gain,
    wqkv,
    wout,
    head_vec,
):
    first = (lax.axis_index("pipe") == 0).astype(I32)
    inner = lax.axis_index(INNER).astype(I32)
    by_dest = jnp.tile(pixels.reshape(TILES_DEV, PATCHES, D), (SHARE, 1, 1))
    whole_tile = lax.all_to_all(by_dest, INNER, 0, 0, tiled=True)
    core = lax.axis_index("core").astype(I32)
    keep, give = call(
        step,
        [SM] * 3 + [VM] * 11,
        [((OWNERS, 16, 128), F32)] * 2,
        jnp.stack([inner, first, core]),
        clear_count,
        batch_slot,
        labels,
        whole_tile,
        encodings(date_days),
        class_tokens,
        section_gain,
        swap(section_gain),
        wqkv,
        swap(wqkv),
        wout,
        swap(wout),
        head_vec.reshape(1, D),
        scratch=STEP_SCRATCH,
    )
    given = lax.ppermute(give, "core", [(0, 1), (1, 0)])
    parts = lax.all_to_all(keep + given, ("y", "b"), 0, 0, tiled=True)
    (total,) = call(reduce_tiles, [VM], [((YS, 16, 128), F32)], parts)
    blocks = lax.all_to_all(total, "y", 0, 0, tiled=True)
    (whole,) = call(assemble, [VM], [((MEMBERS, CHUNK, 128), F32)], blocks)
    mine = lax.all_to_all(whole, INNER, 0, 0, tiled=True)
    other = lax.ppermute(mine, "core", [(0, 1), (1, 0)])
    loss, d_class, d_gain, d_qkv, d_out, d_head = call(
        unpack,
        [SM, VM, VM],
        [
            ((1, D), F32),
            ((16, D), F32),
            ((1, D), F32),
            ((1, D, 3 * D), F32),
            ((1, D, D), F32),
            ((1, D), F32),
        ],
        core[None],
        mine,
        other,
    )
    return (loss[0, :MICRO], d_class, d_gain, d_qkv, d_out, d_head.reshape(D))


def solution(mesh):
    cut = Mesh(mesh.devices.reshape(2, YS, 2, TILES_DEV, SHARE), ("pipe",) + DP + INNER)
    placed = (
        P(DP, INNER, None, None),
        P(DP, None),
        P(DP),
        P(DP),
        P(DP, None),
        P(),
        P("pipe", None),
        P("pipe", None, None),
        P("pipe", None, None),
        P(),
    )
    return jax.shard_map(
        whole_step,
        mesh=cut,
        in_specs=placed,
        out_specs=(P(), P(), P("pipe", None), P("pipe", None, None), P("pipe", None, None), P()),
        check_vma=False,
    )
```

```python
import math

import jax
import jax.numpy as jnp
from jax import lax
from jax.experimental import pallas as pl
from jax.experimental.pallas import tpu as pltpu
from jax.sharding import Mesh, PartitionSpec as P


D = 256
HEADS = 8
CLASSES = 16
PATCHES = 48
MICRO = 4
SHARP = 10.0
CAP = 15.0
NORM_EPS = 1e-05
HEAD_EPS = 1e-06
F32 = jnp.float32
BF16 = jnp.bfloat16
I32 = jnp.int32

TILES_DEV = 4
DATES = 16
CHUNKS = 4
SEQS = PATCHES // CHUNKS
CLASS_CHUNK = CLASSES // CHUNKS
ROWS = SEQS * 16
ALL = CHUNKS * ROWS
MEMBERS = 16
SHARE = 4
YS = 8
OWNERS = 32
CODE_TOP = 32000.0
CHUNK = 72
DP = ("y", "core")
INNER = ("r", "b")


def dot(a, b):
    return lax.dot_general(a, b, (((1,), (0,)), ((), ())), preferred_element_type=F32)


def dot_nt(a, b):
    return lax.dot_general(a, b, (((1,), (1,)), ((), ())), preferred_element_type=F32)


def dot_tn(a, b):
    return lax.dot_general(a, b, (((0,), (0,)), ((), ())), preferred_element_type=F32)


def split(x):
    hi = x.astype(BF16)
    return hi, (x - hi.astype(F32)).astype(BF16)


def rounded(x):
    return x.astype(BF16).astype(F32)


def iota(shape, axis):
    return lax.broadcasted_iota(I32, shape, axis)


def head_ones():
    same = (iota((D, D), 0) >> 5) == (iota((D, D), 1) >> 5)
    return jnp.where(same, 1.0, 0.0).astype(BF16)


def head_sums(x, ones):
    hi, lo = split(x)
    return dot(hi, ones) + dot(lo, ones)


def spread(rows_of, masks):
    n = rows_of.shape[0]
    return jnp.concatenate([rows_of * masks[h, 0:n, :] for h in range(HEADS)], axis=0)


def spread_pair(rows_of, masks):
    hi, lo = split(rows_of)
    return spread(hi, masks), spread(lo, masks)


def gathered_heads(wide):
    n = wide.shape[0] // HEADS
    lane_head = iota((n, D), 1) >> 5
    out = wide[:n]
    for h in range(1, HEADS):
        out = jnp.where(lane_head == h, wide[h * n : (h + 1) * n], out)
    return out


def logits_t(k, q, masks):
    n = k.shape[0]
    k_hi, k_lo = split(k)
    q_hi, q_lo = spread_pair(q, masks)
    both = dot_nt(jnp.concatenate([k_hi, k_lo], axis=0), q_hi)
    return SHARP * (both[:n] + both[n:] + dot_nt(k_hi, q_lo))


def three_pass(x, w_hi, w_lo):
    n = x.shape[0]
    x_hi, x_lo = split(x)
    both = dot(jnp.concatenate([x_hi, x_lo], axis=0), w_hi)
    return both[:n] + both[n:] + dot(x_hi, w_lo)


def three_pass_tn(x, y):
    x_hi, x_lo = split(x)
    y_hi, y_lo = split(y)
    return dot_tn(
        jnp.concatenate([x_hi, x_hi, x_lo], axis=0), jnp.concatenate([y_hi, y_lo, y_hi], axis=0)
    )


def wide_dot_nt(x, w):
    n = x.shape[0]
    hi, lo = split(x)
    both = dot_nt(jnp.concatenate([hi, lo], axis=0), w)
    return both[:n] + both[n:]


def stack(parts):
    return jnp.concatenate(parts, axis=0)


def fold(rows):
    return jnp.sum(rows.reshape(-1, 16, D), axis=0)


def chunk_rows(c):
    return pl.ds(pl.multiple_of(c * ROWS, ROWS), ROWS)


def tile_at(y, c, b):
    n = (2 * y + c) * TILES_DEV + b
    return 8 * (n // 2), 128 * (n % 2)


def put_tiles(keep, give, lower, d_w):
    for y in range(YS):
        for b in range(TILES_DEV):
            pair = []
            for c in range(2):
                row, lane = tile_at(y, c, b)
                pair.append(d_w[row : row + 8, lane : lane + 128])
            keep[TILES_DEV * y + b, 0:8, :] = jnp.where(lower, pair[0], pair[1])
            give[TILES_DEV * y + b, 0:8, :] = jnp.where(lower, pair[1], pair[0])


def step(
    scal, counts, slots, labels, pix, enc, cls, gain_a, gain_b, wqkv_a, wqkv_b, wout_a, wout_b, head, keep, give, *scratch
):
    (wt, ws, ot, os, seq_a, seq_b, xhat_t, normed_t, k_t, kn_t, v_t, ad, ac, att_t, q_t, qn_t, e_cls, inv_c,
     u_s, xhat_s, normed_s, inv_s, k_s, kn_s, q_s, qn_s, v_s, a_s, att_s, log_s, tot, rows_s, y_hi, y_lo,
     acc_q, acc_k, acc_v, acc_n, acc_g, d_cls, masks) = scratch
    first = scal[1] == 1
    tile = scal[0] & 3
    share = scal[0] >> 2
    lower = scal[2] == 0
    ones = head_ones()
    lane_head = iota((PATCHES, D), 1) >> 5
    for h in range(HEADS):
        masks[h] = jnp.where(lane_head == h, 1.0, 0.0).astype(BF16)
    wt[...] = jnp.where(first, wqkv_a[0], wqkv_b[0])
    ws[...] = jnp.where(first, wqkv_b[0], wqkv_a[0])
    ot[...] = jnp.where(first, wout_a[0], wout_b[0])
    os[...] = jnp.where(first, wout_b[0], wout_a[0])
    gain_t = jnp.where(first, gain_a[...], gain_b[...])
    gain_s = jnp.where(first, gain_b[...], gain_a[...])
    head_row = head[...]
    h_hi, h_mid = split(head_row)
    h_lo = (head_row - h_hi.astype(F32) - h_mid.astype(F32)).astype(BF16)
    h_rows = stack([h_hi, h_mid, h_lo, jnp.zeros((13, D), BF16)])
    rows_s[...] = jnp.zeros((8, D), F32)
    rows_s[0:1, :] = jnp.sum(dot_nt(h_rows, os[...]), axis=0, keepdims=True)
    rows_s[6:7, :] = gain_t
    rows_s[7:8, :] = gain_s
    for ref in (acc_q, acc_k, acc_v, acc_n, acc_g):
        ref[...] = jnp.zeros((16, D), F32)

    xc = cls[...].astype(F32)
    inv = lax.rsqrt(jnp.mean(xc * xc, axis=-1, keepdims=True) + NORM_EPS)
    xhat_c = xc * inv
    normed_c = (xhat_c * gain_t).astype(BF16)
    qkv_c = dot(normed_c, wt[...])
    kq = stack([qkv_c[:, D : 2 * D], qkv_c[:, :D]])
    kq_inv = lax.rsqrt(head_sums(kq * kq, ones) + HEAD_EPS)
    kq_unit = kq * kq_inv
    xhat_t[ALL:, :] = xhat_c
    normed_t[ALL:, :] = normed_c
    inv_c[...] = jnp.broadcast_to(inv, (16, 128))
    k_t[ALL:, :] = kq_unit[:16]
    kn_t[ALL:, :] = kq_inv[:16]
    q_t[...] = kq_unit[16:]
    qn_t[...] = kq_inv[16:]
    v_t[ALL:, :] = qkv_c[:, 2 * D :].astype(BF16)
    e_cls[...] = jnp.exp(logits_t(kq_unit[:16], kq_unit[16:], masks))

    @pl.loop(0, CHUNKS)
    def _(c):
        rows = chunk_rows(c)
        tile_enc = enc[pl.ds(pl.multiple_of(tile * 16, 16), 16), :]
        pixel = pix[pl.ds(c * 4, 4), :, :].astype(F32).reshape(SEQS, 16, D)
        x = (pixel + tile_enc[None]).reshape(ROWS, D)
        inv = lax.rsqrt(jnp.mean(x * x, axis=-1, keepdims=True) + NORM_EPS)
        xhat = x * inv
        normed = (xhat * rows_s[6:7, :]).astype(BF16)
        xhat_t[rows, :] = xhat
        normed_t[rows, :] = normed
        kv = dot(normed, wt[:, D:])
        v = kv[:, D:].astype(BF16)
        v_t[rows, :] = v
        k = kv[:, :D]
        k_inv = lax.rsqrt(head_sums(k * k, head_ones()) + HEAD_EPS)
        k = k * k_inv
        k_t[rows, :] = k
        kn_t[rows, :] = k_inv
        raised = jnp.exp(logits_t(k, q_t[...], masks))
        shown = (iota((ROWS, 128), 0) & 15) < counts[tile]
        e_dates = jnp.where(shown, raised, 0.0).reshape(SEQS, DATES, 128)
        e_class = e_cls[...]
        total = jnp.sum(e_dates, axis=1, keepdims=True) + jnp.sum(e_class, axis=0, keepdims=True)[None]
        total_inv = 1.0 / total
        a_dates = e_dates * total_inv
        a_class = e_class[None] * total_inv
        ad[rows, :] = a_dates.reshape(ROWS, 128)
        ac[rows, :] = a_class.reshape(ROWS, 128)
        v_class = v_t[ALL:, :]
        parts = []
        for s in range(SEQS):
            weights = stack([a_class[s], a_dates[s]]).astype(BF16)
            values = stack([v_class, v[s * 16 : s * 16 + 16]])
            parts.append(gathered_heads(dot_tn(weights, values)))
        att = stack(parts).astype(BF16)
        att_t[rows, :] = att
        updated = rounded(stack([cls[...].astype(F32)] * SEQS) + dot(att, ot[...]))
        seq_a[rows, :] = updated[:, :128]
        seq_b[rows, :] = updated[:, 128:]

    for i in range(CLASSES):
        u_s[i * PATCHES : (i + 1) * PATCHES, :128] = seq_a[pl.ds(i, PATCHES, stride=16), :]
        u_s[i * PATCHES : (i + 1) * PATCHES, 128:] = seq_b[pl.ds(i, PATCHES, stride=16), :]

    @pl.loop(0, CHUNKS)
    def _(c):
        rows = chunk_rows(c)
        u = u_s[rows, :]
        inv = lax.rsqrt(jnp.mean(u * u, axis=-1, keepdims=True) + NORM_EPS)
        xhat = u * inv
        normed = (xhat * rows_s[7:8, :]).astype(BF16)
        xhat_s[rows, :] = xhat
        normed_s[rows, :] = normed
        inv_s[rows, :] = jnp.broadcast_to(inv, (ROWS, 128))
        qkv = dot(normed, ws[...])
        v = qkv[:, 2 * D :].astype(BF16)
        kq = stack([qkv[:, D : 2 * D], qkv[:, :D]])
        kq_inv = lax.rsqrt(head_sums(kq * kq, head_ones()) + HEAD_EPS)
        kq_unit = kq * kq_inv
        k, q = kq_unit[:ROWS], kq_unit[ROWS:]
        k_s[rows, :] = k
        q_s[rows, :] = q
        kn_s[rows, :] = kq_inv[:ROWS]
        qn_s[rows, :] = kq_inv[ROWS:]
        v_s[rows, :] = v
        part = [slice(b * PATCHES, b * PATCHES + PATCHES) for b in range(CLASS_CHUNK)]
        raised = jnp.exp(stack([logits_t(k[p], q[p], masks) for p in part]))
        raised = raised.reshape(CLASS_CHUNK, PATCHES, HEADS * PATCHES)
        a = raised * (1.0 / jnp.sum(raised, axis=1, keepdims=True))
        a = a.reshape(ROWS, HEADS * PATCHES)
        a_s[rows, :] = a
        a16 = a.astype(BF16)
        wide = [dot_tn(a16[p], v[p]) for p in part]
        att = stack([gathered_heads(m) for m in wide]).astype(BF16)
        att_s[rows, :] = att
        raw = jnp.sum(u * head[...] + att.astype(F32) * rows_s[0:1, :], axis=-1, keepdims=True)
        log_s[rows, :] = jnp.broadcast_to(CAP * jnp.tanh(raw / CAP), (ROWS, 128))

    tot[...] = jnp.sum(jnp.exp(log_s[...]).reshape(CLASSES, PATCHES, 128), axis=0)

    @pl.loop(0, CHUNKS)
    def _(c):
        rows = chunk_rows(c)
        u = u_s[rows, :]
        xhat = xhat_s[rows, :]
        attf = att_s[rows, :].astype(F32)
        logit = log_s[rows, 0:1]
        total = stack([tot[:, 0:1]] * CLASS_CHUNK)
        eye = iota((PATCHES, PATCHES), 0) == iota((PATCHES, PATCHES), 1)
        label_row = labels[pl.ds(tile, 1), :].astype(F32)
        label = jnp.sum(jnp.where(eye, label_row, 0.0), axis=-1, keepdims=True)
        base = (c * CLASS_CHUNK).astype(F32)
        mine = stack([jnp.where(label == base + b, 1.0, 0.0) for b in range(CLASS_CHUNK)])
        d_logit = (jnp.exp(logit) / total - mine) * (1.0 / 64.0)
        ratio = logit / CAP
        d_raw_logit = d_logit * (1.0 - ratio * ratio)
        ce = jnp.sum(mine * (jnp.log(total) - logit), axis=0, keepdims=True) * (1.0 / 768.0)
        rows_s[5:6, :] += jnp.where(iota((1, D), 1) == slots[tile], ce, 0.0)
        rows_s[1:2, :] += jnp.sum(attf * d_raw_logit, axis=0, keepdims=True)
        rows_s[2:3, :] += jnp.sum(u * d_raw_logit, axis=0, keepdims=True)
        d_att = (d_raw_logit * rows_s[0:1, :]).astype(BF16)
        v = v_s[rows, :]
        k = k_s[rows, :]
        q = q_s[rows, :]
        a_all = a_s[rows, :]
        part = [slice(b * PATCHES, b * PATCHES + PATCHES) for b in range(CLASS_CHUNK)]
        a16 = a_all.astype(BF16)
        da_parts, dv_parts = [], []
        for p in part:
            wide = spread(d_att[p], masks)
            da_parts.append(dot_nt(v[p], wide))
            dv_parts.append(dot(a16[p], wide))
        dv = stack(dv_parts).astype(BF16)
        cube = lambda m: m.reshape(CLASS_CHUNK, PATCHES, HEADS * PATCHES)
        da, a = cube(rounded(stack(da_parts))), cube(a_all)
        ds = (SHARP * a * (da - jnp.sum(da * a, axis=1, keepdims=True))).reshape(ROWS, HEADS * PATCHES)
        dk_parts = [three_pass(ds[p], *spread_pair(q[p], masks)) for p in part]
        dq_parts = [gathered_heads(m) for m in [three_pass_tn(ds[p], k[p]) for p in part]]
        unit = stack([k, q])
        scale = stack([kn_s[rows, :], qn_s[rows, :]])
        d_unit = stack(dk_parts + dq_parts)
        d_raw = scale * (d_unit - unit * head_sums(d_unit * unit, head_ones()))
        dk_raw, dq_raw = d_raw[:ROWS], d_raw[ROWS:]
        c_v = rounded(dot_nt(dv, ws[:, 2 * D :]))
        c_k = rounded(wide_dot_nt(dk_raw, ws[:, D : 2 * D]))
        c_q = rounded(wide_dot_nt(dq_raw, ws[:, :D]))
        dn = rounded(rounded(c_v + c_k) + c_q)
        rows_s[4:5, :] += jnp.sum(dn * xhat, axis=0, keepdims=True)
        y = jnp.where(share == 0, dq_raw, jnp.where(share == 1, dk_raw, dv.astype(F32)))
        hi, lo = split(y)
        y_hi[rows, :] = hi
        y_lo[rows, :] = lo
        z = dn * rows_s[7:8, :]
        dx = inv_s[rows, 0:1] * (z - xhat * jnp.mean(z * xhat, axis=-1, keepdims=True))
        u_s[rows, :] = rounded(d_raw_logit * head[...] + dx)

    for i in range(CLASSES):
        seq_a[pl.ds(i, PATCHES, stride=16), :] = u_s[i * PATCHES : (i + 1) * PATCHES, :128]
        seq_b[pl.ds(i, PATCHES, stride=16), :] = u_s[i * PATCHES : (i + 1) * PATCHES, 128:]

    w_row = rows_s[1:2, :]
    w_hi, w_mid = split(w_row)
    w_lo = (w_row - w_hi.astype(F32) - w_mid.astype(F32)).astype(BF16)
    zero = jnp.zeros((12, D), BF16)
    w_rows = stack([w_hi, w_mid, w_lo, zero, zero[:1]])
    d_head = rows_s[2:3, :] + jnp.sum(dot(w_rows, os[...]), axis=0, keepdims=True)

    @pl.when(jnp.logical_and(scal[1] == 0, share < 3))
    def _():
        x = normed_s[...]
        d_w = dot_tn(x, y_hi[0:ALL, :]) + dot_tn(x, y_lo[0:ALL, :])
        put_tiles(keep, give, lower, d_w)

    @pl.when(jnp.logical_and(scal[1] == 0, share == 3))
    def _():
        d_w = dot_tn(stack([w_hi, w_hi, w_mid, w_mid, zero]), stack([h_hi, h_mid, h_hi, h_mid, zero]))
        put_tiles(keep, give, lower, d_w)

    @pl.loop(0, CHUNKS)
    def _(c):
        rows = chunk_rows(c)
        g = jnp.concatenate([seq_a[rows, :], seq_b[rows, :]], axis=1).astype(BF16)
        d_att = dot_nt(g, ot[...]).astype(BF16)
        v = v_t[rows, :]
        v_class = v_t[ALL:, :]
        k = k_t[rows, :]
        k_class = k_t[ALL:, :]
        q = q_t[...]
        a_dates = ad[rows, :]
        a_class = ac[rows, :]
        da_class, da_dates, dv_class, dv_dates = [], [], [], []
        for s in range(SEQS):
            part = slice(s * 16, s * 16 + 16)
            wide = spread(d_att[part], masks)
            values = stack([v_class, v[part]])
            weights = stack([a_class[part], a_dates[part]]).astype(BF16)
            da = rounded(dot_nt(values, wide))
            dv = dot(weights, wide).astype(BF16)
            da_class.append(da[:16])
            da_dates.append(da[16:])
            dv_class.append(dv[:16])
            dv_dates.append(dv[16:])
        cube = lambda m: m.reshape(SEQS, 16, 128)
        da_c, da_d = stack(da_class), stack(da_dates)
        both = jnp.sum(cube(da_c * a_class), axis=1, keepdims=True) + jnp.sum(
            cube(da_d * a_dates), axis=1, keepdims=True
        )
        ds_c = SHARP * cube(a_class) * (cube(da_c) - both)
        ds_d = SHARP * cube(a_dates) * (cube(da_d) - both)
        q_hi, q_lo = spread_pair(q, masks)
        dk = three_pass(stack([ds_d.reshape(ROWS, 128), ds_c.reshape(ROWS, 128)]), q_hi, q_lo)
        dq_parts = []
        for s in range(SEQS):
            ds_s = stack([ds_c[s], ds_d[s]])
            k_all = stack([k_class, k[s * 16 : s * 16 + 16]])
            dq_parts.append(gathered_heads(three_pass_tn(ds_s, k_all)))
        unit = stack([k] + [k_class] * SEQS + [q] * SEQS)
        scale = stack([kn_t[rows, :]] + [kn_t[ALL:, :]] * SEQS + [qn_t[...]] * SEQS)
        d_unit = stack([dk] + dq_parts)
        d_raw = scale * (d_unit - unit * head_sums(d_unit * unit, head_ones()))
        dk_raw, dq_raw = d_raw[: 2 * ROWS], d_raw[2 * ROWS :]
        dv = stack(dv_dates + dv_class)
        c_v = rounded(dot_nt(dv, wt[:, 2 * D :]))
        c_k = rounded(wide_dot_nt(dk_raw, wt[:, D : 2 * D]))
        c_q = rounded(wide_dot_nt(dq_raw, wt[:, :D]))
        dn = rounded(c_v + c_k)
        rows_s[3:4, :] += jnp.sum(dn[:ROWS] * xhat_t[rows, :], axis=0, keepdims=True)
        acc_n[...] += fold(rounded(dn[ROWS:] + c_q))
        acc_g[...] += fold(g.astype(F32))
        acc_q[...] += fold(dq_raw)
        acc_k[...] += fold(dk_raw[ROWS:])
        acc_v[...] += fold(dv[ROWS:].astype(F32))
        of_dates = jnp.where(share == 1, dk_raw[:ROWS], dv[:ROWS].astype(F32))
        y = jnp.where(share == 0, 0.0, jnp.where(share == 3, g.astype(F32), of_dates))
        hi, lo = split(y)

        @pl.when(first)
        def _():
            y_hi[rows, :] = hi
            y_lo[rows, :] = lo

    dn_c = acc_n[...]
    xhat_c = xhat_t[ALL:, :]
    z = dn_c * rows_s[6:7, :]
    d_norm = inv_c[:, 0:1] * (z - xhat_c * jnp.mean(z * xhat_c, axis=-1, keepdims=True))
    d_cls[...] = acc_g[...] + d_norm
    gain_grad_t = rows_s[3:4, :] + jnp.sum(dn_c * xhat_c, axis=0, keepdims=True)
    gain_grad = jnp.where(first, gain_grad_t, rows_s[4:5, :])

    @pl.when(jnp.logical_and(first, share < 3))
    def _():
        y = jnp.where(share == 0, acc_q[...], jnp.where(share == 1, acc_k[...], acc_v[...]))
        hi, lo = split(y)
        y_hi[ALL:, :] = hi
        y_lo[ALL:, :] = lo
        x = normed_t[...]
        d_w = dot_tn(x, y_hi[...]) + dot_tn(x, y_lo[...])
        put_tiles(keep, give, lower, d_w)

    @pl.when(jnp.logical_and(first, share == 3))
    def _():
        put_tiles(keep, give, lower, dot_tn(att_t[...], y_hi[0:ALL, :]))

    misc = jnp.where(share == 0, gain_grad, jnp.where(share == 1, d_head, rows_s[5:6, :]))
    for b in range(SHARE):
        row = d_cls[pl.ds(4 * share + b, 1), :]
        small = stack([row[:, :128], row[:, 128:], misc[:, :128], misc[:, 128:], jnp.zeros((4, 128), F32)])
        for y in range(YS):
            keep[TILES_DEV * y + b, 8:16, :] = small
            give[TILES_DEV * y + b, 8:16, :] = small


STEP_SCRATCH = [
    ((D, 3 * D), BF16), ((D, 3 * D), BF16), ((D, D), BF16), ((D, D), BF16),
    ((ALL, 128), F32), ((ALL, 128), F32), ((ALL + 16, D), F32), ((ALL + 16, D), BF16), ((ALL + 16, D), F32), ((ALL + 16, D), F32),
    ((ALL + 16, D), BF16), ((ALL, 128), F32), ((ALL, 128), F32), ((ALL, D), BF16),
    ((16, D), F32), ((16, D), F32), ((16, 128), F32), ((16, 128), F32),
    ((ALL, D), F32), ((ALL, D), F32), ((ALL, D), BF16), ((ALL, 128), F32),
    ((ALL, D), F32), ((ALL, D), F32), ((ALL, D), F32), ((ALL, D), F32), ((ALL, D), BF16),
    ((ALL, HEADS * PATCHES), F32), ((ALL, D), BF16), ((ALL, 128), F32), ((PATCHES, 128), F32), ((8, D), F32),
    ((ALL + 16, D), BF16), ((ALL + 16, D), BF16),
    ((16, D), F32), ((16, D), F32), ((16, D), F32), ((16, D), F32), ((16, D), F32), ((16, D), F32),
    ((HEADS, PATCHES, D), BF16),
]


def encode(x, at):
    rows = x.shape[1]
    top = jnp.max(jnp.abs(x), axis=2, keepdims=True)
    power = jnp.floor(jnp.log2(jnp.maximum(top, 1e-30))) + 1.0
    coded = jnp.floor(x * (CODE_TOP * jnp.exp2(-power)) + 0.5)
    eye = iota((1, rows, 128), 1) == iota((1, rows, 128), 2)
    powers = jnp.sum(jnp.where(eye, power, 0.0), axis=1, keepdims=True)
    coded = jnp.where(iota((1, rows, 128), 1) == at, powers, coded)
    return coded.astype(I32).astype(jnp.int16)


def decode(coded, at):
    rows = coded.shape[1]
    x = coded.astype(I32).astype(F32)
    eye = iota((1, rows, 128), 1) == iota((1, rows, 128), 2)
    power = jnp.sum(jnp.where(eye, x[:, at : at + 1, :], 0.0), axis=2, keepdims=True)
    return x * (jnp.exp2(power) * (1.0 / CODE_TOP))


def code_pair(keep, given, out):
    out[...] = encode(keep[...] + given[...], 12)


def reduce_tiles(parts, out):
    total = jnp.sum(decode(parts[...], 12), axis=0)
    out[...] = jnp.broadcast_to(total[None], (YS, 16, 128))


def assemble(blocks, out):
    small = jnp.where(iota((8, 128), 0) < 4, blocks[0, 8:16, :], 0.0)
    whole = stack([blocks[y, 0:8, :] for y in range(YS)] + [small])
    out[...] = jnp.broadcast_to(encode(whole[None], 68), (MEMBERS, CHUNK, 128))


def unpack(core, mine, other, loss, d_class, d_gain, d_qkv, d_out, d_head):
    lower = core[0] == 0
    for part in range(4):
        spot = slice(SHARE * part, SHARE * part + SHARE)
        owns, fars = decode(mine[spot], 68), decode(other[spot], 68)
        for b in range(SHARE):
            own, far = owns[b], fars[b]
            blocks = (jnp.where(lower, own, far), jnp.where(lower, far, own))
            for c in range(2):
                for y in range(YS):
                    tile = blocks[c][8 * y : 8 * y + 8]
                    row, lane = tile_at(y, c, b)
                    if part < 3:
                        d_qkv[0, row : row + 8, part * D + lane : part * D + lane + 128] = tile
                    else:
                        d_out[0, row : row + 8, lane : lane + 128] = tile
            at = 4 * part + b
            small = blocks[0]
            d_class[at : at + 1, :128] = small[64:65]
            d_class[at : at + 1, 128:] = small[65:66]
            if b == 0 and part < 3:
                ref = (d_gain, d_head, loss)[part]
                ref[:, :128] = small[66:67]
                ref[:, 128:] = small[67:68]


VM = pl.BlockSpec()
SM = pl.BlockSpec(memory_space=pltpu.SMEM)


def call(body, in_specs, outs, *args, scratch=()):
    return pl.pallas_call(
        body,
        out_shape=[jax.ShapeDtypeStruct(s, t) for s, t in outs],
        in_specs=in_specs,
        out_specs=[VM] * len(outs),
        scratch_shapes=[pltpu.VMEM(s, t) for s, t in scratch],
        compiler_params=pltpu.CompilerParams(vmem_limit_bytes=48 * 1024 * 1024),
    )(*args)


def encodings(date_days):
    band = jnp.arange(D)
    frequency = jnp.exp((band // 2 * 2).astype(F32) * (-math.log(10000.0) / D))
    phases = date_days.astype(F32)[:, :, None] * frequency
    return jnp.where(band % 2 == 0, jnp.sin(phases), jnp.cos(phases)).reshape(TILES_DEV * 16, D)


def swap(v):
    return lax.ppermute(v, "pipe", [(0, 1), (1, 0)])


def whole_step(
    pixels,
    date_days,
    clear_count,
    batch_slot,
    labels,
    class_tokens,
    section_gain,
    wqkv,
    wout,
    head_vec,
):
    first = (lax.axis_index("pipe") == 0).astype(I32)
    inner = lax.axis_index(INNER).astype(I32)
    by_dest = jnp.tile(pixels.reshape(TILES_DEV, PATCHES, D), (SHARE, 1, 1))
    whole_tile = lax.all_to_all(by_dest, INNER, 0, 0, tiled=True)
    core = lax.axis_index("core").astype(I32)
    keep, give = call(
        step,
        [SM] * 3 + [VM] * 11,
        [((OWNERS, 16, 128), F32)] * 2,
        jnp.stack([inner, first, core]),
        clear_count,
        batch_slot,
        labels,
        whole_tile,
        encodings(date_days),
        class_tokens,
        section_gain,
        swap(section_gain),
        wqkv,
        swap(wqkv),
        wout,
        swap(wout),
        head_vec.reshape(1, D),
        scratch=STEP_SCRATCH,
    )
    given = lax.ppermute(give, "core", [(0, 1), (1, 0)])
    (coded,) = call(code_pair, [VM, VM], [((OWNERS, 16, 128), jnp.int16)], keep, given)
    parts = lax.all_to_all(coded, ("y", "b"), 0, 0, tiled=True)
    (total,) = call(reduce_tiles, [VM], [((YS, 16, 128), F32)], parts)
    blocks = lax.all_to_all(total, "y", 0, 0, tiled=True)
    (whole,) = call(assemble, [VM], [((MEMBERS, CHUNK, 128), jnp.int16)], blocks)
    mine = lax.all_to_all(whole, INNER, 0, 0, tiled=True)
    other = lax.ppermute(mine, "core", [(0, 1), (1, 0)])
    loss, d_class, d_gain, d_qkv, d_out, d_head = call(
        unpack,
        [SM, VM, VM],
        [
            ((1, D), F32),
            ((16, D), F32),
            ((1, D), F32),
            ((1, D, 3 * D), F32),
            ((1, D, D), F32),
            ((1, D), F32),
        ],
        core[None],
        mine,
        other,
    )
    return (loss[0, :MICRO], d_class, d_gain, d_qkv, d_out, d_head.reshape(D))


def solution(mesh):
    cut = Mesh(mesh.devices.reshape(2, YS, 2, TILES_DEV, SHARE), ("pipe",) + DP + INNER)
    placed = (
        P(DP, INNER, None, None),
        P(DP, None),
        P(DP),
        P(DP),
        P(DP, None),
        P(),
        P("pipe", None),
        P("pipe", None, None),
        P("pipe", None, None),
        P(),
    )
    return jax.shard_map(
        whole_step,
        mesh=cut,
        in_specs=placed,
        out_specs=(P(), P(), P("pipe", None), P("pipe", None, None), P("pipe", None, None), P()),
        check_vma=False,
    )
```

```python
import math

import jax
import jax.numpy as jnp
from jax import lax
from jax.experimental import pallas as pl
from jax.experimental.pallas import tpu as pltpu
from jax.sharding import Mesh, PartitionSpec as P


D = 256
HEADS = 8
CLASSES = 16
PATCHES = 48
MICRO = 4
SHARP = 10.0
CAP = 15.0
NORM_EPS = 1e-05
HEAD_EPS = 1e-06
F32 = jnp.float32
BF16 = jnp.bfloat16
I32 = jnp.int32

TILES_DEV = 4
DATES = 16
CHUNKS = 4
SEQS = PATCHES // CHUNKS
CLASS_CHUNK = CLASSES // CHUNKS
ROWS = SEQS * 16
ALL = CHUNKS * ROWS
MEMBERS = 16
SHARE = 4
YS = 8
OWNERS = 32
CODE_TOP = 32000.0
CHUNK = 72
DP = ("y", "core")
INNER = ("r", "b")


def dot(a, b):
    return lax.dot_general(a, b, (((1,), (0,)), ((), ())), preferred_element_type=F32)


def dot_nt(a, b):
    return lax.dot_general(a, b, (((1,), (1,)), ((), ())), preferred_element_type=F32)


def dot_tn(a, b):
    return lax.dot_general(a, b, (((0,), (0,)), ((), ())), preferred_element_type=F32)


def split(x):
    hi = x.astype(BF16)
    return hi, (x - hi.astype(F32)).astype(BF16)


def rounded(x):
    return x.astype(BF16).astype(F32)


def iota(shape, axis):
    return lax.broadcasted_iota(I32, shape, axis)


def head_ones():
    same = (iota((D, D), 0) >> 5) == (iota((D, D), 1) >> 5)
    return jnp.where(same, 1.0, 0.0).astype(BF16)


def head_sums(x, ones):
    hi, lo = split(x)
    return dot(hi, ones) + dot(lo, ones)


def spread(rows_of, masks):
    n = rows_of.shape[0]
    return jnp.concatenate([rows_of * masks[h, 0:n, :] for h in range(HEADS)], axis=0)


def spread_pair(rows_of, masks):
    hi, lo = split(rows_of)
    return spread(hi, masks), spread(lo, masks)


def gathered_heads(wide):
    n = wide.shape[0] // HEADS
    lane_head = iota((n, D), 1) >> 5
    out = wide[:n]
    for h in range(1, HEADS):
        out = jnp.where(lane_head == h, wide[h * n : (h + 1) * n], out)
    return out


def logits_t(k, q, masks):
    n = k.shape[0]
    k_hi, k_lo = split(k)
    q_hi, q_lo = spread_pair(q, masks)
    both = dot_nt(jnp.concatenate([k_hi, k_lo], axis=0), q_hi)
    return SHARP * (both[:n] + both[n:] + dot_nt(k_hi, q_lo))


def three_pass(x_hi, x_lo, w_hi, w_lo):
    n = x_hi.shape[0]
    both = dot(jnp.concatenate([x_hi, x_lo], axis=0), w_hi)
    return both[:n] + both[n:] + dot(x_hi, w_lo)


def three_pass_tn(x_hi, x_lo, y_hi, y_lo):
    return dot_tn(
        jnp.concatenate([x_hi, x_hi, x_lo], axis=0), jnp.concatenate([y_hi, y_lo, y_hi], axis=0)
    )


def stack(parts):
    return jnp.concatenate(parts, axis=0)


def fold(rows):
    return jnp.sum(rows.reshape(-1, 16, D), axis=0)


def chunk_rows(c):
    return pl.ds(pl.multiple_of(c * ROWS, ROWS), ROWS)


def tile_at(y, c, b):
    n = (2 * y + c) * TILES_DEV + b
    return 8 * (n // 2), 128 * (n % 2)


def put_tiles(keep, give, lower, d_w):
    for y in range(YS):
        for b in range(TILES_DEV):
            pair = []
            for c in range(2):
                row, lane = tile_at(y, c, b)
                pair.append(d_w[row : row + 8, lane : lane + 128])
            keep[TILES_DEV * y + b, 0:8, :] = jnp.where(lower, pair[0], pair[1])
            give[TILES_DEV * y + b, 0:8, :] = jnp.where(lower, pair[1], pair[0])


def step(
    scal, counts, slots, labels, pix, enc, cls, gain_a, gain_b, wqkv_a, wout_a, half_a, half_b, head, keep, give, *scratch
):
    (wt, ws, ot, os, seq_a, seq_b, xhat_t, normed_t, k_t, kn_t, v_t, ad, ac, att_t, q_t, qn_t, e_cls, inv_c,
     u_s, xhat_s, normed_s, inv_s, k_s, kn_s, q_s, qn_s, v_s, a_s, att_s, log_s, tot, rows_s, y_w,
     acc_q, acc_k, acc_v, acc_n, acc_g, d_cls, masks) = scratch
    first = scal[1] == 1
    tile = scal[0] & 3
    share = scal[0] >> 2
    lower = scal[2] == 0
    ones = head_ones()
    lane_head = iota((PATCHES, D), 1) >> 5
    for h in range(HEADS):
        masks[h] = jnp.where(lane_head == h, 1.0, 0.0).astype(BF16)
    for i in range(2):
        at = slice(128 * i, 128 * i + 128)
        far = jnp.where(scal[2] == i, half_a[...], half_b[...])
        wt[at, :] = jnp.where(first, wqkv_a[0, at, :], far[:, : 3 * D])
        ws[at, :] = jnp.where(first, far[:, : 3 * D], wqkv_a[0, at, :])
        ot[at, :] = jnp.where(first, wout_a[0, at, :], far[:, 3 * D :])
        os[at, :] = jnp.where(first, far[:, 3 * D :], wout_a[0, at, :])
    gain_t = jnp.where(first, gain_a[...], gain_b[...])
    gain_s = jnp.where(first, gain_b[...], gain_a[...])
    head_row = head[...]
    h_hi, h_mid = split(head_row)
    h_lo = (head_row - h_hi.astype(F32) - h_mid.astype(F32)).astype(BF16)
    h_rows = stack([h_hi, h_mid, h_lo, jnp.zeros((13, D), BF16)])
    rows_s[...] = jnp.zeros((8, D), F32)
    rows_s[0:1, :] = jnp.sum(dot_nt(h_rows, os[...]), axis=0, keepdims=True)
    rows_s[6:7, :] = gain_t
    rows_s[7:8, :] = gain_s
    for ref in (acc_q, acc_k, acc_v, acc_n, acc_g):
        ref[...] = jnp.zeros((16, D), F32)

    xc = cls[...].astype(F32)
    inv = lax.rsqrt(jnp.mean(xc * xc, axis=-1, keepdims=True) + NORM_EPS)
    xhat_c = xc * inv
    normed_c = (xhat_c * gain_t).astype(BF16)
    qkv_c = dot(normed_c, wt[...])
    kq = stack([qkv_c[:, D : 2 * D], qkv_c[:, :D]])
    kq_inv = lax.rsqrt(head_sums(kq * kq, ones) + HEAD_EPS)
    kq_unit = kq * kq_inv
    xhat_t[ALL:, :] = xhat_c
    normed_t[ALL:, :] = normed_c
    inv_c[...] = jnp.broadcast_to(inv, (16, 128))
    k_t[ALL:, :] = kq_unit[:16]
    kn_t[ALL:, :] = kq_inv[:16]
    q_t[...] = kq_unit[16:]
    qn_t[...] = kq_inv[16:]
    v_t[ALL:, :] = qkv_c[:, 2 * D :].astype(BF16)
    e_cls[...] = jnp.exp(logits_t(kq_unit[:16], kq_unit[16:], masks))

    @pl.loop(0, CHUNKS)
    def _(c):
        rows = chunk_rows(c)
        tile_enc = enc[pl.ds(pl.multiple_of(tile * 16, 16), 16), :]
        pixel = pix[pl.ds(c * 4, 4), :, :].astype(F32).reshape(SEQS, 16, D)
        x = (pixel + tile_enc[None]).reshape(ROWS, D)
        inv = lax.rsqrt(jnp.mean(x * x, axis=-1, keepdims=True) + NORM_EPS)
        xhat = x * inv
        normed = (xhat * rows_s[6:7, :]).astype(BF16)
        xhat_t[rows, :] = xhat
        normed_t[rows, :] = normed
        kv = dot(normed, wt[:, D:])
        v = kv[:, D:].astype(BF16)
        v_t[rows, :] = v
        k = kv[:, :D]
        k_inv = lax.rsqrt(head_sums(k * k, head_ones()) + HEAD_EPS)
        k = k * k_inv
        k_t[rows, :] = k
        kn_t[rows, :] = k_inv
        raised = jnp.exp(logits_t(k, q_t[...], masks))
        shown = (iota((ROWS, 128), 0) & 15) < counts[tile]
        e_dates = jnp.where(shown, raised, 0.0).reshape(SEQS, DATES, 128)
        e_class = e_cls[...]
        total = jnp.sum(e_dates, axis=1, keepdims=True) + jnp.sum(e_class, axis=0, keepdims=True)[None]
        total_inv = 1.0 / total
        a_dates = e_dates * total_inv
        a_class = e_class[None] * total_inv
        ad[rows, :] = a_dates.reshape(ROWS, 128)
        ac[rows, :] = a_class.reshape(ROWS, 128)
        v_class = v_t[ALL:, :]
        parts = []
        for s in range(SEQS):
            weights = stack([a_class[s], a_dates[s]]).astype(BF16)
            values = stack([v_class, v[s * 16 : s * 16 + 16]])
            parts.append(gathered_heads(dot_tn(weights, values)))
        att = stack(parts).astype(BF16)
        att_t[rows, :] = att
        updated = rounded(stack([cls[...].astype(F32)] * SEQS) + dot(att, ot[...]))
        seq_a[rows, :] = updated[:, :128]
        seq_b[rows, :] = updated[:, 128:]

    for i in range(CLASSES):
        u_s[i * PATCHES : (i + 1) * PATCHES, :128] = seq_a[pl.ds(i, PATCHES, stride=16), :]
        u_s[i * PATCHES : (i + 1) * PATCHES, 128:] = seq_b[pl.ds(i, PATCHES, stride=16), :]

    @pl.loop(0, CHUNKS)
    def _(c):
        rows = chunk_rows(c)
        u = u_s[rows, :]
        inv = lax.rsqrt(jnp.mean(u * u, axis=-1, keepdims=True) + NORM_EPS)
        xhat = u * inv
        normed = (xhat * rows_s[7:8, :]).astype(BF16)
        xhat_s[rows, :] = xhat
        normed_s[rows, :] = normed
        inv_s[rows, :] = jnp.broadcast_to(inv, (ROWS, 128))
        qkv = dot(normed, ws[...])
        v = qkv[:, 2 * D :].astype(BF16)
        kq = stack([qkv[:, D : 2 * D], qkv[:, :D]])
        kq_inv = lax.rsqrt(head_sums(kq * kq, head_ones()) + HEAD_EPS)
        kq_unit = kq * kq_inv
        k, q = kq_unit[:ROWS], kq_unit[ROWS:]
        k_s[rows, :] = k
        q_s[rows, :] = q
        kn_s[rows, :] = kq_inv[:ROWS]
        qn_s[rows, :] = kq_inv[ROWS:]
        v_s[rows, :] = v
        part = [slice(b * PATCHES, b * PATCHES + PATCHES) for b in range(CLASS_CHUNK)]
        raised = jnp.exp(stack([logits_t(k[p], q[p], masks) for p in part]))
        raised = raised.reshape(CLASS_CHUNK, PATCHES, HEADS * PATCHES)
        a = raised * (1.0 / jnp.sum(raised, axis=1, keepdims=True))
        a = a.reshape(ROWS, HEADS * PATCHES)
        a_s[rows, :] = a
        a16 = a.astype(BF16)
        wide = [dot_tn(a16[p], v[p]) for p in part]
        att = stack([gathered_heads(m) for m in wide]).astype(BF16)
        att_s[rows, :] = att
        raw = jnp.sum(u * head[...] + att.astype(F32) * rows_s[0:1, :], axis=-1, keepdims=True)
        log_s[rows, :] = jnp.broadcast_to(CAP * jnp.tanh(raw / CAP), (ROWS, 128))

    tot[...] = jnp.sum(jnp.exp(log_s[...]).reshape(CLASSES, PATCHES, 128), axis=0)

    @pl.loop(0, CHUNKS)
    def _(c):
        rows = chunk_rows(c)
        u = u_s[rows, :]
        xhat = xhat_s[rows, :]
        attf = att_s[rows, :].astype(F32)
        logit = log_s[rows, 0:1]
        total = stack([tot[:, 0:1]] * CLASS_CHUNK)
        eye = iota((PATCHES, PATCHES), 0) == iota((PATCHES, PATCHES), 1)
        label_row = labels[pl.ds(tile, 1), :].astype(F32)
        label = jnp.sum(jnp.where(eye, label_row, 0.0), axis=-1, keepdims=True)
        base = (c * CLASS_CHUNK).astype(F32)
        mine = stack([jnp.where(label == base + b, 1.0, 0.0) for b in range(CLASS_CHUNK)])
        d_logit = (jnp.exp(logit) / total - mine) * (1.0 / 64.0)
        ratio = logit / CAP
        d_raw_logit = d_logit * (1.0 - ratio * ratio)
        ce = jnp.sum(mine * (jnp.log(total) - logit), axis=0, keepdims=True) * (1.0 / 768.0)
        rows_s[5:6, :] += jnp.where(iota((1, D), 1) == slots[tile], ce, 0.0)
        rows_s[1:2, :] += jnp.sum(attf * d_raw_logit, axis=0, keepdims=True)
        rows_s[2:3, :] += jnp.sum(u * d_raw_logit, axis=0, keepdims=True)
        d_att = (d_raw_logit * rows_s[0:1, :]).astype(BF16)
        v = v_s[rows, :]
        k = k_s[rows, :]
        q = q_s[rows, :]
        a_all = a_s[rows, :]
        part = [slice(b * PATCHES, b * PATCHES + PATCHES) for b in range(CLASS_CHUNK)]
        a16 = a_all.astype(BF16)
        da_parts, dv_parts = [], []
        for p in part:
            wide = spread(d_att[p], masks)
            da_parts.append(dot_nt(v[p], wide))
            dv_parts.append(dot(a16[p], wide))
        dv = stack(dv_parts).astype(BF16)
        cube = lambda m: m.reshape(CLASS_CHUNK, PATCHES, HEADS * PATCHES)
        da, a = cube(rounded(stack(da_parts))), cube(a_all)
        ds = (SHARP * a * (da - jnp.sum(da * a, axis=1, keepdims=True))).reshape(ROWS, HEADS * PATCHES)
        d_hi, d_lo = split(ds)
        k_hi, k_lo = split(k)
        dk_parts = [three_pass(d_hi[p], d_lo[p], *spread_pair(q[p], masks)) for p in part]
        wide = [three_pass_tn(d_hi[p], d_lo[p], k_hi[p], k_lo[p]) for p in part]
        dq_parts = [gathered_heads(m) for m in wide]
        unit = stack([k, q])
        scale = stack([kn_s[rows, :], qn_s[rows, :]])
        d_unit = stack(dk_parts + dq_parts)
        d_raw = scale * (d_unit - unit * head_sums(d_unit * unit, head_ones()))
        dk_raw, dq_raw = d_raw[:ROWS], d_raw[ROWS:]
        c_v = rounded(dot_nt(dv, ws[:, 2 * D :]))
        dk16, dq16 = dk_raw.astype(BF16), dq_raw.astype(BF16)
        c_k = rounded(dot_nt(dk16, ws[:, D : 2 * D]))
        c_q = rounded(dot_nt(dq16, ws[:, :D]))
        dn = rounded(rounded(c_v + c_k) + c_q)
        rows_s[4:5, :] += jnp.sum(dn * xhat, axis=0, keepdims=True)
        y_w[rows, :] = jnp.where(share == 0, dq16, jnp.where(share == 1, dk16, dv))
        z = dn * rows_s[7:8, :]
        dx = inv_s[rows, 0:1] * (z - xhat * jnp.mean(z * xhat, axis=-1, keepdims=True))
        u_s[rows, :] = rounded(d_raw_logit * head[...] + dx)

    for i in range(CLASSES):
        seq_a[pl.ds(i, PATCHES, stride=16), :] = u_s[i * PATCHES : (i + 1) * PATCHES, :128]
        seq_b[pl.ds(i, PATCHES, stride=16), :] = u_s[i * PATCHES : (i + 1) * PATCHES, 128:]

    w_row = rows_s[1:2, :]
    w_hi, w_mid = split(w_row)
    w_lo = (w_row - w_hi.astype(F32) - w_mid.astype(F32)).astype(BF16)
    zero = jnp.zeros((12, D), BF16)
    w_rows = stack([w_hi, w_mid, w_lo, zero, zero[:1]])
    d_head = rows_s[2:3, :] + jnp.sum(dot(w_rows, os[...]), axis=0, keepdims=True)

    @pl.when(jnp.logical_and(scal[1] == 0, share < 3))
    def _():
        x = normed_s[...]
        d_w = dot_tn(x, y_w[0:ALL, :])
        put_tiles(keep, give, lower, d_w)

    @pl.when(jnp.logical_and(scal[1] == 0, share == 3))
    def _():
        d_w = dot_tn(stack([w_hi, w_hi, w_mid, w_mid, zero]), stack([h_hi, h_mid, h_hi, h_mid, zero]))
        put_tiles(keep, give, lower, d_w)

    @pl.loop(0, CHUNKS)
    def _(c):
        rows = chunk_rows(c)
        g = jnp.concatenate([seq_a[rows, :], seq_b[rows, :]], axis=1).astype(BF16)
        d_att = dot_nt(g, ot[...]).astype(BF16)
        v = v_t[rows, :]
        v_class = v_t[ALL:, :]
        k = k_t[rows, :]
        k_class = k_t[ALL:, :]
        q = q_t[...]
        a_dates = ad[rows, :]
        a_class = ac[rows, :]
        da_class, da_dates, dv_class, dv_dates = [], [], [], []
        for s in range(SEQS):
            part = slice(s * 16, s * 16 + 16)
            wide = spread(d_att[part], masks)
            values = stack([v_class, v[part]])
            weights = stack([a_class[part], a_dates[part]]).astype(BF16)
            da = rounded(dot_nt(values, wide))
            dv = dot(weights, wide).astype(BF16)
            da_class.append(da[:16])
            da_dates.append(da[16:])
            dv_class.append(dv[:16])
            dv_dates.append(dv[16:])
        cube = lambda m: m.reshape(SEQS, 16, 128)
        da_c, da_d = stack(da_class), stack(da_dates)
        both = jnp.sum(cube(da_c * a_class), axis=1, keepdims=True) + jnp.sum(
            cube(da_d * a_dates), axis=1, keepdims=True
        )
        ds_c = SHARP * cube(a_class) * (cube(da_c) - both)
        ds_d = SHARP * cube(a_dates) * (cube(da_d) - both)
        q_hi, q_lo = spread_pair(q, masks)
        d_hi, d_lo = split(stack([ds_d.reshape(ROWS, 128), ds_c.reshape(ROWS, 128)]))
        dk = three_pass(d_hi, d_lo, q_hi, q_lo)
        k_hi, k_lo = split(k)
        kc_hi, kc_lo = split(k_class)
        dq_parts = []
        for s in range(SEQS):
            at, far = slice(s * 16, s * 16 + 16), slice(ROWS + s * 16, ROWS + s * 16 + 16)
            ds_s = [stack([m[at], m[far]]) for m in (d_hi, d_lo)]
            k_all = [stack([k_hi[at], kc_hi]), stack([k_lo[at], kc_lo])]
            dq_parts.append(gathered_heads(three_pass_tn(*ds_s, *k_all)))
        unit = stack([k] + [k_class] * SEQS + [q] * SEQS)
        scale = stack([kn_t[rows, :]] + [kn_t[ALL:, :]] * SEQS + [qn_t[...]] * SEQS)
        d_unit = stack([dk] + dq_parts)
        d_raw = scale * (d_unit - unit * head_sums(d_unit * unit, head_ones()))
        dk_raw, dq_raw = d_raw[: 2 * ROWS], d_raw[2 * ROWS :]
        dv = stack(dv_dates + dv_class)
        c_v = rounded(dot_nt(dv, wt[:, 2 * D :]))
        dk16 = dk_raw.astype(BF16)
        c_k = rounded(dot_nt(dk16, wt[:, D : 2 * D]))
        c_q = rounded(dot_nt(dq_raw.astype(BF16), wt[:, :D]))
        dn = rounded(c_v + c_k)
        rows_s[3:4, :] += jnp.sum(dn[:ROWS] * xhat_t[rows, :], axis=0, keepdims=True)
        acc_n[...] += fold(rounded(dn[ROWS:] + c_q))
        acc_g[...] += fold(g.astype(F32))
        acc_q[...] += fold(dq_raw)
        acc_k[...] += fold(dk_raw[ROWS:])
        acc_v[...] += fold(dv[ROWS:].astype(F32))
        of_dates = jnp.where(share == 1, dk16[:ROWS], dv[:ROWS])
        y = jnp.where(share == 3, g, jnp.where(share == 0, jnp.zeros_like(g), of_dates))

        @pl.when(first)
        def _():
            y_w[rows, :] = y

    dn_c = acc_n[...]
    xhat_c = xhat_t[ALL:, :]
    z = dn_c * rows_s[6:7, :]
    d_norm = inv_c[:, 0:1] * (z - xhat_c * jnp.mean(z * xhat_c, axis=-1, keepdims=True))
    d_cls[...] = acc_g[...] + d_norm
    gain_grad_t = rows_s[3:4, :] + jnp.sum(dn_c * xhat_c, axis=0, keepdims=True)
    gain_grad = jnp.where(first, gain_grad_t, rows_s[4:5, :])

    @pl.when(jnp.logical_and(first, share < 3))
    def _():
        y = jnp.where(share == 0, acc_q[...], jnp.where(share == 1, acc_k[...], acc_v[...]))
        hi, lo = split(y)
        y_w[ALL:, :] = hi
        d_w = dot_tn(normed_t[...], y_w[...]) + dot_tn(normed_t[ALL:, :], lo)
        put_tiles(keep, give, lower, d_w)

    @pl.when(jnp.logical_and(first, share == 3))
    def _():
        put_tiles(keep, give, lower, dot_tn(att_t[...], y_w[0:ALL, :]))

    misc = jnp.where(share == 0, gain_grad, jnp.where(share == 1, d_head, rows_s[5:6, :]))
    for b in range(SHARE):
        row = d_cls[pl.ds(4 * share + b, 1), :]
        small = stack([row[:, :128], row[:, 128:], misc[:, :128], misc[:, 128:], jnp.zeros((4, 128), F32)])
        for y in range(YS):
            keep[TILES_DEV * y + b, 8:16, :] = small
            give[TILES_DEV * y + b, 8:16, :] = small


STEP_SCRATCH = [
    ((D, 3 * D), BF16), ((D, 3 * D), BF16), ((D, D), BF16), ((D, D), BF16),
    ((ALL, 128), F32), ((ALL, 128), F32), ((ALL + 16, D), F32), ((ALL + 16, D), BF16), ((ALL + 16, D), F32), ((ALL + 16, D), F32),
    ((ALL + 16, D), BF16), ((ALL, 128), F32), ((ALL, 128), F32), ((ALL, D), BF16),
    ((16, D), F32), ((16, D), F32), ((16, 128), F32), ((16, 128), F32),
    ((ALL, D), F32), ((ALL, D), F32), ((ALL, D), BF16), ((ALL, 128), F32),
    ((ALL, D), F32), ((ALL, D), F32), ((ALL, D), F32), ((ALL, D), F32), ((ALL, D), BF16),
    ((ALL, HEADS * PATCHES), F32), ((ALL, D), BF16), ((ALL, 128), F32), ((PATCHES, 128), F32), ((8, D), F32),
    ((ALL + 16, D), BF16),
    ((16, D), F32), ((16, D), F32), ((16, D), F32), ((16, D), F32), ((16, D), F32), ((16, D), F32),
    ((HEADS, PATCHES, D), BF16),
]


def encode(x, at):
    rows = x.shape[1]
    top = jnp.max(jnp.abs(x), axis=2, keepdims=True)
    power = jnp.floor(jnp.log2(jnp.maximum(top, 1e-30))) + 1.0
    coded = jnp.floor(x * (CODE_TOP * jnp.exp2(-power)) + 0.5)
    eye = iota((1, rows, 128), 1) == iota((1, rows, 128), 2)
    powers = jnp.sum(jnp.where(eye, power, 0.0), axis=1, keepdims=True)
    coded = jnp.where(iota((1, rows, 128), 1) == at, powers, coded)
    return coded.astype(I32).astype(jnp.int16)


def decode(coded, at):
    rows = coded.shape[1]
    x = coded.astype(I32).astype(F32)
    eye = iota((1, rows, 128), 1) == iota((1, rows, 128), 2)
    power = jnp.sum(jnp.where(eye, x[:, at : at + 1, :], 0.0), axis=2, keepdims=True)
    return x * (jnp.exp2(power) * (1.0 / CODE_TOP))


def prepare(core, pixels, wqkv, wout, half, by_dest, sems):
    rows = pl.ds(pl.multiple_of(core[0] * 128, 128), 128)
    copies = [
        pltpu.make_async_copy(wqkv.at[0, rows, :], half.at[:, 0 : 3 * D], sems.at[0]),
        pltpu.make_async_copy(wout.at[0, rows, :], half.at[:, 3 * D : 4 * D], sems.at[1]),
    ]
    for r in range(SHARE):
        to = by_dest.at[pl.ds(TILES_DEV * r, TILES_DEV)]
        copies.append(pltpu.make_async_copy(pixels, to, sems.at[2 + r]))
    for copy in copies:
        copy.start()
    for copy in copies:
        copy.wait()


def code_pair(keep, given, out):
    out[...] = encode(keep[...] + given[...], 12)


def reduce_tiles(parts, out):
    total = jnp.sum(decode(parts[...], 12), axis=0)
    out[...] = jnp.broadcast_to(total[None], (YS, 16, 128))


def assemble(blocks, out):
    small = jnp.where(iota((8, 128), 0) < 4, blocks[0, 8:16, :], 0.0)
    whole = stack([blocks[y, 0:8, :] for y in range(YS)] + [small])
    out[...] = jnp.broadcast_to(encode(whole[None], 68), (MEMBERS, CHUNK, 128))


def unpack(core, mine, other, loss, d_class, d_gain, d_qkv, d_out, d_head):
    lower = core[0] == 0
    for part in range(4):
        spot = slice(SHARE * part, SHARE * part + SHARE)
        owns, fars = decode(mine[spot], 68), decode(other[spot], 68)
        for b in range(SHARE):
            own, far = owns[b], fars[b]
            blocks = (jnp.where(lower, own, far), jnp.where(lower, far, own))
            for c in range(2):
                for y in range(YS):
                    tile = blocks[c][8 * y : 8 * y + 8]
                    row, lane = tile_at(y, c, b)
                    if part < 3:
                        d_qkv[0, row : row + 8, part * D + lane : part * D + lane + 128] = tile
                    else:
                        d_out[0, row : row + 8, lane : lane + 128] = tile
            at = 4 * part + b
            small = blocks[0]
            d_class[at : at + 1, :128] = small[64:65]
            d_class[at : at + 1, 128:] = small[65:66]
            if b == 0 and part < 3:
                ref = (d_gain, d_head, loss)[part]
                ref[:, :128] = small[66:67]
                ref[:, 128:] = small[67:68]


VM = pl.BlockSpec()
SM = pl.BlockSpec(memory_space=pltpu.SMEM)


def call(body, in_specs, outs, *args, scratch=()):
    return pl.pallas_call(
        body,
        out_shape=[jax.ShapeDtypeStruct(s, t) for s, t in outs],
        in_specs=in_specs,
        out_specs=[VM] * len(outs),
        scratch_shapes=[pltpu.VMEM(s, t) for s, t in scratch],
        compiler_params=pltpu.CompilerParams(vmem_limit_bytes=48 * 1024 * 1024),
    )(*args)


def encodings(date_days):
    band = jnp.arange(D)
    frequency = jnp.exp((band // 2 * 2).astype(F32) * (-math.log(10000.0) / D))
    phases = date_days.astype(F32)[:, :, None] * frequency
    return jnp.where(band % 2 == 0, jnp.sin(phases), jnp.cos(phases)).reshape(TILES_DEV * 16, D)


def swap(v):
    return lax.ppermute(v, "pipe", [(0, 1), (1, 0)])


def whole_step(
    pixels,
    date_days,
    clear_count,
    batch_slot,
    labels,
    class_tokens,
    section_gain,
    wqkv,
    wout,
    head_vec,
):
    first = (lax.axis_index("pipe") == 0).astype(I32)
    inner = lax.axis_index(INNER).astype(I32)
    core = lax.axis_index("core").astype(I32)
    any_space = pl.BlockSpec(memory_space=pl.ANY)
    half, by_dest = pl.pallas_call(
        prepare,
        out_shape=[
            jax.ShapeDtypeStruct((128, 4 * D), BF16),
            jax.ShapeDtypeStruct((MEMBERS, PATCHES, D), BF16),
        ],
        in_specs=[SM, any_space, any_space, any_space],
        out_specs=[any_space] * 2,
        scratch_shapes=[pltpu.SemaphoreType.DMA((6,))],
        name="prepare",
    )(core[None], pixels.reshape(TILES_DEV, PATCHES, D), wqkv, wout)
    whole_tile = lax.all_to_all(by_dest, INNER, 0, 0, tiled=True)
    half = swap(half)
    other_half = lax.ppermute(half, "core", [(0, 1), (1, 0)])
    keep, give = call(
        step,
        [SM] * 3 + [VM] * 11,
        [((OWNERS, 16, 128), F32)] * 2,
        jnp.stack([inner, first, core]),
        clear_count,
        batch_slot,
        labels,
        whole_tile,
        encodings(date_days),
        class_tokens,
        section_gain,
        swap(section_gain),
        wqkv,
        wout,
        half,
        other_half,
        head_vec.reshape(1, D),
        scratch=STEP_SCRATCH,
    )
    given = lax.ppermute(give, "core", [(0, 1), (1, 0)])
    (coded,) = call(code_pair, [VM, VM], [((OWNERS, 16, 128), jnp.int16)], keep, given)
    parts = lax.all_to_all(coded, ("y", "b"), 0, 0, tiled=True)
    (total,) = call(reduce_tiles, [VM], [((YS, 16, 128), F32)], parts)
    blocks = lax.all_to_all(total, "y", 0, 0, tiled=True)
    (whole,) = call(assemble, [VM], [((MEMBERS, CHUNK, 128), jnp.int16)], blocks)
    mine = lax.all_to_all(whole, INNER, 0, 0, tiled=True)
    other = lax.ppermute(mine, "core", [(0, 1), (1, 0)])
    loss, d_class, d_gain, d_qkv, d_out, d_head = call(
        unpack,
        [SM, VM, VM],
        [
            ((1, D), F32),
            ((16, D), F32),
            ((1, D), F32),
            ((1, D, 3 * D), F32),
            ((1, D, D), F32),
            ((1, D), F32),
        ],
        core[None],
        mine,
        other,
    )
    return (loss[0, :MICRO], d_class, d_gain, d_qkv, d_out, d_head.reshape(D))


def solution(mesh):
    cut = Mesh(mesh.devices.reshape(2, YS, 2, TILES_DEV, SHARE), ("pipe",) + DP + INNER)
    placed = (
        P(DP, INNER, None, None),
        P(DP, None),
        P(DP),
        P(DP),
        P(DP, None),
        P(),
        P("pipe", None),
        P("pipe", None, None),
        P("pipe", None, None),
        P(),
    )
    return jax.shard_map(
        whole_step,
        mesh=cut,
        in_specs=placed,
        out_specs=(P(), P(), P("pipe", None), P("pipe", None, None), P("pipe", None, None), P()),
        check_vma=False,
    )
```

```python
import math

import jax
import jax.numpy as jnp
from jax import lax
from jax.experimental import pallas as pl
from jax.experimental.pallas import tpu as pltpu
from jax.sharding import Mesh, PartitionSpec as P


D = 256
HEADS = 8
CLASSES = 16
PATCHES = 48
MICRO = 4
SHARP = 10.0
CAP = 15.0
NORM_EPS = 1e-05
HEAD_EPS = 1e-06
F32 = jnp.float32
BF16 = jnp.bfloat16
I32 = jnp.int32

TILES_DEV = 4
DATES = 16
CHUNKS = 4
SEQS = PATCHES // CHUNKS
CLASS_CHUNK = CLASSES // CHUNKS
ROWS = SEQS * 16
ALL = CHUNKS * ROWS
MEMBERS = 16
SHARE = 4
YS = 8
OWNERS = 32
CODE_TOP = 32000.0
CHUNK = 72
DP = ("y", "core")
INNER = ("r", "b")


def dot(a, b):
    return lax.dot_general(a, b, (((1,), (0,)), ((), ())), preferred_element_type=F32)


def dot_nt(a, b):
    return lax.dot_general(a, b, (((1,), (1,)), ((), ())), preferred_element_type=F32)


def dot_tn(a, b):
    return lax.dot_general(a, b, (((0,), (0,)), ((), ())), preferred_element_type=F32)


def split(x):
    hi = x.astype(BF16)
    return hi, (x - hi.astype(F32)).astype(BF16)


def rounded(x):
    return x.astype(BF16).astype(F32)


def iota(shape, axis):
    return lax.broadcasted_iota(I32, shape, axis)


def head_ones():
    same = (iota((D, D), 0) >> 5) == (iota((D, D), 1) >> 5)
    return jnp.where(same, 1.0, 0.0).astype(BF16)


def head_sums(x, ones):
    hi, lo = split(x)
    return dot(hi, ones) + dot(lo, ones)


def spread(rows_of, masks):
    n = rows_of.shape[0]
    return jnp.concatenate([rows_of * masks[h, 0:n, :] for h in range(HEADS)], axis=0)


def spread_pair(rows_of, masks):
    hi, lo = split(rows_of)
    return spread(hi, masks), spread(lo, masks)


def gathered_heads(wide):
    n = wide.shape[0] // HEADS
    lane_head = iota((n, D), 1) >> 5
    out = wide[:n]
    for h in range(1, HEADS):
        out = jnp.where(lane_head == h, wide[h * n : (h + 1) * n], out)
    return out


def logits_t(k, q, masks):
    n = k.shape[0]
    k_hi, k_lo = split(k)
    q_hi, q_lo = spread_pair(q, masks)
    both = dot_nt(jnp.concatenate([k_hi, k_lo], axis=0), q_hi)
    return SHARP * (both[:n] + both[n:] + dot_nt(k_hi, q_lo))


def three_pass(x_hi, x_lo, w_hi, w_lo):
    n = x_hi.shape[0]
    both = dot(jnp.concatenate([x_hi, x_lo], axis=0), w_hi)
    return both[:n] + both[n:] + dot(x_hi, w_lo)


def three_pass_tn(x_hi, x_lo, y_hi, y_lo):
    return dot_tn(
        jnp.concatenate([x_hi, x_hi, x_lo], axis=0), jnp.concatenate([y_hi, y_lo, y_hi], axis=0)
    )


def stack(parts):
    return jnp.concatenate(parts, axis=0)


def fold(rows):
    return jnp.sum(rows.reshape(-1, 16, D), axis=0)


def chunk_rows(c):
    return pl.ds(pl.multiple_of(c * ROWS, ROWS), ROWS)


def tile_at(y, c, b):
    n = (2 * y + c) * TILES_DEV + b
    return 8 * (n // 2), 128 * (n % 2)


def put_tiles(keep, give, lower, d_w):
    for y in range(YS):
        for b in range(TILES_DEV):
            pair = []
            for c in range(2):
                row, lane = tile_at(y, c, b)
                pair.append(d_w[row : row + 8, lane : lane + 128])
            keep[TILES_DEV * y + b, 0:8, :] = jnp.where(lower, pair[0], pair[1])
            give[TILES_DEV * y + b, 0:8, :] = jnp.where(lower, pair[1], pair[0])


def step(
    scal, counts, slots, labels, pix, enc, cls, gain_a, gain_b, wqkv_a, wqkv_b, wout_a, wout_b, head, keep, give, *scratch
):
    (wt, ws, ot, os, seq_a, seq_b, xhat_t, normed_t, k_t, kn_t, v_t, ad, ac, att_t, q_t, qn_t, e_cls, inv_c,
     u_s, xhat_s, normed_s, inv_s, k_s, kn_s, q_s, qn_s, v_s, a_s, att_s, log_s, tot, rows_s, y_w,
     acc_q, acc_k, acc_v, acc_n, acc_g, d_cls, masks) = scratch
    first = scal[1] == 1
    tile = scal[0] & 3
    share = scal[0] >> 2
    lower = scal[2] == 0
    ones = head_ones()
    lane_head = iota((PATCHES, D), 1) >> 5
    for h in range(HEADS):
        masks[h] = jnp.where(lane_head == h, 1.0, 0.0).astype(BF16)
    wt[...] = jnp.where(first, wqkv_a[0], wqkv_b[0])
    ws[...] = jnp.where(first, wqkv_b[0], wqkv_a[0])
    ot[...] = jnp.where(first, wout_a[0], wout_b[0])
    os[...] = jnp.where(first, wout_b[0], wout_a[0])
    gain_t = jnp.where(first, gain_a[...], gain_b[...])
    gain_s = jnp.where(first, gain_b[...], gain_a[...])
    head_row = head[...]
    h_hi, h_mid = split(head_row)
    h_lo = (head_row - h_hi.astype(F32) - h_mid.astype(F32)).astype(BF16)
    h_rows = stack([h_hi, h_mid, h_lo, jnp.zeros((13, D), BF16)])
    rows_s[...] = jnp.zeros((8, D), F32)
    rows_s[0:1, :] = jnp.sum(dot_nt(h_rows, os[...]), axis=0, keepdims=True)
    rows_s[6:7, :] = gain_t
    rows_s[7:8, :] = gain_s
    for ref in (acc_q, acc_k, acc_v, acc_n, acc_g):
        ref[...] = jnp.zeros((16, D), F32)

    xc = cls[...].astype(F32)
    inv = lax.rsqrt(jnp.mean(xc * xc, axis=-1, keepdims=True) + NORM_EPS)
    xhat_c = xc * inv
    normed_c = (xhat_c * gain_t).astype(BF16)
    qkv_c = dot(normed_c, wt[...])
    kq = stack([qkv_c[:, D : 2 * D], qkv_c[:, :D]])
    kq_inv = lax.rsqrt(head_sums(kq * kq, ones) + HEAD_EPS)
    kq_unit = kq * kq_inv
    xhat_t[ALL:, :] = xhat_c
    normed_t[ALL:, :] = normed_c
    inv_c[...] = jnp.broadcast_to(inv, (16, 128))
    k_t[ALL:, :] = kq_unit[:16]
    kn_t[ALL:, :] = kq_inv[:16]
    q_t[...] = kq_unit[16:]
    qn_t[...] = kq_inv[16:]
    v_t[ALL:, :] = qkv_c[:, 2 * D :].astype(BF16)
    e_cls[...] = jnp.exp(logits_t(kq_unit[:16], kq_unit[16:], masks))

    @pl.loop(0, CHUNKS)
    def _(c):
        rows = chunk_rows(c)
        tile_enc = enc[pl.ds(pl.multiple_of(tile * 16, 16), 16), :]
        pixel = pix[pl.ds(c * 4, 4), :, :].astype(F32).reshape(SEQS, 16, D)
        x = (pixel + tile_enc[None]).reshape(ROWS, D)
        inv = lax.rsqrt(jnp.mean(x * x, axis=-1, keepdims=True) + NORM_EPS)
        xhat = x * inv
        normed = (xhat * rows_s[6:7, :]).astype(BF16)
        xhat_t[rows, :] = xhat
        normed_t[rows, :] = normed
        kv = dot(normed, wt[:, D:])
        v = kv[:, D:].astype(BF16)
        v_t[rows, :] = v
        k = kv[:, :D]
        k_inv = lax.rsqrt(head_sums(k * k, head_ones()) + HEAD_EPS)
        k = k * k_inv
        k_t[rows, :] = k
        kn_t[rows, :] = k_inv
        raised = jnp.exp(logits_t(k, q_t[...], masks))
        shown = (iota((ROWS, 128), 0) & 15) < counts[tile]
        e_dates = jnp.where(shown, raised, 0.0).reshape(SEQS, DATES, 128)
        e_class = e_cls[...]
        total = jnp.sum(e_dates, axis=1, keepdims=True) + jnp.sum(e_class, axis=0, keepdims=True)[None]
        total_inv = 1.0 / total
        a_dates = e_dates * total_inv
        a_class = e_class[None] * total_inv
        ad[rows, :] = a_dates.reshape(ROWS, 128)
        ac[rows, :] = a_class.reshape(ROWS, 128)
        v_class = v_t[ALL:, :]
        parts = []
        for s in range(SEQS):
            weights = stack([a_class[s], a_dates[s]]).astype(BF16)
            values = stack([v_class, v[s * 16 : s * 16 + 16]])
            parts.append(gathered_heads(dot_tn(weights, values)))
        att = stack(parts).astype(BF16)
        att_t[rows, :] = att
        updated = rounded(stack([cls[...].astype(F32)] * SEQS) + dot(att, ot[...]))
        seq_a[rows, :] = updated[:, :128]
        seq_b[rows, :] = updated[:, 128:]

    for i in range(CLASSES):
        u_s[i * PATCHES : (i + 1) * PATCHES, :128] = seq_a[pl.ds(i, PATCHES, stride=16), :]
        u_s[i * PATCHES : (i + 1) * PATCHES, 128:] = seq_b[pl.ds(i, PATCHES, stride=16), :]

    @pl.loop(0, CHUNKS)
    def _(c):
        rows = chunk_rows(c)
        u = u_s[rows, :]
        inv = lax.rsqrt(jnp.mean(u * u, axis=-1, keepdims=True) + NORM_EPS)
        xhat = u * inv
        normed = (xhat * rows_s[7:8, :]).astype(BF16)
        xhat_s[rows, :] = xhat
        normed_s[rows, :] = normed
        inv_s[rows, :] = jnp.broadcast_to(inv, (ROWS, 128))
        qkv = dot(normed, ws[...])
        v = qkv[:, 2 * D :].astype(BF16)
        kq = stack([qkv[:, D : 2 * D], qkv[:, :D]])
        kq_inv = lax.rsqrt(head_sums(kq * kq, head_ones()) + HEAD_EPS)
        kq_unit = kq * kq_inv
        k, q = kq_unit[:ROWS], kq_unit[ROWS:]
        k_s[rows, :] = k
        q_s[rows, :] = q
        kn_s[rows, :] = kq_inv[:ROWS]
        qn_s[rows, :] = kq_inv[ROWS:]
        v_s[rows, :] = v
        part = [slice(b * PATCHES, b * PATCHES + PATCHES) for b in range(CLASS_CHUNK)]
        raised = jnp.exp(stack([logits_t(k[p], q[p], masks) for p in part]))
        raised = raised.reshape(CLASS_CHUNK, PATCHES, HEADS * PATCHES)
        a = raised * (1.0 / jnp.sum(raised, axis=1, keepdims=True))
        a = a.reshape(ROWS, HEADS * PATCHES)
        a_s[rows, :] = a
        a16 = a.astype(BF16)
        wide = [dot_tn(a16[p], v[p]) for p in part]
        att = stack([gathered_heads(m) for m in wide]).astype(BF16)
        att_s[rows, :] = att
        raw = jnp.sum(u * head[...] + att.astype(F32) * rows_s[0:1, :], axis=-1, keepdims=True)
        log_s[rows, :] = jnp.broadcast_to(CAP * jnp.tanh(raw / CAP), (ROWS, 128))

    tot[...] = jnp.sum(jnp.exp(log_s[...]).reshape(CLASSES, PATCHES, 128), axis=0)

    @pl.loop(0, CHUNKS)
    def _(c):
        rows = chunk_rows(c)
        u = u_s[rows, :]
        xhat = xhat_s[rows, :]
        attf = att_s[rows, :].astype(F32)
        logit = log_s[rows, 0:1]
        total = stack([tot[:, 0:1]] * CLASS_CHUNK)
        eye = iota((PATCHES, PATCHES), 0) == iota((PATCHES, PATCHES), 1)
        label_row = labels[pl.ds(tile, 1), :].astype(F32)
        label = jnp.sum(jnp.where(eye, label_row, 0.0), axis=-1, keepdims=True)
        base = (c * CLASS_CHUNK).astype(F32)
        mine = stack([jnp.where(label == base + b, 1.0, 0.0) for b in range(CLASS_CHUNK)])
        d_logit = (jnp.exp(logit) / total - mine) * (1.0 / 64.0)
        ratio = logit / CAP
        d_raw_logit = d_logit * (1.0 - ratio * ratio)
        ce = jnp.sum(mine * (jnp.log(total) - logit), axis=0, keepdims=True) * (1.0 / 768.0)
        rows_s[5:6, :] += jnp.where(iota((1, D), 1) == slots[tile], ce, 0.0)
        rows_s[1:2, :] += jnp.sum(attf * d_raw_logit, axis=0, keepdims=True)
        rows_s[2:3, :] += jnp.sum(u * d_raw_logit, axis=0, keepdims=True)
        d_att = (d_raw_logit * rows_s[0:1, :]).astype(BF16)
        v = v_s[rows, :]
        k = k_s[rows, :]
        q = q_s[rows, :]
        a_all = a_s[rows, :]
        part = [slice(b * PATCHES, b * PATCHES + PATCHES) for b in range(CLASS_CHUNK)]
        a16 = a_all.astype(BF16)
        da_parts, dv_parts = [], []
        for p in part:
            wide = spread(d_att[p], masks)
            da_parts.append(dot_nt(v[p], wide))
            dv_parts.append(dot(a16[p], wide))
        dv = stack(dv_parts).astype(BF16)
        cube = lambda m: m.reshape(CLASS_CHUNK, PATCHES, HEADS * PATCHES)
        da, a = cube(rounded(stack(da_parts))), cube(a_all)
        ds = (SHARP * a * (da - jnp.sum(da * a, axis=1, keepdims=True))).reshape(ROWS, HEADS * PATCHES)
        d_hi, d_lo = split(ds)
        k_hi, k_lo = split(k)
        dk_parts = [three_pass(d_hi[p], d_lo[p], *spread_pair(q[p], masks)) for p in part]
        wide = [three_pass_tn(d_hi[p], d_lo[p], k_hi[p], k_lo[p]) for p in part]
        dq_parts = [gathered_heads(m) for m in wide]
        unit = stack([k, q])
        scale = stack([kn_s[rows, :], qn_s[rows, :]])
        d_unit = stack(dk_parts + dq_parts)
        d_raw = scale * (d_unit - unit * head_sums(d_unit * unit, head_ones()))
        dk_raw, dq_raw = d_raw[:ROWS], d_raw[ROWS:]
        c_v = rounded(dot_nt(dv, ws[:, 2 * D :]))
        dk16, dq16 = dk_raw.astype(BF16), dq_raw.astype(BF16)
        c_k = rounded(dot_nt(dk16, ws[:, D : 2 * D]))
        c_q = rounded(dot_nt(dq16, ws[:, :D]))
        dn = rounded(rounded(c_v + c_k) + c_q)
        rows_s[4:5, :] += jnp.sum(dn * xhat, axis=0, keepdims=True)
        y_w[rows, :] = jnp.where(share == 0, dq16, jnp.where(share == 1, dk16, dv))
        z = dn * rows_s[7:8, :]
        dx = inv_s[rows, 0:1] * (z - xhat * jnp.mean(z * xhat, axis=-1, keepdims=True))
        u_s[rows, :] = rounded(d_raw_logit * head[...] + dx)

    for i in range(CLASSES):
        seq_a[pl.ds(i, PATCHES, stride=16), :] = u_s[i * PATCHES : (i + 1) * PATCHES, :128]
        seq_b[pl.ds(i, PATCHES, stride=16), :] = u_s[i * PATCHES : (i + 1) * PATCHES, 128:]

    w_row = rows_s[1:2, :]
    w_hi, w_mid = split(w_row)
    w_lo = (w_row - w_hi.astype(F32) - w_mid.astype(F32)).astype(BF16)
    zero = jnp.zeros((12, D), BF16)
    w_rows = stack([w_hi, w_mid, w_lo, zero, zero[:1]])
    d_head = rows_s[2:3, :] + jnp.sum(dot(w_rows, os[...]), axis=0, keepdims=True)

    @pl.when(jnp.logical_and(scal[1] == 0, share < 3))
    def _():
        x = normed_s[...]
        d_w = dot_tn(x, y_w[0:ALL, :])
        put_tiles(keep, give, lower, d_w)

    @pl.when(jnp.logical_and(scal[1] == 0, share == 3))
    def _():
        d_w = dot_tn(stack([w_hi, w_hi, w_mid, w_mid, zero]), stack([h_hi, h_mid, h_hi, h_mid, zero]))
        put_tiles(keep, give, lower, d_w)

    @pl.loop(0, CHUNKS)
    def _(c):
        rows = chunk_rows(c)
        g = jnp.concatenate([seq_a[rows, :], seq_b[rows, :]], axis=1).astype(BF16)
        d_att = dot_nt(g, ot[...]).astype(BF16)
        v = v_t[rows, :]
        v_class = v_t[ALL:, :]
        k = k_t[rows, :]
        k_class = k_t[ALL:, :]
        q = q_t[...]
        a_dates = ad[rows, :]
        a_class = ac[rows, :]
        da_class, da_dates, dv_class, dv_dates = [], [], [], []
        for s in range(SEQS):
            part = slice(s * 16, s * 16 + 16)
            wide = spread(d_att[part], masks)
            values = stack([v_class, v[part]])
            weights = stack([a_class[part], a_dates[part]]).astype(BF16)
            da = rounded(dot_nt(values, wide))
            dv = dot(weights, wide).astype(BF16)
            da_class.append(da[:16])
            da_dates.append(da[16:])
            dv_class.append(dv[:16])
            dv_dates.append(dv[16:])
        cube = lambda m: m.reshape(SEQS, 16, 128)
        da_c, da_d = stack(da_class), stack(da_dates)
        both = jnp.sum(cube(da_c * a_class), axis=1, keepdims=True) + jnp.sum(
            cube(da_d * a_dates), axis=1, keepdims=True
        )
        ds_c = SHARP * cube(a_class) * (cube(da_c) - both)
        ds_d = SHARP * cube(a_dates) * (cube(da_d) - both)
        q_hi, q_lo = spread_pair(q, masks)
        d_hi, d_lo = split(stack([ds_d.reshape(ROWS, 128), ds_c.reshape(ROWS, 128)]))
        dk = three_pass(d_hi, d_lo, q_hi, q_lo)
        k_hi, k_lo = split(k)
        kc_hi, kc_lo = split(k_class)
        dq_parts = []
        for s in range(SEQS):
            at, far = slice(s * 16, s * 16 + 16), slice(ROWS + s * 16, ROWS + s * 16 + 16)
            ds_s = [stack([m[at], m[far]]) for m in (d_hi, d_lo)]
            k_all = [stack([k_hi[at], kc_hi]), stack([k_lo[at], kc_lo])]
            dq_parts.append(gathered_heads(three_pass_tn(*ds_s, *k_all)))
        unit = stack([k] + [k_class] * SEQS + [q] * SEQS)
        scale = stack([kn_t[rows, :]] + [kn_t[ALL:, :]] * SEQS + [qn_t[...]] * SEQS)
        d_unit = stack([dk] + dq_parts)
        d_raw = scale * (d_unit - unit * head_sums(d_unit * unit, head_ones()))
        dk_raw, dq_raw = d_raw[: 2 * ROWS], d_raw[2 * ROWS :]
        dv = stack(dv_dates + dv_class)
        c_v = rounded(dot_nt(dv, wt[:, 2 * D :]))
        dk16 = dk_raw.astype(BF16)
        c_k = rounded(dot_nt(dk16, wt[:, D : 2 * D]))
        c_q = rounded(dot_nt(dq_raw.astype(BF16), wt[:, :D]))
        dn = rounded(c_v + c_k)
        rows_s[3:4, :] += jnp.sum(dn[:ROWS] * xhat_t[rows, :], axis=0, keepdims=True)
        acc_n[...] += fold(rounded(dn[ROWS:] + c_q))
        acc_g[...] += fold(g.astype(F32))
        acc_q[...] += fold(dq_raw)
        acc_k[...] += fold(dk_raw[ROWS:])
        acc_v[...] += fold(dv[ROWS:].astype(F32))
        of_dates = jnp.where(share == 1, dk16[:ROWS], dv[:ROWS])
        y = jnp.where(share == 3, g, jnp.where(share == 0, jnp.zeros_like(g), of_dates))

        @pl.when(first)
        def _():
            y_w[rows, :] = y

    dn_c = acc_n[...]
    xhat_c = xhat_t[ALL:, :]
    z = dn_c * rows_s[6:7, :]
    d_norm = inv_c[:, 0:1] * (z - xhat_c * jnp.mean(z * xhat_c, axis=-1, keepdims=True))
    d_cls[...] = acc_g[...] + d_norm
    gain_grad_t = rows_s[3:4, :] + jnp.sum(dn_c * xhat_c, axis=0, keepdims=True)
    gain_grad = jnp.where(first, gain_grad_t, rows_s[4:5, :])

    @pl.when(jnp.logical_and(first, share < 3))
    def _():
        y = jnp.where(share == 0, acc_q[...], jnp.where(share == 1, acc_k[...], acc_v[...]))
        hi, lo = split(y)
        y_w[ALL:, :] = hi
        d_w = dot_tn(normed_t[...], y_w[...]) + dot_tn(normed_t[ALL:, :], lo)
        put_tiles(keep, give, lower, d_w)

    @pl.when(jnp.logical_and(first, share == 3))
    def _():
        put_tiles(keep, give, lower, dot_tn(att_t[...], y_w[0:ALL, :]))

    misc = jnp.where(share == 0, gain_grad, jnp.where(share == 1, d_head, rows_s[5:6, :]))
    for b in range(SHARE):
        row = d_cls[pl.ds(4 * share + b, 1), :]
        small = stack([row[:, :128], row[:, 128:], misc[:, :128], misc[:, 128:], jnp.zeros((4, 128), F32)])
        for y in range(YS):
            keep[TILES_DEV * y + b, 8:16, :] = small
            give[TILES_DEV * y + b, 8:16, :] = small


STEP_SCRATCH = [
    ((D, 3 * D), BF16), ((D, 3 * D), BF16), ((D, D), BF16), ((D, D), BF16),
    ((ALL, 128), F32), ((ALL, 128), F32), ((ALL + 16, D), F32), ((ALL + 16, D), BF16), ((ALL + 16, D), F32), ((ALL + 16, D), F32),
    ((ALL + 16, D), BF16), ((ALL, 128), F32), ((ALL, 128), F32), ((ALL, D), BF16),
    ((16, D), F32), ((16, D), F32), ((16, 128), F32), ((16, 128), F32),
    ((ALL, D), F32), ((ALL, D), F32), ((ALL, D), BF16), ((ALL, 128), F32),
    ((ALL, D), F32), ((ALL, D), F32), ((ALL, D), F32), ((ALL, D), F32), ((ALL, D), BF16),
    ((ALL, HEADS * PATCHES), F32), ((ALL, D), BF16), ((ALL, 128), F32), ((PATCHES, 128), F32), ((8, D), F32),
    ((ALL + 16, D), BF16),
    ((16, D), F32), ((16, D), F32), ((16, D), F32), ((16, D), F32), ((16, D), F32), ((16, D), F32),
    ((HEADS, PATCHES, D), BF16),
]


def encode(x, at):
    rows = x.shape[1]
    top = jnp.max(jnp.abs(x), axis=2, keepdims=True)
    power = jnp.floor(jnp.log2(jnp.maximum(top, 1e-30))) + 1.0
    coded = jnp.floor(x * (CODE_TOP * jnp.exp2(-power)) + 0.5)
    eye = iota((1, rows, 128), 1) == iota((1, rows, 128), 2)
    powers = jnp.sum(jnp.where(eye, power, 0.0), axis=1, keepdims=True)
    coded = jnp.where(iota((1, rows, 128), 1) == at, powers, coded)
    return coded.astype(I32).astype(jnp.int16)


def decode(coded, at):
    rows = coded.shape[1]
    x = coded.astype(I32).astype(F32)
    eye = iota((1, rows, 128), 1) == iota((1, rows, 128), 2)
    power = jnp.sum(jnp.where(eye, x[:, at : at + 1, :], 0.0), axis=2, keepdims=True)
    return x * (jnp.exp2(power) * (1.0 / CODE_TOP))


def code_pair(keep, given, out):
    out[...] = encode(keep[...] + given[...], 12)


def reduce_tiles(parts, out):
    total = jnp.sum(decode(parts[...], 12), axis=0)
    out[...] = jnp.broadcast_to(total[None], (YS, 16, 128))


def assemble(blocks, out):
    small = jnp.where(iota((8, 128), 0) < 4, blocks[0, 8:16, :], 0.0)
    whole = stack([blocks[y, 0:8, :] for y in range(YS)] + [small])
    out[...] = jnp.broadcast_to(encode(whole[None], 68), (MEMBERS, CHUNK, 128))


def unpack(core, mine, other, loss, d_class, d_gain, d_qkv, d_out, d_head):
    lower = core[0] == 0
    for part in range(4):
        spot = slice(SHARE * part, SHARE * part + SHARE)
        owns, fars = decode(mine[spot], 68), decode(other[spot], 68)
        for b in range(SHARE):
            own, far = owns[b], fars[b]
            blocks = (jnp.where(lower, own, far), jnp.where(lower, far, own))
            for c in range(2):
                for y in range(YS):
                    tile = blocks[c][8 * y : 8 * y + 8]
                    row, lane = tile_at(y, c, b)
                    if part < 3:
                        d_qkv[0, row : row + 8, part * D + lane : part * D + lane + 128] = tile
                    else:
                        d_out[0, row : row + 8, lane : lane + 128] = tile
            at = 4 * part + b
            small = blocks[0]
            d_class[at : at + 1, :128] = small[64:65]
            d_class[at : at + 1, 128:] = small[65:66]
            if b == 0 and part < 3:
                ref = (d_gain, d_head, loss)[part]
                if part == 2:
                    ref[...] = small[66:67, :MICRO]
                else:
                    ref[:, :128] = small[66:67]
                    ref[:, 128:] = small[67:68]


VM = pl.BlockSpec()
SM = pl.BlockSpec(memory_space=pltpu.SMEM)


def call(body, in_specs, outs, *args, scratch=()):
    return pl.pallas_call(
        body,
        out_shape=[jax.ShapeDtypeStruct(s, t) for s, t in outs],
        in_specs=in_specs,
        out_specs=[VM] * len(outs),
        scratch_shapes=[pltpu.VMEM(s, t) for s, t in scratch],
        compiler_params=pltpu.CompilerParams(vmem_limit_bytes=48 * 1024 * 1024),
    )(*args)


def encodings(date_days):
    band = jnp.arange(D)
    frequency = jnp.exp((band // 2 * 2).astype(F32) * (-math.log(10000.0) / D))
    phases = date_days.astype(F32)[:, :, None] * frequency
    return jnp.where(band % 2 == 0, jnp.sin(phases), jnp.cos(phases)).reshape(TILES_DEV * 16, D)


def swap(v):
    return lax.ppermute(v, "pipe", [(0, 1), (1, 0)])


def whole_step(
    pixels,
    date_days,
    clear_count,
    batch_slot,
    labels,
    class_tokens,
    section_gain,
    wqkv,
    wout,
    head_vec,
):
    first = (lax.axis_index("pipe") == 0).astype(I32)
    inner = lax.axis_index(INNER).astype(I32)
    by_dest = jnp.tile(pixels.reshape(TILES_DEV, PATCHES, D), (SHARE, 1, 1))
    whole_tile = lax.all_to_all(by_dest, INNER, 0, 0, tiled=True)
    core = lax.axis_index("core").astype(I32)
    keep, give = call(
        step,
        [SM] * 3 + [VM] * 11,
        [((OWNERS, 16, 128), F32)] * 2,
        jnp.stack([inner, first, core]),
        clear_count,
        batch_slot,
        labels,
        whole_tile,
        encodings(date_days),
        class_tokens,
        section_gain,
        swap(section_gain),
        wqkv,
        swap(wqkv),
        wout,
        swap(wout),
        head_vec.reshape(1, D),
        scratch=STEP_SCRATCH,
    )
    given = lax.ppermute(give, "core", [(0, 1), (1, 0)])
    (coded,) = call(code_pair, [VM, VM], [((OWNERS, 16, 128), jnp.int16)], keep, given)
    parts = lax.all_to_all(coded, ("y", "b"), 0, 0, tiled=True)
    (total,) = call(reduce_tiles, [VM], [((YS, 16, 128), F32)], parts)
    blocks = lax.all_to_all(total, "y", 0, 0, tiled=True)
    (whole,) = call(assemble, [VM], [((MEMBERS, CHUNK, 128), jnp.int16)], blocks)
    mine = lax.all_to_all(whole, INNER, 0, 0, tiled=True)
    other = lax.ppermute(mine, "core", [(0, 1), (1, 0)])
    loss, d_class, d_gain, d_qkv, d_out, d_head = call(
        unpack,
        [SM, VM, VM],
        [
            ((1, MICRO), F32),
            ((16, D), F32),
            ((1, D), F32),
            ((1, D, 3 * D), F32),
            ((1, D, D), F32),
            ((1, D), F32),
        ],
        core[None],
        mine,
        other,
    )
    return (loss.reshape(MICRO), d_class, d_gain, d_qkv, d_out, d_head.reshape(D))


def solution(mesh):
    cut = Mesh(mesh.devices.reshape(2, YS, 2, TILES_DEV, SHARE), ("pipe",) + DP + INNER)
    placed = (
        P(DP, INNER, None, None),
        P(DP, None),
        P(DP),
        P(DP),
        P(DP, None),
        P(),
        P("pipe", None),
        P("pipe", None, None),
        P("pipe", None, None),
        P(),
    )
    return jax.shard_map(
        whole_step,
        mesh=cut,
        in_specs=placed,
        out_specs=(P(), P(), P("pipe", None), P("pipe", None, None), P("pipe", None, None), P()),
        check_vma=False,
    )
```

```python
import math

import jax
import jax.numpy as jnp
from jax import lax
from jax.experimental import pallas as pl
from jax.experimental.pallas import tpu as pltpu
from jax.sharding import Mesh, PartitionSpec as P


D = 256
HEADS = 8
CLASSES = 16
PATCHES = 48
MICRO = 4
SHARP = 10.0
CAP = 15.0
NORM_EPS = 1e-05
HEAD_EPS = 1e-06
F32 = jnp.float32
BF16 = jnp.bfloat16
I32 = jnp.int32

TILES_DEV = 4
DATES = 16
CHUNKS = 4
SEQS = PATCHES // CHUNKS
CLASS_CHUNK = CLASSES // CHUNKS
ROWS = SEQS * 16
ALL = CHUNKS * ROWS
MEMBERS = 16
SHARE = 4
YS = 8
OWNERS = 32
CODE_TOP = 32000.0
CHUNK = 72
DP = ("y", "core")
INNER = ("r", "b")


def dot(a, b):
    return lax.dot_general(a, b, (((1,), (0,)), ((), ())), preferred_element_type=F32)


def dot_nt(a, b):
    return lax.dot_general(a, b, (((1,), (1,)), ((), ())), preferred_element_type=F32)


def dot_tn(a, b):
    return lax.dot_general(a, b, (((0,), (0,)), ((), ())), preferred_element_type=F32)


def split(x):
    hi = x.astype(BF16)
    return hi, (x - hi.astype(F32)).astype(BF16)


def rounded(x):
    return x.astype(BF16).astype(F32)


def iota(shape, axis):
    return lax.broadcasted_iota(I32, shape, axis)


def head_ones():
    same = (iota((D, D), 0) >> 5) == (iota((D, D), 1) >> 5)
    return jnp.where(same, 1.0, 0.0).astype(BF16)


def head_sums(x, ones):
    hi, lo = split(x)
    return dot(hi, ones) + dot(lo, ones)


def spread(rows_of, masks):
    n = rows_of.shape[0]
    return jnp.concatenate([rows_of * masks[h, 0:n, :] for h in range(HEADS)], axis=0)


def spread_pair(rows_of, masks):
    hi, lo = split(rows_of)
    return spread(hi, masks), spread(lo, masks)


def gathered_heads(wide):
    n = wide.shape[0] // HEADS
    lane_head = iota((n, D), 1) >> 5
    out = wide[:n]
    for h in range(1, HEADS):
        out = jnp.where(lane_head == h, wide[h * n : (h + 1) * n], out)
    return out


def logits_t(k, q, masks):
    n = k.shape[0]
    k_hi, k_lo = split(k)
    q_hi, q_lo = spread_pair(q, masks)
    both = dot_nt(jnp.concatenate([k_hi, k_lo], axis=0), q_hi)
    return SHARP * (both[:n] + both[n:] + dot_nt(k_hi, q_lo))


def three_pass(x_hi, x_lo, w_hi, w_lo):
    n = x_hi.shape[0]
    both = dot(jnp.concatenate([x_hi, x_lo], axis=0), w_hi)
    return both[:n] + both[n:] + dot(x_hi, w_lo)


def three_pass_tn(x_hi, x_lo, y_hi, y_lo):
    return dot_tn(
        jnp.concatenate([x_hi, x_hi, x_lo], axis=0), jnp.concatenate([y_hi, y_lo, y_hi], axis=0)
    )


def stack(parts):
    return jnp.concatenate(parts, axis=0)


def fold(rows):
    return jnp.sum(rows.reshape(-1, 16, D), axis=0)


def chunk_rows(c):
    return pl.ds(pl.multiple_of(c * ROWS, ROWS), ROWS)


def tile_at(y, c, b):
    n = (2 * y + c) * TILES_DEV + b
    return 8 * (n // 2), 128 * (n % 2)


def put_tiles(keep, give, lower, d_w):
    for y in range(YS):
        for b in range(TILES_DEV):
            pair = []
            for c in range(2):
                row, lane = tile_at(y, c, b)
                pair.append(d_w[row : row + 8, lane : lane + 128])
            keep[TILES_DEV * y + b, 0:8, :] = jnp.where(lower, pair[0], pair[1])
            give[TILES_DEV * y + b, 0:8, :] = jnp.where(lower, pair[1], pair[0])


def step(
    scal, counts, slots, labels, pix, enc, cls, gain_a, gain_b, wqkv_a, wqkv_b, wout_a, wout_b, head, keep, give, *scratch
):
    (wt, ws, ot, os, seq_a, seq_b, xhat_t, normed_t, k_t, kn_t, v_t, ad, ac, att_t, q_t, qn_t, e_cls, inv_c,
     u_s, xhat_s, normed_s, inv_s, k_s, kn_s, q_s, qn_s, v_s, a_s, att_s, log_s, tot, rows_s, y_w,
     acc_q, acc_k, acc_v, acc_n, acc_g, d_cls, masks) = scratch
    first = scal[1] == 1
    tile = scal[0] & 3
    share = scal[0] >> 2
    lower = scal[2] == 0
    ones = head_ones()
    lane_head = iota((PATCHES, D), 1) >> 5
    for h in range(HEADS):
        masks[h] = jnp.where(lane_head == h, 1.0, 0.0).astype(BF16)
    wt[...] = jnp.where(first, wqkv_a[0], wqkv_b[0])
    ws[...] = jnp.where(first, wqkv_b[0], wqkv_a[0])
    ot[...] = jnp.where(first, wout_a[0], wout_b[0])
    os[...] = jnp.where(first, wout_b[0], wout_a[0])
    gain_t = jnp.where(first, gain_a[...], gain_b[...])
    gain_s = jnp.where(first, gain_b[...], gain_a[...])
    head_row = head[...]
    h_hi, h_mid = split(head_row)
    h_lo = (head_row - h_hi.astype(F32) - h_mid.astype(F32)).astype(BF16)
    h_rows = stack([h_hi, h_mid, h_lo, jnp.zeros((13, D), BF16)])
    rows_s[...] = jnp.zeros((8, D), F32)
    rows_s[0:1, :] = jnp.sum(dot_nt(h_rows, os[...]), axis=0, keepdims=True)
    rows_s[6:7, :] = gain_t
    rows_s[7:8, :] = gain_s
    for ref in (acc_q, acc_k, acc_v, acc_n, acc_g):
        ref[...] = jnp.zeros((16, D), F32)

    xc = cls[...].astype(F32)
    inv = lax.rsqrt(jnp.mean(xc * xc, axis=-1, keepdims=True) + NORM_EPS)
    xhat_c = xc * inv
    normed_c = (xhat_c * gain_t).astype(BF16)
    qkv_c = dot(normed_c, wt[...])
    kq = stack([qkv_c[:, D : 2 * D], qkv_c[:, :D]])
    kq_inv = lax.rsqrt(head_sums(kq * kq, ones) + HEAD_EPS)
    kq_unit = kq * kq_inv
    xhat_t[ALL:, :] = xhat_c
    normed_t[ALL:, :] = normed_c
    inv_c[...] = jnp.broadcast_to(inv, (16, 128))
    k_t[ALL:, :] = kq_unit[:16]
    kn_t[ALL:, :] = kq_inv[:16]
    q_t[...] = kq_unit[16:]
    qn_t[...] = kq_inv[16:]
    v_t[ALL:, :] = qkv_c[:, 2 * D :].astype(BF16)
    e_cls[...] = jnp.exp(logits_t(kq_unit[:16], kq_unit[16:], masks))

    @pl.loop(0, CHUNKS)
    def _(c):
        rows = chunk_rows(c)
        tile_enc = enc[pl.ds(pl.multiple_of(tile * 16, 16), 16), :]
        pixel = pix[pl.ds(c * 4, 4), :, :].astype(F32).reshape(SEQS, 16, D)
        x = (pixel + tile_enc[None]).reshape(ROWS, D)
        inv = lax.rsqrt(jnp.mean(x * x, axis=-1, keepdims=True) + NORM_EPS)
        xhat = x * inv
        normed = (xhat * rows_s[6:7, :]).astype(BF16)
        xhat_t[rows, :] = xhat
        normed_t[rows, :] = normed
        kv = dot(normed, wt[:, D:])
        v = kv[:, D:].astype(BF16)
        v_t[rows, :] = v
        k = kv[:, :D]
        k_inv = lax.rsqrt(head_sums(k * k, head_ones()) + HEAD_EPS)
        k = k * k_inv
        k_t[rows, :] = k
        kn_t[rows, :] = k_inv
        raised = jnp.exp(logits_t(k, q_t[...], masks))
        shown = (iota((ROWS, 128), 0) & 15) < counts[tile]
        e_dates = jnp.where(shown, raised, 0.0).reshape(SEQS, DATES, 128)
        e_class = e_cls[...]
        total = jnp.sum(e_dates, axis=1, keepdims=True) + jnp.sum(e_class, axis=0, keepdims=True)[None]
        total_inv = 1.0 / total
        a_dates = e_dates * total_inv
        a_class = e_class[None] * total_inv
        ad[rows, :] = a_dates.reshape(ROWS, 128)
        ac[rows, :] = a_class.reshape(ROWS, 128)
        v_class = v_t[ALL:, :]
        parts = []
        for s in range(SEQS):
            weights = stack([a_class[s], a_dates[s]]).astype(BF16)
            values = stack([v_class, v[s * 16 : s * 16 + 16]])
            parts.append(gathered_heads(dot_tn(weights, values)))
        att = stack(parts).astype(BF16)
        att_t[rows, :] = att
        updated = rounded(stack([cls[...].astype(F32)] * SEQS) + dot(att, ot[...]))
        seq_a[rows, :] = updated[:, :128]
        seq_b[rows, :] = updated[:, 128:]

    for i in range(CLASSES):
        u_s[i * PATCHES : (i + 1) * PATCHES, :128] = seq_a[pl.ds(i, PATCHES, stride=16), :]
        u_s[i * PATCHES : (i + 1) * PATCHES, 128:] = seq_b[pl.ds(i, PATCHES, stride=16), :]

    @pl.loop(0, CHUNKS)
    def _(c):
        rows = chunk_rows(c)
        u = u_s[rows, :]
        inv = lax.rsqrt(jnp.mean(u * u, axis=-1, keepdims=True) + NORM_EPS)
        xhat = u * inv
        normed = (xhat * rows_s[7:8, :]).astype(BF16)
        xhat_s[rows, :] = xhat
        normed_s[rows, :] = normed
        inv_s[rows, :] = jnp.broadcast_to(inv, (ROWS, 128))
        qkv = dot(normed, ws[...])
        v = qkv[:, 2 * D :].astype(BF16)
        kq = stack([qkv[:, D : 2 * D], qkv[:, :D]])
        kq_inv = lax.rsqrt(head_sums(kq * kq, head_ones()) + HEAD_EPS)
        kq_unit = kq * kq_inv
        k, q = kq_unit[:ROWS], kq_unit[ROWS:]
        k_s[rows, :] = k
        q_s[rows, :] = q
        kn_s[rows, :] = kq_inv[:ROWS]
        qn_s[rows, :] = kq_inv[ROWS:]
        v_s[rows, :] = v
        part = [slice(b * PATCHES, b * PATCHES + PATCHES) for b in range(CLASS_CHUNK)]
        raised = jnp.exp(stack([logits_t(k[p], q[p], masks) for p in part]))
        raised = raised.reshape(CLASS_CHUNK, PATCHES, HEADS * PATCHES)
        a = raised * (1.0 / jnp.sum(raised, axis=1, keepdims=True))
        a = a.reshape(ROWS, HEADS * PATCHES)
        a_s[rows, :] = a
        a16 = a.astype(BF16)
        wide = [dot_tn(a16[p], v[p]) for p in part]
        att = stack([gathered_heads(m) for m in wide]).astype(BF16)
        att_s[rows, :] = att
        raw = jnp.sum(u * head[...] + att.astype(F32) * rows_s[0:1, :], axis=-1, keepdims=True)
        log_s[rows, :] = jnp.broadcast_to(CAP * jnp.tanh(raw / CAP), (ROWS, 128))

    tot[...] = jnp.sum(jnp.exp(log_s[...]).reshape(CLASSES, PATCHES, 128), axis=0)

    @pl.loop(0, CHUNKS)
    def _(c):
        rows = chunk_rows(c)
        u = u_s[rows, :]
        xhat = xhat_s[rows, :]
        attf = att_s[rows, :].astype(F32)
        logit = log_s[rows, 0:1]
        total = stack([tot[:, 0:1]] * CLASS_CHUNK)
        eye = iota((PATCHES, PATCHES), 0) == iota((PATCHES, PATCHES), 1)
        label_row = labels[pl.ds(tile, 1), :].astype(F32)
        label = jnp.sum(jnp.where(eye, label_row, 0.0), axis=-1, keepdims=True)
        base = (c * CLASS_CHUNK).astype(F32)
        mine = stack([jnp.where(label == base + b, 1.0, 0.0) for b in range(CLASS_CHUNK)])
        d_logit = (jnp.exp(logit) / total - mine) * (1.0 / 64.0)
        ratio = logit / CAP
        d_raw_logit = d_logit * (1.0 - ratio * ratio)
        ce = jnp.sum(mine * (jnp.log(total) - logit), axis=0, keepdims=True) * (1.0 / 768.0)
        rows_s[5:6, :] += jnp.where(iota((1, D), 1) == slots[tile], ce, 0.0)
        rows_s[1:2, :] += jnp.sum(attf * d_raw_logit, axis=0, keepdims=True)
        rows_s[2:3, :] += jnp.sum(u * d_raw_logit, axis=0, keepdims=True)
        d_att = (d_raw_logit * rows_s[0:1, :]).astype(BF16)
        v = v_s[rows, :]
        k = k_s[rows, :]
        q = q_s[rows, :]
        a_all = a_s[rows, :]
        part = [slice(b * PATCHES, b * PATCHES + PATCHES) for b in range(CLASS_CHUNK)]
        a16 = a_all.astype(BF16)
        da_parts, dv_parts = [], []
        for p in part:
            wide = spread(d_att[p], masks)
            da_parts.append(dot_nt(v[p], wide))
            dv_parts.append(dot(a16[p], wide))
        dv = stack(dv_parts).astype(BF16)
        cube = lambda m: m.reshape(CLASS_CHUNK, PATCHES, HEADS * PATCHES)
        da, a = cube(rounded(stack(da_parts))), cube(a_all)
        ds = (SHARP * a * (da - jnp.sum(da * a, axis=1, keepdims=True))).reshape(ROWS, HEADS * PATCHES)
        d_hi, d_lo = split(ds)
        k_hi, k_lo = split(k)
        dk_parts = [three_pass(d_hi[p], d_lo[p], *spread_pair(q[p], masks)) for p in part]
        wide = [three_pass_tn(d_hi[p], d_lo[p], k_hi[p], k_lo[p]) for p in part]
        dq_parts = [gathered_heads(m) for m in wide]
        unit = stack([k, q])
        scale = stack([kn_s[rows, :], qn_s[rows, :]])
        d_unit = stack(dk_parts + dq_parts)
        d_raw = scale * (d_unit - unit * head_sums(d_unit * unit, head_ones()))
        dk_raw, dq_raw = d_raw[:ROWS], d_raw[ROWS:]
        c_v = rounded(dot_nt(dv, ws[:, 2 * D :]))
        dk16, dq16 = dk_raw.astype(BF16), dq_raw.astype(BF16)
        c_k = rounded(dot_nt(dk16, ws[:, D : 2 * D]))
        c_q = rounded(dot_nt(dq16, ws[:, :D]))
        dn = rounded(rounded(c_v + c_k) + c_q)
        rows_s[4:5, :] += jnp.sum(dn * xhat, axis=0, keepdims=True)
        y_w[rows, :] = jnp.where(share == 0, dq16, jnp.where(share == 1, dk16, dv))
        z = dn * rows_s[7:8, :]
        dx = inv_s[rows, 0:1] * (z - xhat * jnp.mean(z * xhat, axis=-1, keepdims=True))
        u_s[rows, :] = rounded(d_raw_logit * head[...] + dx)

    for i in range(CLASSES):
        seq_a[pl.ds(i, PATCHES, stride=16), :] = u_s[i * PATCHES : (i + 1) * PATCHES, :128]
        seq_b[pl.ds(i, PATCHES, stride=16), :] = u_s[i * PATCHES : (i + 1) * PATCHES, 128:]

    w_row = rows_s[1:2, :]
    w_hi, w_mid = split(w_row)
    w_lo = (w_row - w_hi.astype(F32) - w_mid.astype(F32)).astype(BF16)
    zero = jnp.zeros((12, D), BF16)
    w_rows = stack([w_hi, w_mid, w_lo, zero, zero[:1]])
    d_head = rows_s[2:3, :] + jnp.sum(dot(w_rows, os[...]), axis=0, keepdims=True)

    @pl.when(jnp.logical_and(scal[1] == 0, share < 3))
    def _():
        x = normed_s[...]
        d_w = dot_tn(x, y_w[0:ALL, :])
        put_tiles(keep, give, lower, d_w)

    @pl.when(jnp.logical_and(scal[1] == 0, share == 3))
    def _():
        d_w = dot_tn(stack([w_hi, w_hi, w_mid, w_mid, zero]), stack([h_hi, h_mid, h_hi, h_mid, zero]))
        put_tiles(keep, give, lower, d_w)

    @pl.loop(0, CHUNKS)
    def _(c):
        rows = chunk_rows(c)
        g = jnp.concatenate([seq_a[rows, :], seq_b[rows, :]], axis=1).astype(BF16)
        d_att = dot_nt(g, ot[...]).astype(BF16)
        v = v_t[rows, :]
        v_class = v_t[ALL:, :]
        k = k_t[rows, :]
        k_class = k_t[ALL:, :]
        q = q_t[...]
        a_dates = ad[rows, :]
        a_class = ac[rows, :]
        da_class, da_dates, dv_class, dv_dates = [], [], [], []
        for s in range(SEQS):
            part = slice(s * 16, s * 16 + 16)
            wide = spread(d_att[part], masks)
            values = stack([v_class, v[part]])
            weights = stack([a_class[part], a_dates[part]]).astype(BF16)
            da = rounded(dot_nt(values, wide))
            dv = dot(weights, wide).astype(BF16)
            da_class.append(da[:16])
            da_dates.append(da[16:])
            dv_class.append(dv[:16])
            dv_dates.append(dv[16:])
        cube = lambda m: m.reshape(SEQS, 16, 128)
        da_c, da_d = stack(da_class), stack(da_dates)
        both = jnp.sum(cube(da_c * a_class), axis=1, keepdims=True) + jnp.sum(
            cube(da_d * a_dates), axis=1, keepdims=True
        )
        ds_c = SHARP * cube(a_class) * (cube(da_c) - both)
        ds_d = SHARP * cube(a_dates) * (cube(da_d) - both)
        q_hi, q_lo = spread_pair(q, masks)
        d_hi, d_lo = split(stack([ds_d.reshape(ROWS, 128), ds_c.reshape(ROWS, 128)]))
        dk = three_pass(d_hi, d_lo, q_hi, q_lo)
        k_hi, k_lo = split(k)
        kc_hi, kc_lo = split(k_class)
        dq_parts = []
        for s in range(SEQS):
            at, far = slice(s * 16, s * 16 + 16), slice(ROWS + s * 16, ROWS + s * 16 + 16)
            ds_s = [stack([m[at], m[far]]) for m in (d_hi, d_lo)]
            k_all = [stack([k_hi[at], kc_hi]), stack([k_lo[at], kc_lo])]
            dq_parts.append(gathered_heads(three_pass_tn(*ds_s, *k_all)))
        unit = stack([k] + [k_class] * SEQS + [q] * SEQS)
        scale = stack([kn_t[rows, :]] + [kn_t[ALL:, :]] * SEQS + [qn_t[...]] * SEQS)
        d_unit = stack([dk] + dq_parts)
        d_raw = scale * (d_unit - unit * head_sums(d_unit * unit, head_ones()))
        dk_raw, dq_raw = d_raw[: 2 * ROWS], d_raw[2 * ROWS :]
        dv = stack(dv_dates + dv_class)
        c_v = rounded(dot_nt(dv, wt[:, 2 * D :]))
        dk16 = dk_raw.astype(BF16)
        c_k = rounded(dot_nt(dk16, wt[:, D : 2 * D]))
        c_q = rounded(dot_nt(dq_raw.astype(BF16), wt[:, :D]))
        dn = rounded(c_v + c_k)
        rows_s[3:4, :] += jnp.sum(dn[:ROWS] * xhat_t[rows, :], axis=0, keepdims=True)
        acc_n[...] += fold(rounded(dn[ROWS:] + c_q))
        acc_g[...] += fold(g.astype(F32))
        acc_q[...] += fold(dq_raw)
        acc_k[...] += fold(dk_raw[ROWS:])
        acc_v[...] += fold(dv[ROWS:].astype(F32))
        of_dates = jnp.where(share == 1, dk16[:ROWS], dv[:ROWS])
        y = jnp.where(share == 3, g, jnp.where(share == 0, jnp.zeros_like(g), of_dates))

        @pl.when(first)
        def _():
            y_w[rows, :] = y

    dn_c = acc_n[...]
    xhat_c = xhat_t[ALL:, :]
    z = dn_c * rows_s[6:7, :]
    d_norm = inv_c[:, 0:1] * (z - xhat_c * jnp.mean(z * xhat_c, axis=-1, keepdims=True))
    d_cls[...] = acc_g[...] + d_norm
    gain_grad_t = rows_s[3:4, :] + jnp.sum(dn_c * xhat_c, axis=0, keepdims=True)
    gain_grad = jnp.where(first, gain_grad_t, rows_s[4:5, :])

    @pl.when(jnp.logical_and(first, share < 3))
    def _():
        y = jnp.where(share == 0, acc_q[...], jnp.where(share == 1, acc_k[...], acc_v[...]))
        hi, lo = split(y)
        y_w[ALL:, :] = hi
        d_w = dot_tn(normed_t[...], y_w[...]) + dot_tn(normed_t[ALL:, :], lo)
        put_tiles(keep, give, lower, d_w)

    @pl.when(jnp.logical_and(first, share == 3))
    def _():
        put_tiles(keep, give, lower, dot_tn(att_t[...], y_w[0:ALL, :]))

    misc = jnp.where(share == 0, gain_grad, jnp.where(share == 1, d_head, rows_s[5:6, :]))
    for b in range(SHARE):
        row = d_cls[pl.ds(4 * share + b, 1), :]
        small = stack([row[:, :128], row[:, 128:], misc[:, :128], misc[:, 128:], jnp.zeros((4, 128), F32)])
        for y in range(YS):
            keep[TILES_DEV * y + b, 8:16, :] = small
            give[TILES_DEV * y + b, 8:16, :] = small


STEP_SCRATCH = [
    ((D, 3 * D), BF16), ((D, 3 * D), BF16), ((D, D), BF16), ((D, D), BF16),
    ((ALL, 128), F32), ((ALL, 128), F32), ((ALL + 16, D), F32), ((ALL + 16, D), BF16), ((ALL + 16, D), F32), ((ALL + 16, D), F32),
    ((ALL + 16, D), BF16), ((ALL, 128), F32), ((ALL, 128), F32), ((ALL, D), BF16),
    ((16, D), F32), ((16, D), F32), ((16, 128), F32), ((16, 128), F32),
    ((ALL, D), F32), ((ALL, D), F32), ((ALL, D), BF16), ((ALL, 128), F32),
    ((ALL, D), F32), ((ALL, D), F32), ((ALL, D), F32), ((ALL, D), F32), ((ALL, D), BF16),
    ((ALL, HEADS * PATCHES), F32), ((ALL, D), BF16), ((ALL, 128), F32), ((PATCHES, 128), F32), ((8, D), F32),
    ((ALL + 16, D), BF16),
    ((16, D), F32), ((16, D), F32), ((16, D), F32), ((16, D), F32), ((16, D), F32), ((16, D), F32),
    ((HEADS, PATCHES, D), BF16),
]


def encode(x, at):
    rows = x.shape[1]
    top = jnp.max(jnp.abs(x), axis=2, keepdims=True)
    power = jnp.floor(jnp.log2(jnp.maximum(top, 1e-30))) + 1.0
    coded = jnp.floor(x * (CODE_TOP * jnp.exp2(-power)) + 0.5)
    eye = iota((1, rows, 128), 1) == iota((1, rows, 128), 2)
    powers = jnp.sum(jnp.where(eye, power, 0.0), axis=1, keepdims=True)
    coded = jnp.where(iota((1, rows, 128), 1) == at, powers, coded)
    return coded.astype(I32).astype(jnp.int16)


def decode(coded, at):
    rows = coded.shape[1]
    x = coded.astype(I32).astype(F32)
    eye = iota((1, rows, 128), 1) == iota((1, rows, 128), 2)
    power = jnp.sum(jnp.where(eye, x[:, at : at + 1, :], 0.0), axis=2, keepdims=True)
    return x * (jnp.exp2(power) * (1.0 / CODE_TOP))


def code_pair(keep, given, out):
    x = keep[...] + given[...]
    spare = iota((8, 128), 0) < 4
    chunks = []
    for b in range(TILES_DEV):
        tiles = [x[TILES_DEV * y + b, 0:8, :] for y in range(YS)]
        chunks.append(stack(tiles + [jnp.where(spare, x[b, 8:16, :], 0.0)])[None])
    coded = encode(jnp.concatenate(chunks, axis=0), 68)
    for y in range(YS):
        out[TILES_DEV * y : TILES_DEV * y + TILES_DEV] = coded


def merge(parts, out):
    total = jnp.sum(decode(parts[...], 68), axis=0)
    out[...] = jnp.broadcast_to(encode(total[None], 68), (MEMBERS, CHUNK, 128))


def unpack(core, mine, other, loss, d_class, d_gain, d_qkv, d_out, d_head):
    lower = core[0] == 0
    for part in range(4):
        spot = slice(SHARE * part, SHARE * part + SHARE)
        owns, fars = decode(mine[spot], 68), decode(other[spot], 68)
        for b in range(SHARE):
            own, far = owns[b], fars[b]
            blocks = (jnp.where(lower, own, far), jnp.where(lower, far, own))
            for c in range(2):
                for y in range(YS):
                    tile = blocks[c][8 * y : 8 * y + 8]
                    row, lane = tile_at(y, c, b)
                    if part < 3:
                        d_qkv[0, row : row + 8, part * D + lane : part * D + lane + 128] = tile
                    else:
                        d_out[0, row : row + 8, lane : lane + 128] = tile
            at = 4 * part + b
            small = blocks[0]
            d_class[at : at + 1, :128] = small[64:65]
            d_class[at : at + 1, 128:] = small[65:66]
            if b == 0 and part < 3:
                ref = (d_gain, d_head, loss)[part]
                if part == 2:
                    ref[...] = small[66:67, :MICRO]
                else:
                    ref[:, :128] = small[66:67]
                    ref[:, 128:] = small[67:68]


VM = pl.BlockSpec()
SM = pl.BlockSpec(memory_space=pltpu.SMEM)


def call(body, in_specs, outs, *args, scratch=()):
    return pl.pallas_call(
        body,
        out_shape=[jax.ShapeDtypeStruct(s, t) for s, t in outs],
        in_specs=in_specs,
        out_specs=[VM] * len(outs),
        scratch_shapes=[pltpu.VMEM(s, t) for s, t in scratch],
        compiler_params=pltpu.CompilerParams(vmem_limit_bytes=48 * 1024 * 1024),
    )(*args)


def encodings(date_days):
    band = jnp.arange(D)
    frequency = jnp.exp((band // 2 * 2).astype(F32) * (-math.log(10000.0) / D))
    phases = date_days.astype(F32)[:, :, None] * frequency
    return jnp.where(band % 2 == 0, jnp.sin(phases), jnp.cos(phases)).reshape(TILES_DEV * 16, D)


def swap(v):
    return lax.ppermute(v, "pipe", [(0, 1), (1, 0)])


def whole_step(
    pixels,
    date_days,
    clear_count,
    batch_slot,
    labels,
    class_tokens,
    section_gain,
    wqkv,
    wout,
    head_vec,
):
    first = (lax.axis_index("pipe") == 0).astype(I32)
    inner = lax.axis_index(INNER).astype(I32)
    by_dest = jnp.tile(pixels.reshape(TILES_DEV, PATCHES, D), (SHARE, 1, 1))
    whole_tile = lax.all_to_all(by_dest, INNER, 0, 0, tiled=True)
    core = lax.axis_index("core").astype(I32)
    keep, give = call(
        step,
        [SM] * 3 + [VM] * 11,
        [((OWNERS, 16, 128), F32)] * 2,
        jnp.stack([inner, first, core]),
        clear_count,
        batch_slot,
        labels,
        whole_tile,
        encodings(date_days),
        class_tokens,
        section_gain,
        swap(section_gain),
        wqkv,
        swap(wqkv),
        wout,
        swap(wout),
        head_vec.reshape(1, D),
        scratch=STEP_SCRATCH,
    )
    given = lax.ppermute(give, "core", [(0, 1), (1, 0)])
    (coded,) = call(code_pair, [VM, VM], [((OWNERS, CHUNK, 128), jnp.int16)], keep, given)
    parts = lax.all_to_all(coded, ("y", "b"), 0, 0, tiled=True)
    (whole,) = call(merge, [VM], [((MEMBERS, CHUNK, 128), jnp.int16)], parts)
    mine = lax.all_to_all(whole, INNER, 0, 0, tiled=True)
    other = lax.ppermute(mine, "core", [(0, 1), (1, 0)])
    loss, d_class, d_gain, d_qkv, d_out, d_head = call(
        unpack,
        [SM, VM, VM],
        [
            ((1, MICRO), F32),
            ((16, D), F32),
            ((1, D), F32),
            ((1, D, 3 * D), F32),
            ((1, D, D), F32),
            ((1, D), F32),
        ],
        core[None],
        mine,
        other,
    )
    return (loss.reshape(MICRO), d_class, d_gain, d_qkv, d_out, d_head.reshape(D))


def solution(mesh):
    cut = Mesh(mesh.devices.reshape(2, YS, 2, TILES_DEV, SHARE), ("pipe",) + DP + INNER)
    placed = (
        P(DP, INNER, None, None),
        P(DP, None),
        P(DP),
        P(DP),
        P(DP, None),
        P(),
        P("pipe", None),
        P("pipe", None, None),
        P("pipe", None, None),
        P(),
    )
    return jax.shard_map(
        whole_step,
        mesh=cut,
        in_specs=placed,
        out_specs=(P(), P(), P("pipe", None), P("pipe", None, None), P("pipe", None, None), P()),
        check_vma=False,
    )
```
